32 devices in a mesh: grp: 4 (over y, core), inner: 8 (over z, x).
Axes of the slice: x: 2, y: 2, z: 4, core: 2. Of those that a mesh axis runs over, the one named last changes fastest.
Arguments:
- grad_out: bfloat16 [4096, 2048], P(('grp', 'inner')), may hold values from -6 to 6
- hidden: bfloat16 [4096, 2048], P(('grp', 'inner')), may hold values from -6 to 6
- norm_gain: float32 [2048], replicated, may hold values from 0.25 to 1.75
- expert_ids: int32 [4096, 8], P(('grp', 'inner')), may hold values from 0 to 31, all different within a row; in each aligned block of 128 rows (0 to 127, 128 to 255, ...) at most 40 rows name the same one
- gate_weights: float32 [4096, 8], P(('grp', 'inner')), may hold values from 0.02 to 0.5
- w_gate: bfloat16 [32, 2048, 768], P(('grp', 'inner')), may hold values from -0.125 to 0.125
- w_up: bfloat16 [32, 2048, 768], P(('grp', 'inner')), may hold values from -0.125 to 0.125
- w_down: bfloat16 [32, 768, 2048], P(('grp', 'inner')), may hold values from -0.21875 to 0.21875
- w_out: bfloat16 [4096, 2048], P('inner'), may hold values from -0.09375 to 0.09375
- queries: bfloat16 [4096, 4096], P(('grp', 'inner')), may hold values from -0.6 to 0.6
- keys: bfloat16 [4096, 512], P(('grp', 'inner')), may hold values from -0.6 to 0.6
- values: bfloat16 [4096, 512], P(('grp', 'inner')), may hold values from -6 to 6
- attn_out: bfloat16 [4096, 4096], P(('grp', 'inner')), may hold values from -6 to 6
- lse: float32 [32, 4096], P('inner', 'grp'), as said below
Outputs:
- grad_resid: bfloat16 [4096, 2048], P(('grp', 'inner'))
- queries_gradient: bfloat16 [4096, 4096], P(('grp', 'inner'))
- keys_gradient: bfloat16 [4096, 512], P(('grp', 'inner'))
- values_gradient: bfloat16 [4096, 512], P(('grp', 'inner'))
The draws below stay inside these ranges and needn't reach their ends.
Inputs may be any that keep to these rules, and one draw needn't show every extreme that they name: `expert_ids`: each token names 8 different experts. Among the 128 tokens of one device (aligned blocks of rows), no expert is named by more than 40 tokens; in some device's tokens one expert is named by exactly 40. lse[h, t] minus log(1 + the position of token t in its sequence of 1024) lies between 0 and 1.5.
All inputs are finite; a program needn't handle non-finite values.
Results may differ from the reference program's by a relative error of at most 0.012.
Values may be sent and summed in bfloat16 or wider, within the bound.
A program may use at most 192 MiB of HBM per device.

```python
import math
import jax
import jax.numpy as jnp
import numpy as np
from jax import lax

D = 2048
QUERY_HEADS = 32
KEY_VALUE_HEADS = 4
HEAD_SIZE = 128
FF = 768
TOPK = 8
TOK_DEV = 128
EXPERTS = 32
CAP = 40
SEQUENCE_TOKENS = 1024
TOTAL_TOKENS = 4096


def draw_lse(key, part):
    position = (jnp.arange(TOTAL_TOKENS, dtype=jnp.int32) % SEQUENCE_TOKENS).astype(jnp.float32)
    base = jnp.log(position + 1.0)[None, :]
    extra = jax.random.uniform(key, (QUERY_HEADS, TOTAL_TOKENS), jnp.float32, 0.3, 1.2)
    return base + extra


def bounded_rows(key, columns):
    second = jax.random.fold_in(key, 23)
    drawn = jax.random.uniform(second, (TOTAL_TOKENS, columns), jnp.float32, -0.59, 0.59)
    return drawn.astype(jnp.bfloat16)


def draw_queries(key, part):
    return bounded_rows(jax.random.fold_in(key, 101), QUERY_HEADS * HEAD_SIZE)


def draw_keys(key, part):
    return bounded_rows(jax.random.fold_in(key, 202), KEY_VALUE_HEADS * HEAD_SIZE)


def shard_levels(own_key, shape, pieces, least, top_value):
    def one(dim, blocks):
        draws = jax.random.uniform(jax.random.fold_in(jax.random.fold_in(own_key, 6), dim), (blocks,), jnp.float32, least / len(pieces), top_value / len(pieces))
        return jnp.repeat(jnp.exp(draws), shape[dim] // blocks).reshape((-1,) + (1,) * (len(shape) - dim - 1))

    factor_of = one(*pieces[0])
    for cut in pieces[1:]:
        factor_of = factor_of * one(*cut)
    return factor_of


def shared_out(rng, own, number, rows, count, top, most, skew):
    order = jax.random.permutation(rng, count)
    crowded, usual = load_shares(count, rows * top, most, skew, True), load_shares(count, rows * top, most, skew, False)
    places = jnp.arange(count)

    def named(tallies, turn):
        used = int((tallies > 0).sum())
        fixed = max(1, used // 4)
        moved = fixed + (places - fixed + turn * (used - fixed)) % max(1, count - fixed)
        return jnp.zeros((count,), jnp.int32).at[order[jnp.where(places < fixed, places, moved)]].set(jnp.asarray(tallies, jnp.int32))

    tallies = jnp.where(number % 4 == 0, named(crowded, number // 4), named(usual, number - number // 4 - 1))
    mixed = jax.random.permutation(jax.random.fold_in(own, 3), count)
    giver, receiver = mixed[0:count // 2 * 2:2], mixed[1:count // 2 * 2:2]
    slack = jnp.minimum(tallies[giver] - 1, most - tallies[receiver]) // 2
    slack = jnp.where((giver == order[0]) | (receiver == order[0]) | (tallies[receiver] == 0), 0, jnp.maximum(slack, 0))
    moved = jax.random.randint(jax.random.fold_in(own, 4), (count // 2,), 0, 1 << 20) % (slack + 1)
    tallies = tallies.at[giver].add(-moved).at[receiver].add(moved)
    members = jnp.searchsorted(jnp.cumsum(tallies), jnp.arange(rows * top), side="right").astype(jnp.int32)
    grid = members.reshape(top, rows).T
    grid = grid[jax.random.permutation(jax.random.fold_in(own, 1), rows)]
    turn = jax.random.randint(jax.random.fold_in(own, 2), (rows, 1), 0, top)
    return jnp.take_along_axis(grid, (jnp.arange(top)[None, :] + turn) % top, axis=1)


def load_shares(count, total, reach, slope, full):
    loads = [(1 << 20) // math.isqrt(grade ** slope) + 1 for grade in range(1, count + 1)]
    largest = reach if full else min(reach, max(-(-total // count), total * loads[0] // sum(loads)))
    least = 1 if total - largest >= count - 1 else 0
    given, surplus = [largest] + [least] * (count - 1), total - largest - least * (count - 1)
    while surplus > 0:
        movable = [i for i in range(1, count) if given[i] < largest] or [i for i in range(1, count) if given[i] < reach]
        pool, left = sum([loads[i] for i in movable]), surplus
        for i in movable:
            more = min(reach - given[i], max(1, left * loads[i] // pool), surplus)
            given[i] = given[i] + more
            surplus = surplus - more
    return np.array(given)


def normal_values(key, extent, width, bound, pieces=(), kind=jnp.bfloat16):
    values = jax.random.normal(key, extent, jnp.float32) * width
    if len(pieces) > 0:
        values = shard_levels(key, extent, pieces, -0.22, 0.18) * values
    return jnp.clip(values, min=-bound, max=bound).astype(kind)


def setup_inputs(seed: int = 0) -> dict:
    splits = jax.random.split(jax.random.key(seed), 15)
    grad_out = normal_values(splits[0], (TOTAL_TOKENS, D), 1.0, 6.0, ((0, 32),))
    hidden = normal_values(splits[1], (TOTAL_TOKENS, D), 1.0, 6.0, ((0, 32),))
    norm_gain = jnp.clip(1.0 + 0.15 * jax.random.normal(splits[2], (D,), jnp.float32), 0.25, 1.75)
    expert_ids_keys = jax.random.split(jax.random.fold_in(splits[3], 1), TOTAL_TOKENS // TOK_DEV)
    expert_ids_turns = jax.random.permutation(jax.random.fold_in(splits[3], 3), TOTAL_TOKENS // TOK_DEV)
    expert_ids = jax.vmap(lambda own, number: shared_out(jax.random.fold_in(splits[3], 2), own, number, TOK_DEV, EXPERTS, TOPK, CAP, 1))(expert_ids_keys, expert_ids_turns).reshape((TOTAL_TOKENS, TOPK))
    gate_weights = jnp.clip(jnp.exp(math.log(0.5) - 3.218876 * jax.random.uniform(splits[4], (TOTAL_TOKENS, TOPK), jnp.float32) ** shard_levels(splits[4], (TOTAL_TOKENS, TOPK), ((0, 32),), -0.2, 0.2)), 0.02, 0.5)
    w_gate = normal_values(splits[5], (EXPERTS, D, FF), D ** -0.5, 0.125, ((0, 32),))
    w_up = normal_values(splits[6], (EXPERTS, D, FF), D ** -0.5, 0.125, ((0, 32),))
    w_down = normal_values(splits[7], (EXPERTS, FF, D), FF ** -0.5, 0.21875, ((0, 32),))
    w_out = normal_values(splits[8], (QUERY_HEADS * HEAD_SIZE, D), (QUERY_HEADS * HEAD_SIZE) ** -0.5, 0.09375, ((0, 8),))
    queries = draw_queries(jax.random.fold_in(splits[14], 71), 0)
    keys = draw_keys(jax.random.fold_in(splits[14], 71), 0)
    values = normal_values(splits[11], (TOTAL_TOKENS, KEY_VALUE_HEADS * HEAD_SIZE), 1.0, 6.0, ((0, 32),))
    attn_out = normal_values(splits[12], (TOTAL_TOKENS, QUERY_HEADS * HEAD_SIZE), 1.0, 6.0, ((0, 32),))
    lse = draw_lse(jax.random.fold_in(splits[14], 71), 0)
    return {"grad_out": grad_out, "hidden": hidden, "norm_gain": norm_gain, "expert_ids": expert_ids, "gate_weights": gate_weights, "w_gate": w_gate, "w_up": w_up, "w_down": w_down, "w_out": w_out, "queries": queries, "keys": keys, "values": values, "attn_out": attn_out, "lse": lse}


def contract_last(left, right):
    return lax.dot_general(left, right, (((1,), (1,)), ((), ())), preferred_element_type=jnp.float32)

def expert_back(inputs, upstream, gate_matrix, up_matrix, down_matrix):
    gate_pre = jnp.dot(inputs, gate_matrix, preferred_element_type=jnp.float32)
    up_pre = jnp.dot(inputs, up_matrix, preferred_element_type=jnp.float32)
    back_hidden = contract_last(upstream, down_matrix)
    sigmoid = jax.nn.sigmoid(gate_pre)
    grad_gate = (back_hidden * up_pre * sigmoid * (1.0 + gate_pre * (1.0 - sigmoid))).astype(jnp.bfloat16)
    grad_up = (back_hidden * gate_pre * sigmoid).astype(jnp.bfloat16)
    grad_in = contract_last(grad_gate, gate_matrix) + contract_last(grad_up, up_matrix)
    return grad_in.astype(jnp.bfloat16)

def head_group(operands):
    query_blk, output_blk, grad_blk, key_blk, value_blk, lse_blk = operands
    scale = float(HEAD_SIZE) ** (-0.5)
    query_f = query_blk.astype(jnp.float32)
    key_f = key_blk.astype(jnp.float32)
    value_f = value_blk.astype(jnp.float32)
    grad_f = grad_blk.astype(jnp.float32)
    output_f = output_blk.astype(jnp.float32)
    scores = jnp.einsum('gid,jd->gij', query_f, key_f) * scale
    position = jnp.arange(SEQUENCE_TOKENS, dtype=jnp.int32)
    visible = position[None, :] <= position[:, None]
    probs = jnp.where(visible[None], jnp.exp(scores - lse_blk[:, :, None]), 0.0)
    probs_low = probs.astype(jnp.bfloat16).astype(jnp.float32)
    grad_probs = jnp.einsum('gid,jd->gij', grad_f, value_f)
    delta = lax.optimization_barrier(jnp.sum(grad_f * output_f, axis=-1))
    grad_scores = (probs * (grad_probs - delta[:, :, None])).astype(jnp.bfloat16).astype(jnp.float32)
    query_gradient_fn = jnp.einsum('gij,jd->gid', grad_scores, key_f) * scale
    key_gradient_fn = jnp.einsum('gij,gid->jd', grad_scores, query_f) * scale
    value_gradient_fn = jnp.einsum('gij,gid->jd', probs_low, grad_f)
    return (query_gradient_fn.astype(jnp.bfloat16), key_gradient_fn.astype(jnp.bfloat16), value_gradient_fn.astype(jnp.bfloat16))

def reference(grad_out, hidden, norm_gain, expert_ids, gate_weights, w_gate, w_up, w_down, w_out, queries, keys, values, attn_out, lse):
    hidden_f = hidden.astype(jnp.float32)
    inverse = lax.rsqrt(lax.optimization_barrier(jnp.mean(hidden_f * hidden_f, axis=1, keepdims=True)) + 1e-06)
    normed = (hidden_f * inverse * norm_gain).astype(jnp.bfloat16)
    upstream = grad_out.astype(jnp.float32)
    flat_count = TOTAL_TOKENS * TOPK
    flat_ids = expert_ids.reshape(-1)
    flat_weights = gate_weights.reshape(-1)
    order = jnp.argsort(flat_ids, stable=True).astype(jnp.int32)
    counts = lax.optimization_barrier(jnp.sum((flat_ids[:, None] == jnp.arange(EXPERTS, dtype=jnp.int32)[None, :]).astype(jnp.int32), axis=0))
    starts = jnp.cumsum(counts) - counts
    most = TOTAL_TOKENS // TOK_DEV * CAP

    def one_expert(total, expert):
        offsets = jnp.arange(most, dtype=jnp.int32)
        place = starts[expert] + offsets
        valid = offsets < counts[expert]
        rows = order[jnp.minimum(place, flat_count - 1)]
        tok_index = rows // TOPK
        inputs = normed[tok_index]
        scaled = (upstream[tok_index] * flat_weights[rows][:, None]).astype(jnp.bfloat16)
        grad_in = expert_back(inputs, scaled, w_gate[expert], w_up[expert], w_down[expert])
        grad_in = jnp.where(valid[:, None], grad_in.astype(jnp.float32), 0.0)
        return (total.at[tok_index].add(grad_in), None)
    grad_normed, _ = lax.scan(one_expert, jnp.zeros((TOTAL_TOKENS, D), jnp.float32), jnp.arange(EXPERTS, dtype=jnp.int32))
    gained = grad_normed * norm_gain
    statistic = lax.optimization_barrier(jnp.mean(gained * hidden_f, axis=1, keepdims=True))
    grad_resid = (upstream + inverse * gained - hidden_f * inverse * inverse * inverse * statistic).astype(jnp.bfloat16)
    grad_attn = contract_last(grad_resid, w_out).astype(jnp.bfloat16)
    sequence_count = TOTAL_TOKENS // SEQUENCE_TOKENS
    shared_result = QUERY_HEADS // KEY_VALUE_HEADS

    def by_head(numeric_array):
        return numeric_array.reshape(sequence_count, SEQUENCE_TOKENS, KEY_VALUE_HEADS, shared_result, HEAD_SIZE).transpose(0, 2, 3, 1, 4).reshape(sequence_count * KEY_VALUE_HEADS, shared_result, SEQUENCE_TOKENS, HEAD_SIZE)

    def by_kv(numeric_array):
        return numeric_array.reshape(sequence_count, SEQUENCE_TOKENS, KEY_VALUE_HEADS, HEAD_SIZE).transpose(0, 2, 1, 3).reshape(sequence_count * KEY_VALUE_HEADS, SEQUENCE_TOKENS, HEAD_SIZE)
    logsumexp_heads = lse.reshape(KEY_VALUE_HEADS, shared_result, sequence_count, SEQUENCE_TOKENS).transpose(2, 0, 1, 3).reshape(sequence_count * KEY_VALUE_HEADS, shared_result, SEQUENCE_TOKENS)
    query_gradient_fn, key_gradient_fn, value_gradient_fn = lax.map(head_group, (by_head(queries), by_head(attn_out), by_head(grad_attn), by_kv(keys), by_kv(values), logsumexp_heads))
    queries_gradient = query_gradient_fn.reshape(sequence_count, KEY_VALUE_HEADS, shared_result, SEQUENCE_TOKENS, HEAD_SIZE).transpose(0, 3, 1, 2, 4).reshape(TOTAL_TOKENS, QUERY_HEADS * HEAD_SIZE)
    keys_gradient = key_gradient_fn.reshape(sequence_count, KEY_VALUE_HEADS, SEQUENCE_TOKENS, HEAD_SIZE).transpose(0, 2, 1, 3).reshape(TOTAL_TOKENS, KEY_VALUE_HEADS * HEAD_SIZE)
    values_gradient = value_gradient_fn.reshape(sequence_count, KEY_VALUE_HEADS, SEQUENCE_TOKENS, HEAD_SIZE).transpose(0, 2, 1, 3).reshape(TOTAL_TOKENS, KEY_VALUE_HEADS * HEAD_SIZE)
    return (grad_resid, queries_gradient, keys_gradient, values_gradient)
```

```python
import functools

import jax
import jax.numpy as jnp
from jax import lax
from jax.experimental import pallas as pl
from jax.experimental.pallas import tpu as pltpu
from jax.sharding import PartitionSpec as P

KEY_VALUE_HEADS = 4
HEAD_SIZE = 128


EPSILON = 1e-06


def contract_last(left, right):
    return lax.dot_general(
        left, right, (((1,), (1,)), ((), ())), preferred_element_type=jnp.float32
    )


def contract_first(left, right):
    return lax.dot_general(
        left, right, (((0,), (0,)), ((), ())), preferred_element_type=jnp.float32
    )


def expert_grads(received, w_gate, w_up, w_down):
    local = w_gate.shape[0]
    width = w_gate.shape[1]
    shaped = received.reshape((-1, local) + received.shape[1:])
    inputs = shaped[..., :width]
    upstream = shaped[..., width:]
    gate_pre = jnp.einsum("nlcd,ldf->nlcf", inputs, w_gate, preferred_element_type=jnp.float32)
    up_pre = jnp.einsum("nlcd,ldf->nlcf", inputs, w_up, preferred_element_type=jnp.float32)
    back_hidden = jnp.einsum("nlcd,lfd->nlcf", upstream, w_down, preferred_element_type=jnp.float32)
    sigmoid = jax.nn.sigmoid(gate_pre)
    grad_gate = (back_hidden * up_pre * sigmoid * (1.0 + gate_pre * (1.0 - sigmoid))).astype(
        jnp.bfloat16
    )
    grad_up = (back_hidden * gate_pre * sigmoid).astype(jnp.bfloat16)
    grad_in = jnp.einsum("nlcf,ldf->nlcd", grad_gate, w_gate, preferred_element_type=jnp.float32)
    grad_in = grad_in + jnp.einsum(
        "nlcf,ldf->nlcd", grad_up, w_up, preferred_element_type=jnp.float32
    )
    return grad_in.astype(jnp.bfloat16).reshape(received.shape[:-1] + (width,))


MESH_ID = pl.DeviceIdType.MESH
FEATURE_CHUNKS = 4
FF_TILE = 256
TILE_ROWS = 16


def moe_kernel(
    lines,
    cols,
    capacity,
    hidden_ref,
    grad_ref,
    gain_ref,
    ids_ref,
    gates_ref,
    gate_hbm,
    up_hbm,
    down_hbm,
    out_ref,
    block,
    meta,
    pick,
    pick_back,
    weight,
    outgoing,
    received,
    w_gate,
    w_up,
    w_down,
    hidden_gate,
    hidden_up,
    returned,
    partial,
    arrived,
    own_sum,
    weight_sem,
    line_send,
    line_recv,
    meta_send,
    meta_recv,
    out_send,
    out_recv,
    back_send,
    back_recv,
    sum_send,
    sum_recv,
):
    group = lax.axis_index("grp")
    place = lax.axis_index("inner")
    plane, col = place // cols, place % cols
    groups = 2 * cols
    members = groups * cols
    me = group * cols + col
    tokens, width = hidden_ref.shape
    chunk = 2 * width // FEATURE_CHUNKS
    halves = FEATURE_CHUNKS // 2
    pair_rows = 2 * capacity
    peers = lines * cols
    tiles = w_gate.shape[0]

    def member(number):
        return (number // cols, plane * cols + number % cols)

    def ahead(step):
        return member(lax.rem(me + step, members))

    def behind(step):
        return member(lax.rem(me + members - step, members))

    def across(away):
        far = (plane, plane + 1 - 2 * (plane % 2), (plane + 2) % 4, 3 - plane)[away]
        return (group, far * cols + col)

    def remote(source, target, send, recv, device):
        return pltpu.make_async_remote_copy(
            src_ref=source,
            dst_ref=target,
            send_sem=send,
            recv_sem=recv,
            device_id=device,
            device_id_type=MESH_ID,
        )

    def line_copy(away, part):
        rows = pl.ds((away % 2) * tokens, tokens)
        return remote(
            block.at[0, part, pl.ds(0, tokens)],
            block.at[away // 2, part, rows],
            line_send.at[away, part],
            line_recv.at[away, part],
            across(away),
        )

    def meta_copy(away):
        return remote(
            meta.at[0], meta.at[away], meta_send.at[away], meta_recv.at[away], across(away)
        )

    def step_rows(step):
        return pl.ds(step * pair_rows, pair_rows)

    def out_copy(phase, part, step):
        return remote(
            outgoing.at[phase, part, step_rows(step)],
            received.at[phase, part, step_rows(step)],
            out_send.at[phase, part, step],
            out_recv.at[phase, part, step],
            ahead(step),
        )

    def back_copy(phase, half, step):
        return remote(
            outgoing.at[phase, half, step_rows(step)],
            returned.at[phase, half, step_rows(step)],
            back_send.at[phase, half, step],
            back_recv.at[phase, half, step],
            behind(step),
        )

    def sum_copy(away, half):
        return remote(
            partial.at[away - 1, half],
            arrived.at[away - 1, half],
            sum_send.at[away - 1, half],
            sum_recv.at[away - 1, half],
            across(away),
        )

    barrier = pltpu.get_barrier_semaphore()
    for step in range(1, members):
        pl.semaphore_signal(barrier, inc=1, device_id=ahead(step), device_id_type=MESH_ID)
    for away in range(1, lines):
        pl.semaphore_signal(barrier, inc=1, device_id=across(away), device_id_type=MESH_ID)

    weight_copies = []
    for tile in range(tiles):
        columns = pl.ds(tile * FF_TILE, FF_TILE)
        weight_copies += [
            pltpu.make_async_copy(
                gate_hbm.at[0, :, columns], w_gate.at[tile], weight_sem.at[0, tile]
            ),
            pltpu.make_async_copy(up_hbm.at[0, :, columns], w_up.at[tile], weight_sem.at[1, tile]),
            pltpu.make_async_copy(
                down_hbm.at[0, columns, :], w_down.at[tile], weight_sem.at[2, tile]
            ),
        ]
    for copy in weight_copies:
        copy.start()

    def norm_rows(index, carry):
        rows = pl.ds(pl.multiple_of(index * TILE_ROWS, TILE_ROWS), TILE_ROWS)
        hidden = hidden_ref[rows, :].astype(jnp.float32)
        inverse = lax.rsqrt(jnp.mean(hidden * hidden, axis=1, keepdims=True) + EPSILON)
        normed = (hidden * inverse * gain_ref[...]).astype(jnp.bfloat16)
        upstream = grad_ref[rows, :]
        for half in range(halves):
            columns = slice(half * chunk, (half + 1) * chunk)
            block[0, half, rows, :] = normed[:, columns]
            block[0, halves + half, rows, :] = upstream[:, columns]
        return carry

    lax.fori_loop(0, tokens // TILE_ROWS, norm_rows, 0)

    experts = meta.shape[1] // 2
    topk = ids_ref.shape[0]
    expert = lax.broadcasted_iota(jnp.int32, (experts, tokens), 0)
    mine = jnp.zeros((experts, tokens), jnp.float32)
    gates = jnp.zeros((experts, tokens), jnp.float32)
    for slot in range(topk):
        hit = ids_ref[slot : slot + 1, :] == expert
        mine = mine + jnp.where(hit, 1.0, 0.0)
        gates = gates + jnp.where(hit, gates_ref[slot : slot + 1, :], 0.0)
    earlier = lax.broadcasted_iota(jnp.int32, (tokens, tokens), 0)
    later = lax.broadcasted_iota(jnp.int32, (tokens, tokens), 1)
    before = jnp.where(earlier < later, 1.0, 0.0).astype(jnp.bfloat16)
    rank = jnp.dot(mine.astype(jnp.bfloat16), before, preferred_element_type=jnp.float32)
    meta[0, :experts, :] = jnp.where(mine > 0.5, rank, -1.0)
    meta[0, experts:, :] = gates

    pl.semaphore_wait(barrier, members + lines - 2)
    for away in range(1, lines):
        meta_copy(away).start()
    for part in range(FEATURE_CHUNKS):
        line_copy(1, part).start()
    for part in range(FEATURE_CHUNKS):
        for away in range(2, lines):
            line_copy(away, part).start()

    def build_pick(phase):
        lane = lax.broadcasted_iota(jnp.int32, (1, 2 * tokens), 1)
        shift = jnp.where(lane >= tokens, float(capacity), 0.0)
        row = lax.broadcasted_iota(jnp.int32, (pair_rows, 2 * tokens), 0).astype(jnp.float32)
        for step in range(members):
            number = lax.rem(me + step, members)
            named = (number // cols) * peers + plane * cols + number % cols
            slots = jnp.concatenate(
                [meta[2 * phase + j, pl.ds(named, 1), :] for j in range(2)], axis=1
            )
            shares = jnp.concatenate(
                [meta[2 * phase + j, pl.ds(experts + named, 1), :] for j in range(2)], axis=1
            )
            goal = jnp.where(slots >= 0.0, slots + shift, -1.0)
            hot = jnp.where(row == goal, 1.0, 0.0)
            rows = slice(step * pair_rows, (step + 1) * pair_rows)
            pick[phase, rows, :] = hot.astype(jnp.bfloat16)
            weight[phase, rows, :] = jnp.broadcast_to(
                jnp.sum(hot * shares, axis=1, keepdims=True), (pair_rows, 128)
            )
        pick_back[phase] = pick[phase].astype(jnp.float32).T.astype(jnp.bfloat16)

    tile_width = min(chunk, 512)

    def select(phase, part):
        def columns_of(index, carry):
            columns = pl.ds(pl.multiple_of(index * tile_width, tile_width), tile_width)
            rows = jnp.dot(
                pick[phase], block[phase, part, :, columns], preferred_element_type=jnp.float32
            )
            if part >= halves:
                rows = rows * weight[phase][:, :1]
            rows = rows.astype(jnp.bfloat16)
            outgoing[phase, part, :, columns] = rows
            received[phase, part, :pair_rows, columns] = rows[:pair_rows]
            return carry

        lax.fori_loop(0, chunk // tile_width, columns_of, 0)

    for phase in range(2):
        for part in range(FEATURE_CHUNKS):
            for away in (1,) if phase == 0 else (2, 3):
                if part == 0:
                    meta_copy(away).wait_recv()
                line_copy(away, part).wait_recv()
            if part == 0:
                build_pick(phase)
            select(phase, part)
            for step in range(1, members):
                out_copy(phase, part, step).start()

    for copy in weight_copies:
        copy.wait()

    def expert_products(phase):
        for part in range(FEATURE_CHUNKS):
            for step in range(1, members):
                out_copy(phase, part, step).wait_recv()

        def hidden_tile(tile, carry):
            def product(weights):
                return sum(
                    jnp.dot(
                        received[phase, half],
                        weights[tile, half * chunk : (half + 1) * chunk, :],
                        preferred_element_type=jnp.float32,
                    )
                    for half in range(halves)
                )

            gate_pre = product(w_gate)
            up_pre = product(w_up)
            back_hidden = sum(
                contract_last(
                    received[phase, halves + half],
                    w_down[tile, :, half * chunk : (half + 1) * chunk],
                )
                for half in range(halves)
            )
            sigmoid = jax.nn.sigmoid(gate_pre)
            hidden_gate[tile] = (
                back_hidden * up_pre * sigmoid * (1.0 + gate_pre * (1.0 - sigmoid))
            ).astype(jnp.bfloat16)
            hidden_up[tile] = (back_hidden * gate_pre * sigmoid).astype(jnp.bfloat16)
            return carry

        lax.fori_loop(0, tiles, hidden_tile, 0)
        for half in range(halves):
            for step in range(1, members):
                out_copy(phase, half, step).wait_send()

            def columns_of(index, carry):
                columns = pl.ds(pl.multiple_of(index * tile_width, tile_width), tile_width)
                rows = pl.ds(
                    pl.multiple_of(half * chunk + index * tile_width, tile_width), tile_width
                )
                total = contract_last(hidden_gate[0], w_gate[0, rows, :])
                for tile in range(tiles):
                    if tile:
                        total = total + contract_last(hidden_gate[tile], w_gate[tile, rows, :])
                    total = total + contract_last(hidden_up[tile], w_up[tile, rows, :])
                total = total.astype(jnp.bfloat16)
                outgoing[phase, half, :, columns] = total
                returned[phase, half, :pair_rows, columns] = total[:pair_rows]
                return carry

            lax.fori_loop(0, chunk // tile_width, columns_of, 0)
            for step in range(1, members):
                back_copy(phase, half, step).start()

    def combine(phase):
        for half in range(halves):
            for step in range(1, members):
                back_copy(phase, half, step).wait_recv()

            def columns_of(index, carry):
                columns = pl.ds(pl.multiple_of(index * tile_width, tile_width), tile_width)
                total = jnp.dot(
                    pick_back[phase],
                    returned[phase, half, :, columns],
                    preferred_element_type=jnp.float32,
                )
                for j in range(2):
                    rows = total[j * tokens : (j + 1) * tokens]
                    away = 2 * phase + j
                    if away:
                        partial[away - 1, half, :, columns] = rows.astype(jnp.bfloat16)
                    else:
                        own_sum[half, :, columns] = rows
                return carry

            lax.fori_loop(0, chunk // tile_width, columns_of, 0)
            for away in (1,) if phase == 0 else (2, 3):
                sum_copy(away, half).start()

    for phase in range(2):
        expert_products(phase)
    for phase in range(2):
        combine(phase)

    for away in range(1, lines):
        for half in range(halves):
            sum_copy(away, half).wait_recv()

    def finish(index, carry):
        rows = pl.ds(pl.multiple_of(index * TILE_ROWS, TILE_ROWS), TILE_ROWS)
        hidden = hidden_ref[rows, :].astype(jnp.float32)
        inverse = lax.rsqrt(jnp.mean(hidden * hidden, axis=1, keepdims=True) + EPSILON)
        grad_normed = []
        for half in range(halves):
            total = own_sum[half, rows, :]
            for away in range(1, lines):
                total = total + arrived[away - 1, half, rows, :].astype(jnp.float32)
            grad_normed.append(total)
        gained = jnp.concatenate(grad_normed, axis=1) * gain_ref[...]
        statistic = jnp.mean(gained * hidden, axis=1, keepdims=True)
        out_ref[rows, :] = (
            grad_ref[rows, :].astype(jnp.float32)
            + inverse * gained
            - hidden * (inverse * inverse * inverse * statistic)
        ).astype(jnp.bfloat16)
        return carry

    lax.fori_loop(0, tokens // TILE_ROWS, finish, 0)

    for away in range(1, lines):
        meta_copy(away).wait_send()
        for part in range(FEATURE_CHUNKS):
            line_copy(away, part).wait_send()
        for half in range(halves):
            sum_copy(away, half).wait_send()
    for phase in range(2):
        for step in range(1, members):
            for part in range(halves, FEATURE_CHUNKS):
                out_copy(phase, part, step).wait_send()
            for half in range(halves):
                back_copy(phase, half, step).wait_send()


def moe_input_grads(
    hidden, grad_out, norm_gain, expert_ids, gate_weights, w_gate, w_up, w_down, lines, cols, capacity
):
    tokens, width = hidden.shape
    ff = w_gate.shape[2]
    experts = 2 * cols * lines * cols
    members = 2 * cols * cols
    chunk = 2 * width // FEATURE_CHUNKS
    halves = FEATURE_CHUNKS // 2
    rows = members * 2 * capacity
    tiles = ff // FF_TILE
    low, full = jnp.bfloat16, jnp.float32
    dma = pltpu.SemaphoreType.DMA
    vmem = pl.BlockSpec(memory_space=pltpu.VMEM)
    hbm = pl.BlockSpec(memory_space=pl.ANY)
    return pl.pallas_call(
        functools.partial(moe_kernel, lines, cols, capacity),
        out_shape=jax.ShapeDtypeStruct((tokens, width), low),
        in_specs=[vmem] * 5 + [hbm] * 3,
        out_specs=vmem,
        scratch_shapes=[
            pltpu.VMEM((2, FEATURE_CHUNKS, 2 * tokens, chunk), low),
            pltpu.VMEM((lines, 2 * experts, tokens), full),
            pltpu.VMEM((2, rows, 2 * tokens), low),
            pltpu.VMEM((2, 2 * tokens, rows), low),
            pltpu.VMEM((2, rows, 128), full),
            pltpu.VMEM((2, FEATURE_CHUNKS, rows, chunk), low),
            pltpu.VMEM((2, FEATURE_CHUNKS, rows, chunk), low),
            pltpu.VMEM((tiles, width, FF_TILE), low),
            pltpu.VMEM((tiles, width, FF_TILE), low),
            pltpu.VMEM((tiles, FF_TILE, width), low),
            pltpu.VMEM((tiles, rows, FF_TILE), low),
            pltpu.VMEM((tiles, rows, FF_TILE), low),
            pltpu.VMEM((2, halves, rows, chunk), low),
            pltpu.VMEM((lines - 1, halves, tokens, chunk), low),
            pltpu.VMEM((lines - 1, halves, tokens, chunk), low),
            pltpu.VMEM((halves, tokens, chunk), full),
            dma((3, tiles)),
            dma((lines, FEATURE_CHUNKS)),
            dma((lines, FEATURE_CHUNKS)),
            dma((lines,)),
            dma((lines,)),
            dma((2, FEATURE_CHUNKS, members)),
            dma((2, FEATURE_CHUNKS, members)),
            dma((2, halves, members)),
            dma((2, halves, members)),
            dma((lines - 1, halves)),
            dma((lines - 1, halves)),
        ],
        compiler_params=pltpu.CompilerParams(
            collective_id=0, has_side_effects=True, vmem_limit_bytes=60 * 2**20
        ),
        cost_estimate=pl.CostEstimate(
            flops=20 * rows * width * ff, bytes_accessed=400 * 2**20, transcendentals=0
        ),
    )(
        hidden,
        grad_out,
        norm_gain.reshape(1, width),
        expert_ids.T,
        gate_weights.T,
        w_gate,
        w_up,
        w_down,
    )


def per_device(
    grad_out,
    hidden,
    norm_gain,
    expert_ids,
    gate_weights,
    w_gate,
    w_up,
    w_down,
    w_out,
    queries,
    keys,
    values,
    attn_out,
    lse,
):
    token_rows, width = hidden.shape
    topk = expert_ids.shape[1]
    groups = lax.axis_size("grp")
    inner_product = lax.axis_size("inner")
    experts_all = w_gate.shape[0] * groups * inner_product
    capacity = max(2, 5 * token_rows * topk // (4 * experts_all))
    cols = groups // 2
    lines = inner_product // cols if cols else 0
    kernel_plan = (
        cols == 2
        and lines == 4
        and inner_product == lines * cols
        and w_gate.shape[0] == 1
        and (2 * capacity) % 16 == 0
        and token_rows == 128
        and width % 1024 == 0
        and w_gate.shape[2] % FF_TILE == 0
    )
    if kernel_plan:
        grad_resid = moe_input_grads(
            hidden,
            grad_out,
            norm_gain,
            expert_ids,
            gate_weights,
            w_gate,
            w_up,
            w_down,
            lines,
            cols,
            capacity,
        )
    else:
        hidden_f = hidden.astype(jnp.float32)
        inverse = lax.rsqrt(jnp.mean(hidden_f * hidden_f, axis=1, keepdims=True) + EPSILON)
        normed = (hidden_f * inverse * norm_gain).astype(jnp.bfloat16)
        upstream = grad_out.astype(jnp.float32)
        flat_count = token_rows * topk
        flat_ids = expert_ids.reshape(-1)
        one_hot = (flat_ids[:, None] == jnp.arange(experts_all, dtype=jnp.int32)[None, :]).astype(
            jnp.int32
        )
        before = jnp.tril(jnp.ones((flat_count, flat_count), jnp.bfloat16), -1)
        ahead = jnp.dot(
            before, one_hot.astype(jnp.bfloat16), preferred_element_type=jnp.float32
        ).astype(jnp.int32)
        slot_rank = jnp.sum(ahead * one_hot, axis=1)
        target = flat_ids * capacity + slot_rank
        owner = (
            jnp.full((experts_all * capacity,), flat_count, jnp.int32)
            .at[target]
            .set(jnp.arange(flat_count, dtype=jnp.int32))
        )
        source_tok = owner // topk
        scaled = (
            (upstream[:, None, :] * gate_weights[:, :, None])
            .reshape(flat_count, width)
            .astype(jnp.bfloat16)
        )
        zero_row = jnp.zeros((1, width), jnp.bfloat16)
        slot_inputs = jnp.concatenate([normed, zero_row], axis=0)[source_tok]
        slot_grads = jnp.concatenate([scaled, zero_row], axis=0)[owner]
        outgoing = jnp.concatenate([slot_inputs, slot_grads], axis=1).reshape(
            experts_all, capacity, 2 * width
        )
        returned = lax.all_to_all(
            expert_grads(
                lax.all_to_all(outgoing, ("grp", "inner"), split_axis=0, concat_axis=0, tiled=True),
                w_gate,
                w_up,
                w_down,
            ),
            ("grp", "inner"),
            split_axis=0,
            concat_axis=0,
            tiled=True,
        )
        expert_rows = returned.reshape(-1, width)[target].astype(jnp.float32)
        grad_normed = jnp.sum(expert_rows.reshape(token_rows, topk, width), axis=1)
        gained = grad_normed * norm_gain
        statistic = jnp.mean(gained * hidden_f, axis=1, keepdims=True)
        grad_resid = (
            upstream + inverse * gained - hidden_f * inverse * inverse * inverse * statistic
        ).astype(jnp.bfloat16)
    head_width = queries.shape[1] // inner_product
    per_head = head_width // HEAD_SIZE
    shared_portion = inner_product // KEY_VALUE_HEADS
    if True:
        key_value_pairs = jnp.concatenate(
            [
                keys.reshape(token_rows, KEY_VALUE_HEADS, 1, HEAD_SIZE),
                values.reshape(token_rows, KEY_VALUE_HEADS, 1, HEAD_SIZE),
            ],
            axis=2,
        )
        key_value_broadcast = jnp.broadcast_to(
            key_value_pairs[:, :, None], (token_rows, KEY_VALUE_HEADS, shared_portion, 2, HEAD_SIZE)
        ).reshape(token_rows, inner_product * 2 * HEAD_SIZE)
        head_query, head_output, head_kv = (
            lax.all_to_all(queries, "inner", split_axis=1, concat_axis=0, tiled=True),
            lax.all_to_all(attn_out, "inner", split_axis=1, concat_axis=0, tiled=True),
            lax.all_to_all(key_value_broadcast, "inner", split_axis=1, concat_axis=0, tiled=True),
        )
    head_grad = contract_last(
        lax.all_gather(grad_resid, "inner", axis=0, tiled=True), w_out
    ).astype(jnp.bfloat16)
    seq_len = head_query.shape[0]
    if True:
        head_key = head_kv[:, :HEAD_SIZE]
        head_value = head_kv[:, HEAD_SIZE:]
    lse_rows = lse.T
    scale = float(HEAD_SIZE) ** (-0.5)
    blocks = 1
    while blocks < 8 and seq_len % (2 * blocks) == 0 and (seq_len // (2 * blocks) >= 512):
        blocks = blocks * 2
    block_len = seq_len // blocks
    grad_key_acc = jnp.zeros((seq_len, HEAD_SIZE), jnp.float32)
    grad_value_acc = jnp.zeros((seq_len, HEAD_SIZE), jnp.float32)
    query_parts = []
    for block_index in range(blocks):
        low = block_index * block_len
        high = low + block_len
        block_query = head_query[low:high].reshape(block_len * per_head, HEAD_SIZE)
        block_output = head_output[low:high].reshape(block_len * per_head, HEAD_SIZE)
        block_grad = head_grad[low:high].reshape(block_len * per_head, HEAD_SIZE)
        block_lse = lse_rows[low:high].reshape(-1)
        seen_key = head_key[:high]
        seen_value = head_value[:high]
        scores = contract_last(block_query, seen_key) * scale
        row_position = low + jnp.arange(block_len * per_head, dtype=jnp.int32) // per_head
        visible = jnp.arange(high, dtype=jnp.int32)[None, :] <= row_position[:, None]
        probs = jnp.where(visible, jnp.exp(scores - block_lse[:, None]), 0.0)
        grad_probs = contract_last(block_grad, seen_value)
        delta = jnp.sum(
            block_grad.astype(jnp.float32) * block_output.astype(jnp.float32), axis=1, keepdims=True
        )
        grad_scores = (probs * (grad_probs - delta)).astype(jnp.bfloat16)
        query_part = jnp.dot(grad_scores, seen_key, preferred_element_type=jnp.float32) * scale
        query_parts.append(query_part.reshape(block_len, head_width))
        grad_key_acc = grad_key_acc.at[:high].add(contract_first(grad_scores, block_query) * scale)
        grad_value_acc = grad_value_acc.at[:high].add(
            contract_first(probs.astype(jnp.bfloat16), block_grad)
        )
    grad_query_heads = jnp.concatenate(query_parts, axis=0)
    kv_heads = jnp.concatenate([grad_key_acc, grad_value_acc], axis=1)
    token_query, token_key_value = (
        lax.all_to_all(
            grad_query_heads.astype(jnp.bfloat16), "inner", split_axis=0, concat_axis=1, tiled=True
        ).astype(grad_query_heads.dtype),
        lax.all_to_all(
            kv_heads.astype(jnp.bfloat16), "inner", split_axis=0, concat_axis=1, tiled=True
        ).astype(kv_heads.dtype),
    )
    summed_total = jnp.sum(
        token_key_value.reshape(token_rows, KEY_VALUE_HEADS, shared_portion, 2, HEAD_SIZE), axis=2
    )
    keys_gradient = (
        summed_total[:, :, 0].reshape(token_rows, KEY_VALUE_HEADS * HEAD_SIZE).astype(jnp.bfloat16)
    )
    values_gradient = (
        summed_total[:, :, 1].reshape(token_rows, KEY_VALUE_HEADS * HEAD_SIZE).astype(jnp.bfloat16)
    )
    return (grad_resid, token_query.astype(jnp.bfloat16), keys_gradient, values_gradient)


def solution(mesh):
    placed = (
        P(("grp", "inner"), None),
        P(("grp", "inner"), None),
        P(),
        P(("grp", "inner"), None),
        P(("grp", "inner"), None),
        P(("grp", "inner"), None, None),
        P(("grp", "inner"), None, None),
        P(("grp", "inner"), None, None),
        P("inner", None),
        P(("grp", "inner"), None),
        P(("grp", "inner"), None),
        P(("grp", "inner"), None),
        P(("grp", "inner"), None),
        P("inner", "grp"),
    )
    return jax.shard_map(
        per_device,
        mesh=mesh,
        in_specs=placed,
        out_specs=(
            P(("grp", "inner"), None),
            P(("grp", "inner"), None),
            P(("grp", "inner"), None),
            P(("grp", "inner"), None),
        ),
        check_vma=False,
    )
```

```python
import functools

import jax
import jax.numpy as jnp
from jax import lax
from jax.experimental import pallas as pl
from jax.experimental.pallas import tpu as pltpu
from jax.sharding import PartitionSpec as P

KEY_VALUE_HEADS = 4
HEAD_SIZE = 128


EPSILON = 1e-06


def contract_last(left, right):
    return lax.dot_general(
        left, right, (((1,), (1,)), ((), ())), preferred_element_type=jnp.float32
    )


def contract_first(left, right):
    return lax.dot_general(
        left, right, (((0,), (0,)), ((), ())), preferred_element_type=jnp.float32
    )


def expert_grads(received, w_gate, w_up, w_down):
    local = w_gate.shape[0]
    width = w_gate.shape[1]
    shaped = received.reshape((-1, local) + received.shape[1:])
    inputs = shaped[..., :width]
    upstream = shaped[..., width:]
    gate_pre = jnp.einsum("nlcd,ldf->nlcf", inputs, w_gate, preferred_element_type=jnp.float32)
    up_pre = jnp.einsum("nlcd,ldf->nlcf", inputs, w_up, preferred_element_type=jnp.float32)
    back_hidden = jnp.einsum("nlcd,lfd->nlcf", upstream, w_down, preferred_element_type=jnp.float32)
    sigmoid = jax.nn.sigmoid(gate_pre)
    grad_gate = (back_hidden * up_pre * sigmoid * (1.0 + gate_pre * (1.0 - sigmoid))).astype(
        jnp.bfloat16
    )
    grad_up = (back_hidden * gate_pre * sigmoid).astype(jnp.bfloat16)
    grad_in = jnp.einsum("nlcf,ldf->nlcd", grad_gate, w_gate, preferred_element_type=jnp.float32)
    grad_in = grad_in + jnp.einsum(
        "nlcf,ldf->nlcd", grad_up, w_up, preferred_element_type=jnp.float32
    )
    return grad_in.astype(jnp.bfloat16).reshape(received.shape[:-1] + (width,))


MESH_ID = pl.DeviceIdType.MESH
FEATURE_CHUNKS = 4
FF_TILE = 256
TILE_ROWS = 16


def moe_kernel(
    lines,
    cols,
    capacity,
    hidden_ref,
    grad_ref,
    gain_ref,
    ids_ref,
    gates_ref,
    gate_hbm,
    up_hbm,
    down_hbm,
    query_hbm,
    output_hbm,
    key_hbm,
    value_hbm,
    out_ref,
    head_query,
    head_output,
    head_key,
    head_value,
    block,
    meta,
    pick,
    pick_back,
    weight,
    outgoing,
    received,
    w_gate,
    w_up,
    w_down,
    hidden_gate,
    hidden_up,
    slope_gate,
    slope_up,
    returned,
    partial,
    arrived,
    own_sum,
    weight_sem,
    line_send,
    line_recv,
    meta_send,
    meta_recv,
    out_send,
    out_recv,
    back_send,
    back_recv,
    sum_send,
    sum_recv,
    head_send,
    head_recv,
    head_own,
):
    group = lax.axis_index("grp")
    place = lax.axis_index("inner")
    plane, col = place // cols, place % cols
    groups = 2 * cols
    members = groups * cols
    me = group * cols + col
    tokens, width = hidden_ref.shape
    chunk = 2 * width // FEATURE_CHUNKS
    halves = FEATURE_CHUNKS // 2
    pair_rows = 2 * capacity
    peers = lines * cols
    tiles = w_gate.shape[0]

    def member(number):
        return (number // cols, plane * cols + number % cols)

    def ahead(step):
        return member(lax.rem(me + step, members))

    def behind(step):
        return member(lax.rem(me + members - step, members))

    def across(away):
        far = (plane, (plane + 2) % 4, plane + 1 - 2 * (plane % 2), 3 - plane)[away]
        return (group, far * cols + col)

    def remote(source, target, send, recv, device):
        return pltpu.make_async_remote_copy(
            src_ref=source,
            dst_ref=target,
            send_sem=send,
            recv_sem=recv,
            device_id=device,
            device_id_type=MESH_ID,
        )

    def line_copy(away, part):
        rows = pl.ds((away % 2) * tokens, tokens)
        return remote(
            block.at[0, part, pl.ds(0, tokens)],
            block.at[away // 2, part, rows],
            line_send.at[away, part],
            line_recv.at[away, part],
            across(away),
        )

    def meta_copy(away):
        return remote(
            meta.at[0], meta.at[away], meta_send.at[away], meta_recv.at[away], across(away)
        )

    def step_rows(step):
        return pl.ds(step * pair_rows, pair_rows)

    def out_copy(phase, part, step):
        return remote(
            outgoing.at[phase, part, step_rows(step)],
            received.at[phase, part, step_rows(step)],
            out_send.at[phase, part, step],
            out_recv.at[phase, part, step],
            ahead(step),
        )

    def back_copy(phase, half, step):
        return remote(
            outgoing.at[phase, half, step_rows(step)],
            returned.at[phase, half, step_rows(step)],
            back_send.at[phase, half, step],
            back_recv.at[phase, half, step],
            behind(step),
        )

    def sum_copy(away, half):
        return remote(
            partial.at[away - 1, half],
            arrived.at[away - 1, half],
            sum_send.at[away - 1, half],
            sum_recv.at[away - 1, half],
            across(away),
        )

    head_width = head_query.shape[1]
    kv_width = head_key.shape[1]
    share = peers // (key_hbm.shape[1] // kv_width)

    def head_pairs(to, source):
        columns = pl.ds(pl.multiple_of(to * head_width, head_width), head_width)
        kv_columns = pl.ds(pl.multiple_of((to // share) * kv_width, kv_width), kv_width)
        rows = pl.ds(pl.multiple_of(source * tokens, tokens), tokens)
        return (
            (query_hbm.at[:, columns], head_query.at[rows]),
            (output_hbm.at[:, columns], head_output.at[rows]),
            (key_hbm.at[:, kv_columns], head_key.at[rows]),
            (value_hbm.at[:, kv_columns], head_value.at[rows]),
        )

    def head_copies(to, slot, source, target):
        return [
            remote(
                src, dst, head_send.at[number, slot], head_recv.at[number, slot], (group, target)
            )
            for number, (src, dst) in enumerate(head_pairs(to, source))
        ]

    own_heads = [
        pltpu.make_async_copy(src, dst, head_own.at[number])
        for number, (src, dst) in enumerate(head_pairs(place, place))
    ]

    barrier = pltpu.get_barrier_semaphore()
    for step in range(1, peers):
        pl.semaphore_signal(
            barrier, inc=1, device_id=(group, lax.rem(place + step, peers)), device_id_type=MESH_ID
        )
    for step in range(1, members):
        pl.semaphore_signal(barrier, inc=1, device_id=ahead(step), device_id_type=MESH_ID)

    weight_copies = []
    for tile in range(tiles):
        columns = pl.ds(tile * FF_TILE, FF_TILE)
        weight_copies += [
            pltpu.make_async_copy(
                gate_hbm.at[0, :, columns], w_gate.at[tile], weight_sem.at[0, tile]
            ),
            pltpu.make_async_copy(up_hbm.at[0, :, columns], w_up.at[tile], weight_sem.at[1, tile]),
            pltpu.make_async_copy(
                down_hbm.at[0, columns, :], w_down.at[tile], weight_sem.at[2, tile]
            ),
        ]
    for copy in weight_copies:
        copy.start()

    def norm_rows(index, carry):
        rows = pl.ds(pl.multiple_of(index * TILE_ROWS, TILE_ROWS), TILE_ROWS)
        hidden = hidden_ref[rows, :].astype(jnp.float32)
        inverse = lax.rsqrt(jnp.mean(hidden * hidden, axis=1, keepdims=True) + EPSILON)
        normed = (hidden * inverse * gain_ref[...]).astype(jnp.bfloat16)
        upstream = grad_ref[rows, :]
        for half in range(halves):
            columns = slice(half * chunk, (half + 1) * chunk)
            block[0, half, rows, :] = normed[:, columns]
            block[0, halves + half, rows, :] = upstream[:, columns]
        return carry

    lax.fori_loop(0, tokens // TILE_ROWS, norm_rows, 0)

    experts = meta.shape[1] // 2
    topk = ids_ref.shape[0]
    expert = lax.broadcasted_iota(jnp.int32, (experts, tokens), 0)
    mine = jnp.zeros((experts, tokens), jnp.float32)
    gates = jnp.zeros((experts, tokens), jnp.float32)
    for slot in range(topk):
        hit = ids_ref[slot : slot + 1, :] == expert
        mine = mine + jnp.where(hit, 1.0, 0.0)
        gates = gates + jnp.where(hit, gates_ref[slot : slot + 1, :], 0.0)
    earlier = lax.broadcasted_iota(jnp.int32, (tokens, tokens), 0)
    later = lax.broadcasted_iota(jnp.int32, (tokens, tokens), 1)
    before = jnp.where(earlier < later, 1.0, 0.0).astype(jnp.bfloat16)
    rank = jnp.dot(mine.astype(jnp.bfloat16), before, preferred_element_type=jnp.float32)
    meta[0, :experts, :] = jnp.where(mine > 0.5, rank, -1.0)
    meta[0, experts:, :] = gates

    pl.semaphore_wait(barrier, members + peers - 2)
    for away in range(1, lines):
        meta_copy(away).start()
    for part in range(FEATURE_CHUNKS):
        line_copy(1, part).start()
    for part in range(FEATURE_CHUNKS):
        for away in range(2, lines):
            line_copy(away, part).start()

    def build_pick(phase):
        lane = lax.broadcasted_iota(jnp.int32, (1, 2 * tokens), 1)
        shift = jnp.where(lane >= tokens, float(capacity), 0.0)
        row = lax.broadcasted_iota(jnp.int32, (pair_rows, 2 * tokens), 0).astype(jnp.float32)
        for step in range(members):
            number = lax.rem(me + step, members)
            named = (number // cols) * peers + plane * cols + number % cols
            slots = jnp.concatenate(
                [meta[2 * phase + j, pl.ds(named, 1), :] for j in range(2)], axis=1
            )
            shares = jnp.concatenate(
                [meta[2 * phase + j, pl.ds(experts + named, 1), :] for j in range(2)], axis=1
            )
            goal = jnp.where(slots >= 0.0, slots + shift, -1.0)
            hot = jnp.where(row == goal, 1.0, 0.0)
            rows = slice(step * pair_rows, (step + 1) * pair_rows)
            pick[phase, rows, :] = hot.astype(jnp.bfloat16)
            weight[phase, rows, :] = jnp.broadcast_to(
                jnp.sum(hot * shares, axis=1, keepdims=True), (pair_rows, 128)
            )
        pick_back[phase] = pick[phase].astype(jnp.float32).T.astype(jnp.bfloat16)

    tile_width = min(chunk, 512)

    def select(phase, part):
        def columns_of(index, carry):
            columns = pl.ds(pl.multiple_of(index * tile_width, tile_width), tile_width)
            rows = jnp.dot(
                pick[phase], block[phase, part, :, columns], preferred_element_type=jnp.float32
            )
            if part >= halves:
                rows = rows * weight[phase][:, :1]
            rows = rows.astype(jnp.bfloat16)
            outgoing[phase, part, :, columns] = rows
            received[phase, part, :pair_rows, columns] = rows[:pair_rows]
            return carry

        lax.fori_loop(0, chunk // tile_width, columns_of, 0)

    for phase in range(2):
        for part in range(FEATURE_CHUNKS):
            for away in (1,) if phase == 0 else (2, 3):
                if part == 0:
                    meta_copy(away).wait_recv()
                line_copy(away, part).wait_recv()
            if part == 0:
                build_pick(phase)
            select(phase, part)
            for step in range(1, members):
                out_copy(phase, part, step).start()

    for step in range(1, peers):
        to = lax.rem(place + step, peers)
        for copy in head_copies(to, step, place, to):
            copy.start()
    for copy in own_heads:
        copy.start()

    for copy in weight_copies:
        copy.wait()

    def expert_products(phase):
        def take(part):
            for step in range(1, members):
                out_copy(phase, part, step).wait_recv()

        for half in range(halves):
            take(half)

        def gate_tile(tile, carry):
            def product(weights):
                return sum(
                    jnp.dot(
                        received[phase, half],
                        weights[tile, half * chunk : (half + 1) * chunk, :],
                        preferred_element_type=jnp.float32,
                    )
                    for half in range(halves)
                )

            gate_pre = product(w_gate)
            up_pre = product(w_up)
            sigmoid = jax.nn.sigmoid(gate_pre)
            slope_gate[tile] = up_pre * sigmoid * (1.0 + gate_pre * (1.0 - sigmoid))
            slope_up[tile] = gate_pre * sigmoid
            return carry

        lax.fori_loop(0, tiles, gate_tile, 0)
        for half in range(halves):
            take(halves + half)

        def hidden_tile(tile, carry):
            back_hidden = sum(
                contract_last(
                    received[phase, halves + half],
                    w_down[tile, :, half * chunk : (half + 1) * chunk],
                )
                for half in range(halves)
            )
            hidden_gate[tile] = (back_hidden * slope_gate[tile]).astype(jnp.bfloat16)
            hidden_up[tile] = (back_hidden * slope_up[tile]).astype(jnp.bfloat16)
            return carry

        lax.fori_loop(0, tiles, hidden_tile, 0)
        for half in range(halves):
            for step in range(1, members):
                out_copy(phase, half, step).wait_send()

            def columns_of(index, carry):
                columns = pl.ds(pl.multiple_of(index * tile_width, tile_width), tile_width)
                rows = pl.ds(
                    pl.multiple_of(half * chunk + index * tile_width, tile_width), tile_width
                )
                total = contract_last(hidden_gate[0], w_gate[0, rows, :])
                for tile in range(tiles):
                    if tile:
                        total = total + contract_last(hidden_gate[tile], w_gate[tile, rows, :])
                    total = total + contract_last(hidden_up[tile], w_up[tile, rows, :])
                total = total.astype(jnp.bfloat16)
                outgoing[phase, half, :, columns] = total
                returned[phase, half, :pair_rows, columns] = total[:pair_rows]
                return carry

            lax.fori_loop(0, chunk // tile_width, columns_of, 0)
            for step in range(1, members):
                back_copy(phase, half, step).start()

    def combine(phase):
        for half in range(halves):
            for step in range(1, members):
                back_copy(phase, half, step).wait_recv()

            def columns_of(index, carry):
                columns = pl.ds(pl.multiple_of(index * tile_width, tile_width), tile_width)
                total = jnp.dot(
                    pick_back[phase],
                    returned[phase, half, :, columns],
                    preferred_element_type=jnp.float32,
                )
                for j in range(2):
                    rows = total[j * tokens : (j + 1) * tokens]
                    away = 2 * phase + j
                    if away:
                        partial[away - 1, half, :, columns] = rows.astype(jnp.bfloat16)
                    else:
                        own_sum[half, :, columns] = rows
                return carry

            lax.fori_loop(0, chunk // tile_width, columns_of, 0)
            for away in (1,) if phase == 0 else (2, 3):
                sum_copy(away, half).start()

    for phase in range(2):
        expert_products(phase)
    for phase in range(2):
        combine(phase)

    for away in range(1, lines):
        for half in range(halves):
            sum_copy(away, half).wait_recv()

    def finish(index, carry):
        rows = pl.ds(pl.multiple_of(index * TILE_ROWS, TILE_ROWS), TILE_ROWS)
        hidden = hidden_ref[rows, :].astype(jnp.float32)
        inverse = lax.rsqrt(jnp.mean(hidden * hidden, axis=1, keepdims=True) + EPSILON)
        grad_normed = []
        for half in range(halves):
            total = own_sum[half, rows, :]
            for away in range(1, lines):
                total = total + arrived[away - 1, half, rows, :].astype(jnp.float32)
            grad_normed.append(total)
        gained = jnp.concatenate(grad_normed, axis=1) * gain_ref[...]
        statistic = jnp.mean(gained * hidden, axis=1, keepdims=True)
        out_ref[rows, :] = (
            grad_ref[rows, :].astype(jnp.float32)
            + inverse * gained
            - hidden * (inverse * inverse * inverse * statistic)
        ).astype(jnp.bfloat16)
        return carry

    lax.fori_loop(0, tokens // TILE_ROWS, finish, 0)

    for step in range(1, peers):
        source = lax.rem(place + peers - step, peers)
        for copy in head_copies(place, step, source, source):
            copy.wait_recv()
        for copy in head_copies(lax.rem(place + step, peers), step, place, source):
            copy.wait_send()
    for copy in own_heads:
        copy.wait()
    for away in range(1, lines):
        meta_copy(away).wait_send()
        for part in range(FEATURE_CHUNKS):
            line_copy(away, part).wait_send()
        for half in range(halves):
            sum_copy(away, half).wait_send()
    for phase in range(2):
        for step in range(1, members):
            for part in range(halves, FEATURE_CHUNKS):
                out_copy(phase, part, step).wait_send()
            for half in range(halves):
                back_copy(phase, half, step).wait_send()


def moe_input_grads(
    hidden,
    grad_out,
    norm_gain,
    expert_ids,
    gate_weights,
    w_gate,
    w_up,
    w_down,
    queries,
    attn_out,
    keys,
    values,
    lines,
    cols,
    capacity,
):
    tokens, width = hidden.shape
    ff = w_gate.shape[2]
    peers = lines * cols
    experts = 2 * cols * peers
    members = 2 * cols * cols
    chunk = 2 * width // FEATURE_CHUNKS
    halves = FEATURE_CHUNKS // 2
    rows = members * 2 * capacity
    tiles = ff // FF_TILE
    head_width = queries.shape[1] // peers
    low, full = jnp.bfloat16, jnp.float32
    dma = pltpu.SemaphoreType.DMA
    vmem = pl.BlockSpec(memory_space=pltpu.VMEM)
    hbm = pl.BlockSpec(memory_space=pl.ANY)
    sequence = peers * tokens
    return pl.pallas_call(
        functools.partial(moe_kernel, lines, cols, capacity),
        out_shape=(
            jax.ShapeDtypeStruct((tokens, width), low),
            jax.ShapeDtypeStruct((sequence, head_width), low),
            jax.ShapeDtypeStruct((sequence, head_width), low),
            jax.ShapeDtypeStruct((sequence, HEAD_SIZE), low),
            jax.ShapeDtypeStruct((sequence, HEAD_SIZE), low),
        ),
        in_specs=[vmem] * 5 + [hbm] * 7,
        out_specs=[vmem] + [hbm] * 4,
        scratch_shapes=[
            pltpu.VMEM((2, FEATURE_CHUNKS, 2 * tokens, chunk), low),
            pltpu.VMEM((lines, 2 * experts, tokens), full),
            pltpu.VMEM((2, rows, 2 * tokens), low),
            pltpu.VMEM((2, 2 * tokens, rows), low),
            pltpu.VMEM((2, rows, 128), full),
            pltpu.VMEM((2, FEATURE_CHUNKS, rows, chunk), low),
            pltpu.VMEM((2, FEATURE_CHUNKS, rows, chunk), low),
            pltpu.VMEM((tiles, width, FF_TILE), low),
            pltpu.VMEM((tiles, width, FF_TILE), low),
            pltpu.VMEM((tiles, FF_TILE, width), low),
            pltpu.VMEM((tiles, rows, FF_TILE), low),
            pltpu.VMEM((tiles, rows, FF_TILE), low),
            pltpu.VMEM((tiles, rows, FF_TILE), full),
            pltpu.VMEM((tiles, rows, FF_TILE), full),
            pltpu.VMEM((2, halves, rows, chunk), low),
            pltpu.VMEM((lines - 1, halves, tokens, chunk), low),
            pltpu.VMEM((lines - 1, halves, tokens, chunk), low),
            pltpu.VMEM((halves, tokens, chunk), full),
            dma((3, tiles)),
            dma((lines, FEATURE_CHUNKS)),
            dma((lines, FEATURE_CHUNKS)),
            dma((lines,)),
            dma((lines,)),
            dma((2, FEATURE_CHUNKS, members)),
            dma((2, FEATURE_CHUNKS, members)),
            dma((2, halves, members)),
            dma((2, halves, members)),
            dma((lines - 1, halves)),
            dma((lines - 1, halves)),
            dma((4, peers)),
            dma((4, peers)),
            dma((4,)),
        ],
        compiler_params=pltpu.CompilerParams(
            collective_id=0, has_side_effects=True, vmem_limit_bytes=60 * 2**20
        ),
        cost_estimate=pl.CostEstimate(
            flops=20 * rows * width * ff, bytes_accessed=400 * 2**20, transcendentals=0
        ),
    )(
        hidden,
        grad_out,
        norm_gain.reshape(1, width),
        expert_ids.T,
        gate_weights.T,
        w_gate,
        w_up,
        w_down,
        queries,
        attn_out,
        keys,
        values,
    )


def attention_kernel(
    lines,
    cols,
    resid_ref,
    w_out_ref,
    query_ref,
    output_ref,
    key_ref,
    value_ref,
    lse_ref,
    grad_query,
    grad_key,
    grad_value,
    resid_all,
    key_turned,
    query_rows,
    grad_rows,
    query_sum,
    query_parts,
    key_sum,
    value_sum,
    kv_out,
    kv_in,
    resid_send,
    resid_recv,
    query_send,
    query_recv,
    kv_send,
    kv_recv,
    own_sem,
):
    group = lax.axis_index("grp")
    place = lax.axis_index("inner")
    plane, col = place // cols, place % cols
    tokens, width = resid_ref.shape
    halves, part_width = resid_all.shape[2], resid_all.shape[4]
    head_width = query_ref.shape[1]
    heads = head_width // HEAD_SIZE
    peers = lines * cols
    scale = float(HEAD_SIZE) ** (-0.5)
    key_block = 2 * tokens

    def far_plane(away):
        return (plane, plane + 1 - 2 * (plane % 2), (plane + 2) % 4, 3 - plane)[away]

    def source_of(side, away):
        return far_plane(away) * cols + (col if side == 0 else 1 - col)

    def remote(source, target, send, recv, to):
        return pltpu.make_async_remote_copy(
            src_ref=source,
            dst_ref=target,
            send_sem=send,
            recv_sem=recv,
            device_id=(group, to),
            device_id_type=MESH_ID,
        )

    def resid_copy(side, away, half):
        return remote(
            resid_all.at[0, away if side else 0, half],
            resid_all.at[side, away, half],
            resid_send.at[side, away, half],
            resid_recv.at[side, away, half],
            source_of(1, 0) if side else source_of(0, away),
        )

    own_columns = pl.ds(pl.multiple_of(place * head_width, head_width), head_width)

    def query_copy(side, away):
        return remote(
            query_parts.at[side, away],
            grad_query.at[:, own_columns],
            query_send.at[side, away],
            query_recv.at[side, away],
            source_of(side, away),
        )

    def query_landing(side, away):
        source = source_of(side, away)
        columns = pl.ds(pl.multiple_of(source * head_width, head_width), head_width)
        return remote(
            query_parts.at[side, away],
            grad_query.at[:, columns],
            query_send.at[side, away],
            query_recv.at[side, away],
            source,
        )

    def kv_copy(side, away):
        return remote(
            kv_out.at[side, away],
            kv_in.at[side, away],
            kv_send.at[side, away],
            kv_recv.at[side, away],
            source_of(side, away),
        )

    others = [(side, away) for side in range(cols) for away in range(lines) if side or away]
    barrier = pltpu.get_barrier_semaphore()
    for side, away in others:
        pl.semaphore_signal(
            barrier, inc=1, device_id=(group, source_of(side, away)), device_id_type=MESH_ID
        )
    for half in range(halves):
        resid_all[0, 0, half] = resid_ref[:, half * part_width : (half + 1) * part_width]
    pl.semaphore_wait(barrier, peers - 1)
    for half in range(halves):
        resid_copy(1, 0, half).start()
        for away in range(1, lines):
            resid_copy(0, away, half).start()

    key_turned[...] = key_ref[...].astype(jnp.float32).T.astype(jnp.bfloat16)
    key_sum[...] = jnp.zeros_like(key_sum)
    value_sum[...] = jnp.zeros_like(value_sum)

    def attend(side, away):
        source = source_of(side, away)
        start = pl.multiple_of(source * tokens, tokens)
        rows = pl.ds(start, tokens)
        grad = sum(
            contract_last(
                resid_all[side, away, half],
                w_out_ref[:, half * part_width : (half + 1) * part_width],
            )
            for half in range(halves)
        ).astype(jnp.bfloat16)
        deltas, lses = [], []
        for head in range(heads):
            columns = slice(head * HEAD_SIZE, (head + 1) * HEAD_SIZE)
            lanes = slice(head * tokens, (head + 1) * tokens)
            query_rows[lanes, :] = query_ref[rows, columns]
            grad_rows[lanes, :] = grad[:, columns]
            product = grad[:, columns].astype(jnp.float32) * output_ref[rows, columns].astype(
                jnp.float32
            )
            deltas.append(jnp.sum(product.T, axis=0, keepdims=True))
            lses.append(lse_ref[head : head + 1, rows])
        delta = jnp.concatenate(deltas, axis=1)
        lse = jnp.concatenate(lses, axis=1)
        lane = lax.broadcasted_iota(jnp.int32, (1, heads * tokens), 1)
        token = start + lane % tokens
        query_sum[...] = jnp.zeros_like(query_sum)

        def keys_of(index, carry):
            first = pl.multiple_of(index * key_block, key_block)
            seen = pl.ds(first, key_block)
            scores = contract_last(key_ref[seen, :], query_rows[...]) * scale
            position = first + lax.broadcasted_iota(jnp.int32, (key_block, 1), 0)
            probs = jnp.where(position <= token, jnp.exp(scores - lse), 0.0)
            grad_probs = contract_last(value_ref[seen, :], grad_rows[...])
            grad_scores = (probs * (grad_probs - delta)).astype(jnp.bfloat16)
            value_sum[seen, :] += jnp.dot(
                probs.astype(jnp.bfloat16), grad_rows[...], preferred_element_type=jnp.float32
            )
            key_sum[seen, :] += jnp.dot(
                grad_scores, query_rows[...], preferred_element_type=jnp.float32
            )
            query_sum[...] += jnp.dot(
                key_turned[:, seen], grad_scores, preferred_element_type=jnp.float32
            )
            return carry

        lax.fori_loop(0, source // 2 + 1, keys_of, 0)
        for head in range(heads):
            lanes = slice(head * tokens, (head + 1) * tokens)
            query_parts[side, away, :, head * HEAD_SIZE : (head + 1) * HEAD_SIZE] = (
                (query_sum[:, lanes] * scale).T.astype(jnp.bfloat16)
            )
        if side or away:
            query_copy(side, away).start()

    def forward(away):
        for half in range(halves):
            resid_copy(0, away, half).wait_recv()
            resid_copy(1, away, half).start()

    attend(0, 0)
    own_query = pltpu.make_async_copy(
        query_parts.at[0, 0], grad_query.at[:, own_columns], own_sem.at[0]
    )
    own_query.start()
    for away in range(1, lines):
        forward(away)
        for half in range(halves):
            resid_copy(1, away - 1, half).wait_recv()
        attend(1, away - 1)
        attend(0, away)
    for half in range(halves):
        resid_copy(1, lines - 1, half).wait_recv()
    attend(1, lines - 1)

    for side in range(cols):
        for away in range(lines):
            start = pl.multiple_of(source_of(side, away) * tokens, tokens)
            rows = pl.ds(start, tokens)
            kept = kv_in if (side, away) == (0, 0) else kv_out
            kept[side, away, :, :HEAD_SIZE] = (key_sum[rows, :] * scale).astype(jnp.bfloat16)
            kept[side, away, :, HEAD_SIZE:] = value_sum[rows, :].astype(jnp.bfloat16)
            if side or away:
                kv_copy(side, away).start()
    for away in range(lines):
        for side in range(cols):
            if side or away:
                kv_copy(side, away).wait_recv()
        head = pl.ds(pl.multiple_of(far_plane(away) * HEAD_SIZE, HEAD_SIZE), HEAD_SIZE)
        total = sum(kv_in[side, away].astype(jnp.float32) for side in range(cols))
        grad_key[:, head] = total[:, :HEAD_SIZE].astype(jnp.bfloat16)
        grad_value[:, head] = total[:, HEAD_SIZE:].astype(jnp.bfloat16)
    own_query.wait()
    for side, away in others:
        query_landing(side, away).wait_recv()
        query_copy(side, away).wait_send()
        kv_copy(side, away).wait_send()
        for half in range(halves):
            resid_copy(side, away, half).wait_send()


def attention_grads(
    grad_resid, w_out, head_query, head_output, head_key, head_value, lse, lines, cols
):
    tokens, width = grad_resid.shape
    sequence, head_width = head_query.shape
    heads = head_width // HEAD_SIZE
    peers = lines * cols
    halves = 2
    low, full = jnp.bfloat16, jnp.float32
    dma = pltpu.SemaphoreType.DMA
    vmem = pl.BlockSpec(memory_space=pltpu.VMEM)
    hbm = pl.BlockSpec(memory_space=pl.ANY)
    kv_shape = jax.ShapeDtypeStruct((tokens, KEY_VALUE_HEADS * HEAD_SIZE), low)
    return pl.pallas_call(
        functools.partial(attention_kernel, lines, cols),
        out_shape=(
            jax.ShapeDtypeStruct((tokens, peers * head_width), low),
            kv_shape,
            kv_shape,
        ),
        in_specs=[vmem] * 7,
        out_specs=[hbm, vmem, vmem],
        scratch_shapes=[
            pltpu.VMEM((cols, lines, halves, tokens, width // halves), low),
            pltpu.VMEM((HEAD_SIZE, sequence), low),
            pltpu.VMEM((heads * tokens, HEAD_SIZE), low),
            pltpu.VMEM((heads * tokens, HEAD_SIZE), low),
            pltpu.VMEM((HEAD_SIZE, heads * tokens), full),
            pltpu.VMEM((cols, lines, tokens, head_width), low),
            pltpu.VMEM((sequence, HEAD_SIZE), full),
            pltpu.VMEM((sequence, HEAD_SIZE), full),
            pltpu.VMEM((cols, lines, tokens, 2 * HEAD_SIZE), low),
            pltpu.VMEM((cols, lines, tokens, 2 * HEAD_SIZE), low),
            dma((cols, lines, halves)),
            dma((cols, lines, halves)),
            dma((cols, lines)),
            dma((cols, lines)),
            dma((cols, lines)),
            dma((cols, lines)),
            dma((1,)),
        ],
        compiler_params=pltpu.CompilerParams(
            collective_id=1, has_side_effects=True, vmem_limit_bytes=48 * 2**20
        ),
        cost_estimate=pl.CostEstimate(
            flops=10 * sequence * sequence * head_width,
            bytes_accessed=100 * 2**20,
            transcendentals=0,
        ),
    )(grad_resid, w_out, head_query, head_output, head_key, head_value, lse)


def per_device(
    grad_out,
    hidden,
    norm_gain,
    expert_ids,
    gate_weights,
    w_gate,
    w_up,
    w_down,
    w_out,
    queries,
    keys,
    values,
    attn_out,
    lse,
):
    token_rows, width = hidden.shape
    topk = expert_ids.shape[1]
    groups = lax.axis_size("grp")
    inner_product = lax.axis_size("inner")
    experts_all = w_gate.shape[0] * groups * inner_product
    capacity = max(2, 5 * token_rows * topk // (4 * experts_all))
    cols = groups // 2
    lines = inner_product // cols if cols else 0
    kernel_plan = (
        cols == 2
        and lines == 4
        and inner_product == lines * cols
        and w_gate.shape[0] == 1
        and (2 * capacity) % 16 == 0
        and token_rows == 128
        and width % 1024 == 0
        and w_gate.shape[2] % FF_TILE == 0
        and inner_product == KEY_VALUE_HEADS * cols
    )
    if kernel_plan:
        grad_resid, head_query, head_output, head_key, head_value = moe_input_grads(
            hidden,
            grad_out,
            norm_gain,
            expert_ids,
            gate_weights,
            w_gate,
            w_up,
            w_down,
            queries,
            attn_out,
            keys,
            values,
            lines,
            cols,
            capacity,
        )
        grads = attention_grads(
            grad_resid, w_out, head_query, head_output, head_key, head_value, lse, lines, cols
        )
        return (grad_resid,) + tuple(grads)
    hidden_f = hidden.astype(jnp.float32)
    inverse = lax.rsqrt(jnp.mean(hidden_f * hidden_f, axis=1, keepdims=True) + EPSILON)
    normed = (hidden_f * inverse * norm_gain).astype(jnp.bfloat16)
    upstream = grad_out.astype(jnp.float32)
    flat_count = token_rows * topk
    flat_ids = expert_ids.reshape(-1)
    one_hot = (flat_ids[:, None] == jnp.arange(experts_all, dtype=jnp.int32)[None, :]).astype(
        jnp.int32
    )
    before = jnp.tril(jnp.ones((flat_count, flat_count), jnp.bfloat16), -1)
    ahead = jnp.dot(
        before, one_hot.astype(jnp.bfloat16), preferred_element_type=jnp.float32
    ).astype(jnp.int32)
    slot_rank = jnp.sum(ahead * one_hot, axis=1)
    target = flat_ids * capacity + slot_rank
    owner = (
        jnp.full((experts_all * capacity,), flat_count, jnp.int32)
        .at[target]
        .set(jnp.arange(flat_count, dtype=jnp.int32))
    )
    source_tok = owner // topk
    scaled = (
        (upstream[:, None, :] * gate_weights[:, :, None])
        .reshape(flat_count, width)
        .astype(jnp.bfloat16)
    )
    zero_row = jnp.zeros((1, width), jnp.bfloat16)
    slot_inputs = jnp.concatenate([normed, zero_row], axis=0)[source_tok]
    slot_grads = jnp.concatenate([scaled, zero_row], axis=0)[owner]
    outgoing = jnp.concatenate([slot_inputs, slot_grads], axis=1).reshape(
        experts_all, capacity, 2 * width
    )
    returned = lax.all_to_all(
        expert_grads(
            lax.all_to_all(outgoing, ("grp", "inner"), split_axis=0, concat_axis=0, tiled=True),
            w_gate,
            w_up,
            w_down,
        ),
        ("grp", "inner"),
        split_axis=0,
        concat_axis=0,
        tiled=True,
    )
    expert_rows = returned.reshape(-1, width)[target].astype(jnp.float32)
    grad_normed = jnp.sum(expert_rows.reshape(token_rows, topk, width), axis=1)
    gained = grad_normed * norm_gain
    statistic = jnp.mean(gained * hidden_f, axis=1, keepdims=True)
    grad_resid = (
        upstream + inverse * gained - hidden_f * inverse * inverse * inverse * statistic
    ).astype(jnp.bfloat16)
    head_width = queries.shape[1] // inner_product
    per_head = head_width // HEAD_SIZE
    shared_portion = inner_product // KEY_VALUE_HEADS
    key_value_pairs = jnp.concatenate(
        [
            keys.reshape(token_rows, KEY_VALUE_HEADS, 1, HEAD_SIZE),
            values.reshape(token_rows, KEY_VALUE_HEADS, 1, HEAD_SIZE),
        ],
        axis=2,
    )
    key_value_broadcast = jnp.broadcast_to(
        key_value_pairs[:, :, None], (token_rows, KEY_VALUE_HEADS, shared_portion, 2, HEAD_SIZE)
    ).reshape(token_rows, inner_product * 2 * HEAD_SIZE)
    head_query, head_output, head_kv = (
        lax.all_to_all(queries, "inner", split_axis=1, concat_axis=0, tiled=True),
        lax.all_to_all(attn_out, "inner", split_axis=1, concat_axis=0, tiled=True),
        lax.all_to_all(key_value_broadcast, "inner", split_axis=1, concat_axis=0, tiled=True),
    )
    head_grad = contract_last(
        lax.all_gather(grad_resid, "inner", axis=0, tiled=True), w_out
    ).astype(jnp.bfloat16)
    seq_len = head_query.shape[0]
    head_key = head_kv[:, :HEAD_SIZE]
    head_value = head_kv[:, HEAD_SIZE:]
    lse_rows = lse.T
    scale = float(HEAD_SIZE) ** (-0.5)
    blocks = 1
    while blocks < 8 and seq_len % (2 * blocks) == 0 and (seq_len // (2 * blocks) >= 512):
        blocks = blocks * 2
    block_len = seq_len // blocks
    grad_key_acc = jnp.zeros((seq_len, HEAD_SIZE), jnp.float32)
    grad_value_acc = jnp.zeros((seq_len, HEAD_SIZE), jnp.float32)
    query_parts = []
    for block_index in range(blocks):
        low = block_index * block_len
        high = low + block_len
        block_query = head_query[low:high].reshape(block_len * per_head, HEAD_SIZE)
        block_output = head_output[low:high].reshape(block_len * per_head, HEAD_SIZE)
        block_grad = head_grad[low:high].reshape(block_len * per_head, HEAD_SIZE)
        block_lse = lse_rows[low:high].reshape(-1)
        seen_key = head_key[:high]
        seen_value = head_value[:high]
        scores = contract_last(block_query, seen_key) * scale
        row_position = low + jnp.arange(block_len * per_head, dtype=jnp.int32) // per_head
        visible = jnp.arange(high, dtype=jnp.int32)[None, :] <= row_position[:, None]
        probs = jnp.where(visible, jnp.exp(scores - block_lse[:, None]), 0.0)
        grad_probs = contract_last(block_grad, seen_value)
        delta = jnp.sum(
            block_grad.astype(jnp.float32) * block_output.astype(jnp.float32), axis=1, keepdims=True
        )
        grad_scores = (probs * (grad_probs - delta)).astype(jnp.bfloat16)
        query_part = jnp.dot(grad_scores, seen_key, preferred_element_type=jnp.float32) * scale
        query_parts.append(query_part.reshape(block_len, head_width))
        grad_key_acc = grad_key_acc.at[:high].add(contract_first(grad_scores, block_query) * scale)
        grad_value_acc = grad_value_acc.at[:high].add(
            contract_first(probs.astype(jnp.bfloat16), block_grad)
        )
    grad_query_heads = jnp.concatenate(query_parts, axis=0)
    kv_heads = jnp.concatenate([grad_key_acc, grad_value_acc], axis=1)
    token_query, token_key_value = (
        lax.all_to_all(
            grad_query_heads.astype(jnp.bfloat16), "inner", split_axis=0, concat_axis=1, tiled=True
        ).astype(grad_query_heads.dtype),
        lax.all_to_all(
            kv_heads.astype(jnp.bfloat16), "inner", split_axis=0, concat_axis=1, tiled=True
        ).astype(kv_heads.dtype),
    )
    summed_total = jnp.sum(
        token_key_value.reshape(token_rows, KEY_VALUE_HEADS, shared_portion, 2, HEAD_SIZE), axis=2
    )
    keys_gradient = (
        summed_total[:, :, 0].reshape(token_rows, KEY_VALUE_HEADS * HEAD_SIZE).astype(jnp.bfloat16)
    )
    values_gradient = (
        summed_total[:, :, 1].reshape(token_rows, KEY_VALUE_HEADS * HEAD_SIZE).astype(jnp.bfloat16)
    )
    return (grad_resid, token_query.astype(jnp.bfloat16), keys_gradient, values_gradient)


def solution(mesh):
    placed = (
        P(("grp", "inner"), None),
        P(("grp", "inner"), None),
        P(),
        P(("grp", "inner"), None),
        P(("grp", "inner"), None),
        P(("grp", "inner"), None, None),
        P(("grp", "inner"), None, None),
        P(("grp", "inner"), None, None),
        P("inner", None),
        P(("grp", "inner"), None),
        P(("grp", "inner"), None),
        P(("grp", "inner"), None),
        P(("grp", "inner"), None),
        P("inner", "grp"),
    )
    return jax.shard_map(
        per_device,
        mesh=mesh,
        in_specs=placed,
        out_specs=(
            P(("grp", "inner"), None),
            P(("grp", "inner"), None),
            P(("grp", "inner"), None),
            P(("grp", "inner"), None),
        ),
        check_vma=False,
    )
```

```python
import functools

import jax
import jax.numpy as jnp
from jax import lax
from jax.experimental import pallas as pl
from jax.experimental.pallas import tpu as pltpu
from jax.sharding import PartitionSpec as P

KEY_VALUE_HEADS = 4
HEAD_SIZE = 128


EPSILON = 1e-06


def contract_last(left, right):
    return lax.dot_general(
        left, right, (((1,), (1,)), ((), ())), preferred_element_type=jnp.float32
    )


def contract_first(left, right):
    return lax.dot_general(
        left, right, (((0,), (0,)), ((), ())), preferred_element_type=jnp.float32
    )


def expert_grads(received, w_gate, w_up, w_down):
    local = w_gate.shape[0]
    width = w_gate.shape[1]
    shaped = received.reshape((-1, local) + received.shape[1:])
    inputs = shaped[..., :width]
    upstream = shaped[..., width:]
    gate_pre = jnp.einsum("nlcd,ldf->nlcf", inputs, w_gate, preferred_element_type=jnp.float32)
    up_pre = jnp.einsum("nlcd,ldf->nlcf", inputs, w_up, preferred_element_type=jnp.float32)
    back_hidden = jnp.einsum("nlcd,lfd->nlcf", upstream, w_down, preferred_element_type=jnp.float32)
    sigmoid = jax.nn.sigmoid(gate_pre)
    grad_gate = (back_hidden * up_pre * sigmoid * (1.0 + gate_pre * (1.0 - sigmoid))).astype(
        jnp.bfloat16
    )
    grad_up = (back_hidden * gate_pre * sigmoid).astype(jnp.bfloat16)
    grad_in = jnp.einsum("nlcf,ldf->nlcd", grad_gate, w_gate, preferred_element_type=jnp.float32)
    grad_in = grad_in + jnp.einsum(
        "nlcf,ldf->nlcd", grad_up, w_up, preferred_element_type=jnp.float32
    )
    return grad_in.astype(jnp.bfloat16).reshape(received.shape[:-1] + (width,))


MESH_ID = pl.DeviceIdType.MESH
FEATURE_CHUNKS = 4
FF_TILE = 256
TILE_ROWS = 16


def moe_kernel(
    lines,
    cols,
    capacity,
    hidden_ref,
    grad_ref,
    gain_ref,
    ids_ref,
    gates_ref,
    gate_hbm,
    up_hbm,
    down_hbm,
    query_hbm,
    output_hbm,
    key_hbm,
    value_hbm,
    out_ref,
    head_query,
    head_output,
    head_key,
    head_value,
    block,
    meta,
    pick,
    pick_back,
    weight,
    outgoing,
    received,
    w_gate,
    w_up,
    w_down,
    hidden_gate,
    hidden_up,
    slope_gate,
    slope_up,
    returned,
    partial,
    arrived,
    own_sum,
    weight_sem,
    line_send,
    line_recv,
    meta_send,
    meta_recv,
    out_send,
    out_recv,
    back_send,
    back_recv,
    sum_send,
    sum_recv,
    head_send,
    head_recv,
    head_own,
):
    group = lax.axis_index("grp")
    place = lax.axis_index("inner")
    plane, col = place // cols, place % cols
    groups = 2 * cols
    members = groups * cols
    me = group * cols + col
    tokens, width = hidden_ref.shape
    chunk = 2 * width // FEATURE_CHUNKS
    halves = FEATURE_CHUNKS // 2
    pair_rows = 2 * capacity
    peers = lines * cols
    tiles = w_gate.shape[0]

    def member(number):
        return (number // cols, plane * cols + number % cols)

    def ahead(step):
        return member(lax.rem(me + step, members))

    def behind(step):
        return member(lax.rem(me + members - step, members))

    def across(away):
        far = (plane, (plane + 2) % 4, plane + 1 - 2 * (plane % 2), 3 - plane)[away]
        return (group, far * cols + col)

    def remote(source, target, send, recv, device):
        return pltpu.make_async_remote_copy(
            src_ref=source,
            dst_ref=target,
            send_sem=send,
            recv_sem=recv,
            device_id=device,
            device_id_type=MESH_ID,
        )

    def line_copy(away, part):
        rows = pl.ds((away % 2) * tokens, tokens)
        return remote(
            block.at[0, part, pl.ds(0, tokens)],
            block.at[away // 2, part, rows],
            line_send.at[away, part],
            line_recv.at[away, part],
            across(away),
        )

    def meta_copy(away):
        return remote(
            meta.at[0], meta.at[away], meta_send.at[away], meta_recv.at[away], across(away)
        )

    def step_rows(step):
        return pl.ds(step * pair_rows, pair_rows)

    def out_copy(phase, part, step):
        return remote(
            outgoing.at[phase, part, step_rows(step)],
            received.at[phase, part, step_rows(step)],
            out_send.at[phase, part, step],
            out_recv.at[phase, part, step],
            ahead(step),
        )

    tile_width = min(chunk, 512)
    pieces = [
        (half, piece) for half in range(halves) for piece in range(chunk // tile_width)
    ]

    def piece_columns(piece):
        return pl.ds(piece * tile_width, tile_width)

    def back_copy(phase, half, piece, step):
        columns = piece_columns(piece)
        return remote(
            outgoing.at[phase, half, step_rows(step), columns],
            returned.at[phase, half, step_rows(step), columns],
            back_send.at[phase, half, piece, step],
            back_recv.at[phase, half, piece, step],
            behind(step),
        )

    def sum_copy(away, half, piece):
        columns = piece_columns(piece)
        return remote(
            partial.at[away - 1, half, :, columns],
            arrived.at[away - 1, half, :, columns],
            sum_send.at[away - 1, half, piece],
            sum_recv.at[away - 1, half, piece],
            across(away),
        )

    head_width = head_query.shape[1]
    kv_width = head_key.shape[1]
    share = peers // (key_hbm.shape[1] // kv_width)

    def head_pairs(to, source):
        columns = pl.ds(pl.multiple_of(to * head_width, head_width), head_width)
        kv_columns = pl.ds(pl.multiple_of((to // share) * kv_width, kv_width), kv_width)
        rows = pl.ds(pl.multiple_of(source * tokens, tokens), tokens)
        return (
            (query_hbm.at[:, columns], head_query.at[rows]),
            (output_hbm.at[:, columns], head_output.at[rows]),
            (key_hbm.at[:, kv_columns], head_key.at[rows]),
            (value_hbm.at[:, kv_columns], head_value.at[rows]),
        )

    def head_copies(to, slot, source, target):
        return [
            remote(
                src, dst, head_send.at[number, slot], head_recv.at[number, slot], (group, target)
            )
            for number, (src, dst) in enumerate(head_pairs(to, source))
        ]

    own_heads = [
        pltpu.make_async_copy(src, dst, head_own.at[number])
        for number, (src, dst) in enumerate(head_pairs(place, place))
    ]

    barrier = pltpu.get_barrier_semaphore()
    for step in range(1, peers):
        pl.semaphore_signal(
            barrier, inc=1, device_id=(group, lax.rem(place + step, peers)), device_id_type=MESH_ID
        )
    for step in range(1, members):
        pl.semaphore_signal(barrier, inc=1, device_id=ahead(step), device_id_type=MESH_ID)

    weight_copies = []
    for tile in range(tiles):
        columns = pl.ds(tile * FF_TILE, FF_TILE)
        weight_copies += [
            pltpu.make_async_copy(
                gate_hbm.at[0, :, columns], w_gate.at[tile], weight_sem.at[0, tile]
            ),
            pltpu.make_async_copy(up_hbm.at[0, :, columns], w_up.at[tile], weight_sem.at[1, tile]),
            pltpu.make_async_copy(
                down_hbm.at[0, columns, :], w_down.at[tile], weight_sem.at[2, tile]
            ),
        ]
    for copy in weight_copies:
        copy.start()

    def norm_rows(index, carry):
        rows = pl.ds(pl.multiple_of(index * TILE_ROWS, TILE_ROWS), TILE_ROWS)
        hidden = hidden_ref[rows, :].astype(jnp.float32)
        inverse = lax.rsqrt(jnp.mean(hidden * hidden, axis=1, keepdims=True) + EPSILON)
        normed = (hidden * inverse * gain_ref[...]).astype(jnp.bfloat16)
        upstream = grad_ref[rows, :]
        for half in range(halves):
            columns = slice(half * chunk, (half + 1) * chunk)
            block[0, half, rows, :] = normed[:, columns]
            block[0, halves + half, rows, :] = upstream[:, columns]
        return carry

    lax.fori_loop(0, tokens // TILE_ROWS, norm_rows, 0)

    experts = meta.shape[1] // 2
    topk = ids_ref.shape[0]
    expert = lax.broadcasted_iota(jnp.int32, (experts, tokens), 0)
    mine = jnp.zeros((experts, tokens), jnp.float32)
    gates = jnp.zeros((experts, tokens), jnp.float32)
    for slot in range(topk):
        hit = ids_ref[slot : slot + 1, :] == expert
        mine = mine + jnp.where(hit, 1.0, 0.0)
        gates = gates + jnp.where(hit, gates_ref[slot : slot + 1, :], 0.0)
    earlier = lax.broadcasted_iota(jnp.int32, (tokens, tokens), 0)
    later = lax.broadcasted_iota(jnp.int32, (tokens, tokens), 1)
    before = jnp.where(earlier < later, 1.0, 0.0).astype(jnp.bfloat16)
    rank = jnp.dot(mine.astype(jnp.bfloat16), before, preferred_element_type=jnp.float32)
    meta[0, :experts, :] = jnp.where(mine > 0.5, rank, -1.0)
    meta[0, experts:, :] = gates

    pl.semaphore_wait(barrier, members + peers - 2)
    near_step = 1 + (peers - 2) * col

    def start_heads(step):
        to = lax.rem(place + step, peers)
        for copy in head_copies(to, step, place, to):
            copy.start()

    for away in range(1, lines):
        meta_copy(away).start()
    line_copy(1, 0).start()
    start_heads(near_step)
    line_copy(1, 1).start()

    def build_pick(phase):
        lane = lax.broadcasted_iota(jnp.int32, (1, 2 * tokens), 1)
        shift = jnp.where(lane >= tokens, float(capacity), 0.0)
        row = lax.broadcasted_iota(jnp.int32, (pair_rows, 2 * tokens), 0).astype(jnp.float32)
        for step in range(members):
            number = lax.rem(me + step, members)
            named = (number // cols) * peers + plane * cols + number % cols
            slots = jnp.concatenate(
                [meta[2 * phase + j, pl.ds(named, 1), :] for j in range(2)], axis=1
            )
            goal = jnp.where(slots >= 0.0, slots + shift, -1.0)
            hot = jnp.where(row == goal, 1.0, 0.0)
            rows = slice(step * pair_rows, (step + 1) * pair_rows)
            pick[phase, rows, :] = hot.astype(jnp.bfloat16)

    def build_weight(phase):
        for step in range(members):
            number = lax.rem(me + step, members)
            named = (number // cols) * peers + plane * cols + number % cols
            shares = jnp.concatenate(
                [meta[2 * phase + j, pl.ds(experts + named, 1), :] for j in range(2)], axis=1
            )
            rows = slice(step * pair_rows, (step + 1) * pair_rows)
            hot = pick[phase, rows, :].astype(jnp.float32)
            weight[phase, rows, :] = jnp.broadcast_to(
                jnp.sum(hot * shares, axis=1, keepdims=True), (pair_rows, 128)
            )
        pick_back[phase] = pick[phase].astype(jnp.float32).T.astype(jnp.bfloat16)

    def select(phase, part):
        def columns_of(index, carry):
            columns = pl.ds(pl.multiple_of(index * tile_width, tile_width), tile_width)
            rows = jnp.dot(
                pick[phase], block[phase, part, :, columns], preferred_element_type=jnp.float32
            )
            if part >= halves:
                rows = rows * weight[phase][:, :1]
            rows = rows.astype(jnp.bfloat16)
            outgoing[phase, part, :, columns] = rows
            received[phase, part, :pair_rows, columns] = rows[:pair_rows]
            return carry

        lax.fori_loop(0, chunk // tile_width, columns_of, 0)

    for phase in range(2):
        for part in range(FEATURE_CHUNKS):
            for away in (1,) if phase == 0 else (2, 3):
                if part == 0:
                    meta_copy(away).wait_recv()
                line_copy(away, part).wait_recv()
            if part == 0:
                build_pick(phase)
            select(phase, part)
            for step in range(1, members):
                out_copy(phase, part, step).start()
            if phase == 0:
                if part < 2:
                    line_copy(1, part + 2).start()
                for away in range(2, lines):
                    line_copy(away, part).start()
            if part == 0:
                build_weight(phase)

    for step in (peers - near_step,) + tuple(range(2, peers - 1)):
        start_heads(step)
    for copy in own_heads:
        copy.start()

    for copy in weight_copies:
        copy.wait()

    def expert_products(phase):
        def take(part):
            for step in range(1, members):
                out_copy(phase, part, step).wait_recv()

        for half in range(halves):
            take(half)

        def gate_tile(tile, carry):
            def product(weights):
                return sum(
                    jnp.dot(
                        received[phase, half],
                        weights[tile, half * chunk : (half + 1) * chunk, :],
                        preferred_element_type=jnp.float32,
                    )
                    for half in range(halves)
                )

            gate_pre = product(w_gate)
            up_pre = product(w_up)
            sigmoid = jax.nn.sigmoid(gate_pre)
            slope_gate[tile] = up_pre * sigmoid * (1.0 + gate_pre * (1.0 - sigmoid))
            slope_up[tile] = gate_pre * sigmoid
            return carry

        lax.fori_loop(0, tiles, gate_tile, 0)
        for half in range(halves):
            take(halves + half)

        def hidden_tile(tile, carry):
            back_hidden = sum(
                contract_last(
                    received[phase, halves + half],
                    w_down[tile, :, half * chunk : (half + 1) * chunk],
                )
                for half in range(halves)
            )
            hidden_gate[tile] = (back_hidden * slope_gate[tile]).astype(jnp.bfloat16)
            hidden_up[tile] = (back_hidden * slope_up[tile]).astype(jnp.bfloat16)
            return carry

        lax.fori_loop(0, tiles, hidden_tile, 0)
        for half, piece in pieces:
            if piece == 0:
                for step in range(1, members):
                    out_copy(phase, half, step).wait_send()
            columns = piece_columns(piece)
            rows = pl.ds(half * chunk + piece * tile_width, tile_width)

            def add_tile(tile):
                return contract_last(hidden_gate[tile], w_gate[tile, rows, :]) + contract_last(
                    hidden_up[tile], w_up[tile, rows, :]
                )

            total = sum(add_tile(tile) for tile in range(tiles)).astype(jnp.bfloat16)
            outgoing[phase, half, :, columns] = total
            returned[phase, half, :pair_rows, columns] = total[:pair_rows]
            for step in range(1, members):
                back_copy(phase, half, piece, step).start()

    def combine(phase):
        for half, piece in pieces:
            for step in range(1, members):
                back_copy(phase, half, piece, step).wait_recv()
            columns = piece_columns(piece)
            total = jnp.dot(
                pick_back[phase],
                returned[phase, half, :, columns],
                preferred_element_type=jnp.float32,
            )
            for j in range(2):
                rows = total[j * tokens : (j + 1) * tokens]
                away = 2 * phase + j
                if away:
                    partial[away - 1, half, :, columns] = rows.astype(jnp.bfloat16)
                    sum_copy(away, half, piece).start()
                else:
                    own_sum[half, :, columns] = rows

    for phase in range(2):
        expert_products(phase)
    for phase in range(2):
        combine(phase)

    for away in range(1, lines):
        for half, piece in pieces:
            sum_copy(away, half, piece).wait_recv()

    def finish(index, carry):
        rows = pl.ds(pl.multiple_of(index * TILE_ROWS, TILE_ROWS), TILE_ROWS)
        hidden = hidden_ref[rows, :].astype(jnp.float32)
        inverse = lax.rsqrt(jnp.mean(hidden * hidden, axis=1, keepdims=True) + EPSILON)
        grad_normed = []
        for half in range(halves):
            total = own_sum[half, rows, :]
            for away in range(1, lines):
                total = total + arrived[away - 1, half, rows, :].astype(jnp.float32)
            grad_normed.append(total)
        gained = jnp.concatenate(grad_normed, axis=1) * gain_ref[...]
        statistic = jnp.mean(gained * hidden, axis=1, keepdims=True)
        out_ref[rows, :] = (
            grad_ref[rows, :].astype(jnp.float32)
            + inverse * gained
            - hidden * (inverse * inverse * inverse * statistic)
        ).astype(jnp.bfloat16)
        return carry

    lax.fori_loop(0, tokens // TILE_ROWS, finish, 0)

    for step in range(1, peers):
        source = lax.rem(place + peers - step, peers)
        for copy in head_copies(place, step, source, source):
            copy.wait_recv()
        for copy in head_copies(lax.rem(place + step, peers), step, place, source):
            copy.wait_send()
    for copy in own_heads:
        copy.wait()
    for away in range(1, lines):
        meta_copy(away).wait_send()
        for part in range(FEATURE_CHUNKS):
            line_copy(away, part).wait_send()
        for half, piece in pieces:
            sum_copy(away, half, piece).wait_send()
    for phase in range(2):
        for step in range(1, members):
            for part in range(halves, FEATURE_CHUNKS):
                out_copy(phase, part, step).wait_send()
            for half, piece in pieces:
                back_copy(phase, half, piece, step).wait_send()


def moe_input_grads(
    hidden,
    grad_out,
    norm_gain,
    expert_ids,
    gate_weights,
    w_gate,
    w_up,
    w_down,
    queries,
    attn_out,
    keys,
    values,
    lines,
    cols,
    capacity,
):
    tokens, width = hidden.shape
    ff = w_gate.shape[2]
    peers = lines * cols
    experts = 2 * cols * peers
    members = 2 * cols * cols
    chunk = 2 * width // FEATURE_CHUNKS
    halves = FEATURE_CHUNKS // 2
    rows = members * 2 * capacity
    tiles = ff // FF_TILE
    head_width = queries.shape[1] // peers
    low, full = jnp.bfloat16, jnp.float32
    dma = pltpu.SemaphoreType.DMA
    vmem = pl.BlockSpec(memory_space=pltpu.VMEM)
    hbm = pl.BlockSpec(memory_space=pl.ANY)
    sequence = peers * tokens
    return pl.pallas_call(
        functools.partial(moe_kernel, lines, cols, capacity),
        out_shape=(
            jax.ShapeDtypeStruct((tokens, width), low),
            jax.ShapeDtypeStruct((sequence, head_width), low),
            jax.ShapeDtypeStruct((sequence, head_width), low),
            jax.ShapeDtypeStruct((sequence, HEAD_SIZE), low),
            jax.ShapeDtypeStruct((sequence, HEAD_SIZE), low),
        ),
        in_specs=[vmem] * 5 + [hbm] * 7,
        out_specs=[vmem] + [hbm] * 4,
        scratch_shapes=[
            pltpu.VMEM((2, FEATURE_CHUNKS, 2 * tokens, chunk), low),
            pltpu.VMEM((lines, 2 * experts, tokens), full),
            pltpu.VMEM((2, rows, 2 * tokens), low),
            pltpu.VMEM((2, 2 * tokens, rows), low),
            pltpu.VMEM((2, rows, 128), full),
            pltpu.VMEM((2, FEATURE_CHUNKS, rows, chunk), low),
            pltpu.VMEM((2, FEATURE_CHUNKS, rows, chunk), low),
            pltpu.VMEM((tiles, width, FF_TILE), low),
            pltpu.VMEM((tiles, width, FF_TILE), low),
            pltpu.VMEM((tiles, FF_TILE, width), low),
            pltpu.VMEM((tiles, rows, FF_TILE), low),
            pltpu.VMEM((tiles, rows, FF_TILE), low),
            pltpu.VMEM((tiles, rows, FF_TILE), full),
            pltpu.VMEM((tiles, rows, FF_TILE), full),
            pltpu.VMEM((2, halves, rows, chunk), low),
            pltpu.VMEM((lines - 1, halves, tokens, chunk), low),
            pltpu.VMEM((lines - 1, halves, tokens, chunk), low),
            pltpu.VMEM((halves, tokens, chunk), full),
            dma((3, tiles)),
            dma((lines, FEATURE_CHUNKS)),
            dma((lines, FEATURE_CHUNKS)),
            dma((lines,)),
            dma((lines,)),
            dma((2, FEATURE_CHUNKS, members)),
            dma((2, FEATURE_CHUNKS, members)),
            dma((2, halves, chunk // min(chunk, 512), members)),
            dma((2, halves, chunk // min(chunk, 512), members)),
            dma((lines - 1, halves, chunk // min(chunk, 512))),
            dma((lines - 1, halves, chunk // min(chunk, 512))),
            dma((4, peers)),
            dma((4, peers)),
            dma((4,)),
        ],
        compiler_params=pltpu.CompilerParams(
            collective_id=0, has_side_effects=True, vmem_limit_bytes=60 * 2**20
        ),
        cost_estimate=pl.CostEstimate(
            flops=20 * rows * width * ff, bytes_accessed=400 * 2**20, transcendentals=0
        ),
    )(
        hidden,
        grad_out,
        norm_gain.reshape(1, width),
        expert_ids.T,
        gate_weights.T,
        w_gate,
        w_up,
        w_down,
        queries,
        attn_out,
        keys,
        values,
    )


def attention_kernel(
    lines,
    cols,
    resid_ref,
    w_out_ref,
    lse_ref,
    query_hbm,
    output_hbm,
    key_hbm,
    value_hbm,
    grad_query,
    grad_key,
    grad_value,
    query_ref,
    output_ref,
    key_ref,
    value_ref,
    resid_all,
    key_turned,
    query_rows,
    grad_rows,
    query_sum,
    query_parts,
    key_sum,
    value_sum,
    kv_out,
    kv_in,
    line_send,
    side_send,
    resid_recv,
    query_send,
    query_recv,
    kv_send,
    kv_recv,
    own_sem,
):
    group = lax.axis_index("grp")
    place = lax.axis_index("inner")
    plane, col = place // cols, place % cols
    tokens, width = resid_ref.shape
    halves, part_width = resid_all.shape[2], resid_all.shape[4]
    head_width = query_ref.shape[1]
    heads = head_width // HEAD_SIZE
    peers = lines * cols
    scale = float(HEAD_SIZE) ** (-0.5)
    key_block = 2 * tokens
    last = lines - 1

    def device_of(side, there):
        return there * cols + (col if side == 0 else 1 - col)

    def remote(source, target, send, recv, to):
        return pltpu.make_async_remote_copy(
            src_ref=source,
            dst_ref=target,
            send_sem=send,
            recv_sem=recv,
            device_id=(group, to),
            device_id_type=MESH_ID,
        )

    def line_copy(way, origin, half):
        there = jnp.clip(plane + (1 - 2 * way), 0, last)
        return remote(
            resid_all.at[0, origin, half],
            resid_all.at[0, origin, half],
            line_send.at[way, origin, half],
            resid_recv.at[0, origin, half],
            device_of(0, there),
        )

    def side_copy(origin, half):
        return remote(
            resid_all.at[0, origin, half],
            resid_all.at[1, origin, half],
            side_send.at[origin, half],
            resid_recv.at[1, origin, half],
            device_of(1, plane),
        )

    def columns_at(device):
        return pl.ds(pl.multiple_of(device * head_width, head_width), head_width)

    def query_copy(side, there):
        return remote(
            query_parts.at[side, there],
            grad_query.at[:, columns_at(place)],
            query_send.at[side, there],
            query_recv.at[side, plane],
            device_of(side, there),
        )

    def query_landing(side, there):
        source = device_of(side, there)
        return remote(
            query_parts.at[side, there],
            grad_query.at[:, columns_at(source)],
            query_send.at[side, there],
            query_recv.at[side, there],
            source,
        )

    def kv_copy(side, there):
        return remote(
            kv_out.at[side, there],
            kv_in.at[side, plane],
            kv_send.at[side, there],
            kv_recv.at[side, plane],
            device_of(side, there),
        )

    def kv_landing(side, there):
        return remote(
            kv_out.at[side, there],
            kv_in.at[side, there],
            kv_send.at[side, there],
            kv_recv.at[side, there],
            device_of(side, there),
        )

    def nth_plane(number):
        low = jnp.where(plane < 2, plane, last - plane)
        there = 1 - low if number == 1 else number
        return jnp.where(plane < 2, there, last - there)

    others = [(1, plane)]
    for number in range(1, lines):
        others += [(0, nth_plane(number)), (1, nth_plane(number))]

    inputs = [
        pltpu.make_async_copy(source, target, own_sem.at[1 + number])
        for number, (source, target) in enumerate(
            (
                (query_hbm, query_ref),
                (output_hbm, output_ref),
                (key_hbm, key_ref),
                (value_hbm, value_ref),
            )
        )
    ]
    for copy in inputs:
        copy.start()
    barrier = pltpu.get_barrier_semaphore()
    for side, there in others:
        pl.semaphore_signal(
            barrier, inc=1, device_id=(group, device_of(side, there)), device_id_type=MESH_ID
        )
    for half in range(halves):
        resid_all[0, plane, half] = resid_ref[:, half * part_width : (half + 1) * part_width]
    pl.semaphore_wait(barrier, peers - 1)
    for half in range(halves):

        @pl.when(plane < last)
        def _():
            line_copy(0, plane, half).start()

        @pl.when(plane > 0)
        def _():
            line_copy(1, plane, half).start()

        side_copy(plane, half).start()

    key_sum[...] = jnp.zeros_like(key_sum)
    value_sum[...] = jnp.zeros_like(value_sum)
    for copy in inputs:
        copy.wait()
    key_turned[...] = key_ref[...].astype(jnp.float32).T.astype(jnp.bfloat16)

    def attend(side, there):
        source = device_of(side, there)
        start = pl.multiple_of(source * tokens, tokens)
        rows = pl.ds(start, tokens)
        grad = sum(
            contract_last(
                resid_all[side, there, half],
                w_out_ref[:, half * part_width : (half + 1) * part_width],
            )
            for half in range(halves)
        ).astype(jnp.bfloat16)
        deltas, lses = [], []
        for head in range(heads):
            columns = slice(head * HEAD_SIZE, (head + 1) * HEAD_SIZE)
            lanes = slice(head * tokens, (head + 1) * tokens)
            query_rows[lanes, :] = query_ref[rows, columns]
            grad_rows[lanes, :] = grad[:, columns]
            product = grad[:, columns].astype(jnp.float32) * output_ref[rows, columns].astype(
                jnp.float32
            )
            deltas.append(jnp.sum(product.T, axis=0, keepdims=True))
            lses.append(lse_ref[head : head + 1, rows])
        delta = jnp.concatenate(deltas, axis=1)
        lse = jnp.concatenate(lses, axis=1)
        lane = lax.broadcasted_iota(jnp.int32, (1, heads * tokens), 1)
        token = start + lane % tokens
        query_sum[...] = jnp.zeros_like(query_sum)

        def keys_of(index, carry):
            first = pl.multiple_of(index * key_block, key_block)
            seen = pl.ds(first, key_block)
            scores = contract_last(key_ref[seen, :], query_rows[...]) * scale
            position = first + lax.broadcasted_iota(jnp.int32, (key_block, 1), 0)
            probs = jnp.where(position <= token, jnp.exp(scores - lse), 0.0)
            grad_probs = contract_last(value_ref[seen, :], grad_rows[...])
            grad_scores = (probs * (grad_probs - delta)).astype(jnp.bfloat16)
            value_sum[seen, :] += jnp.dot(
                probs.astype(jnp.bfloat16), grad_rows[...], preferred_element_type=jnp.float32
            )
            key_sum[seen, :] += jnp.dot(
                grad_scores, query_rows[...], preferred_element_type=jnp.float32
            )
            query_sum[...] += jnp.dot(
                key_turned[:, seen], grad_scores, preferred_element_type=jnp.float32
            )
            return carry

        lax.fori_loop(0, source // 2 + 1, keys_of, 0)
        for head in range(heads):
            lanes = slice(head * tokens, (head + 1) * tokens)
            query_parts[side, there, :, head * HEAD_SIZE : (head + 1) * HEAD_SIZE] = (
                (query_sum[:, lanes] * scale).T.astype(jnp.bfloat16)
            )

    def take(origin):
        for half in range(halves):
            line_copy(0, origin, half).wait_recv()

            @pl.when((origin < plane) & (plane < last))
            def _():
                line_copy(0, origin, half).start()

            @pl.when((origin > plane) & (plane > 0))
            def _():
                line_copy(1, origin, half).start()

            side_copy(origin, half).start()

    def take_side(origin):
        for half in range(halves):
            side_copy(origin, half).wait_recv()

    attend(0, plane)
    own_query = pltpu.make_async_copy(
        query_parts.at[0, plane], grad_query.at[:, columns_at(place)], own_sem.at[0]
    )
    own_query.start()
    before = plane
    for number in range(1, lines):
        there = nth_plane(number)
        take(there)
        take_side(before)
        attend(1, before)
        query_copy(1, before).start()
        attend(0, there)
        query_copy(0, there).start()
        before = there
    take_side(before)
    attend(1, before)
    query_copy(1, before).start()

    def keep(kept, slot, side, there):
        start = pl.multiple_of(device_of(side, there) * tokens, tokens)
        rows = pl.ds(start, tokens)
        kept[side, slot, :, :HEAD_SIZE] = (key_sum[rows, :] * scale).astype(jnp.bfloat16)
        kept[side, slot, :, HEAD_SIZE:] = value_sum[rows, :].astype(jnp.bfloat16)

    for side, there in others:
        keep(kv_out, there, side, there)
        kv_copy(side, there).start()
    keep(kv_in, plane, 0, plane)
    for side, there in others:
        kv_landing(side, there).wait_recv()
    for there in range(lines):
        head = slice(there * HEAD_SIZE, (there + 1) * HEAD_SIZE)
        total = sum(kv_in[side, there].astype(jnp.float32) for side in range(cols))
        grad_key[:, head] = total[:, :HEAD_SIZE].astype(jnp.bfloat16)
        grad_value[:, head] = total[:, HEAD_SIZE:].astype(jnp.bfloat16)
    own_query.wait()
    for side, there in others:
        query_landing(side, there).wait_recv()
        query_copy(side, there).wait_send()
        kv_copy(side, there).wait_send()
    for origin in range(lines):
        for half in range(halves):
            side_copy(origin, half).wait_send()

            @pl.when((origin <= plane) & (plane < last))
            def _():
                line_copy(0, origin, half).wait_send()

            @pl.when((origin >= plane) & (plane > 0))
            def _():
                line_copy(1, origin, half).wait_send()


def attention_grads(
    grad_resid, w_out, head_query, head_output, head_key, head_value, lse, lines, cols
):
    tokens, width = grad_resid.shape
    sequence, head_width = head_query.shape
    heads = head_width // HEAD_SIZE
    peers = lines * cols
    halves = 2
    low, full = jnp.bfloat16, jnp.float32
    dma = pltpu.SemaphoreType.DMA
    vmem = pl.BlockSpec(memory_space=pltpu.VMEM)
    hbm = pl.BlockSpec(memory_space=pl.ANY)
    kv_shape = jax.ShapeDtypeStruct((tokens, KEY_VALUE_HEADS * HEAD_SIZE), low)
    return pl.pallas_call(
        functools.partial(attention_kernel, lines, cols),
        out_shape=(
            jax.ShapeDtypeStruct((tokens, peers * head_width), low),
            kv_shape,
            kv_shape,
        ),
        in_specs=[vmem] * 3 + [hbm] * 4,
        out_specs=[hbm, vmem, vmem],
        scratch_shapes=[
            pltpu.VMEM(head_query.shape, low),
            pltpu.VMEM(head_output.shape, low),
            pltpu.VMEM(head_key.shape, low),
            pltpu.VMEM(head_value.shape, low),
            pltpu.VMEM((cols, lines, halves, tokens, width // halves), low),
            pltpu.VMEM((HEAD_SIZE, sequence), low),
            pltpu.VMEM((heads * tokens, HEAD_SIZE), low),
            pltpu.VMEM((heads * tokens, HEAD_SIZE), low),
            pltpu.VMEM((HEAD_SIZE, heads * tokens), full),
            pltpu.VMEM((cols, lines, tokens, head_width), low),
            pltpu.VMEM((sequence, HEAD_SIZE), full),
            pltpu.VMEM((sequence, HEAD_SIZE), full),
            pltpu.VMEM((cols, lines, tokens, 2 * HEAD_SIZE), low),
            pltpu.VMEM((cols, lines, tokens, 2 * HEAD_SIZE), low),
            dma((2, lines, halves)),
            dma((lines, halves)),
            dma((cols, lines, halves)),
            dma((cols, lines)),
            dma((cols, lines)),
            dma((cols, lines)),
            dma((cols, lines)),
            dma((5,)),
        ],
        compiler_params=pltpu.CompilerParams(
            collective_id=1, has_side_effects=True, vmem_limit_bytes=58 * 2**20
        ),
        cost_estimate=pl.CostEstimate(
            flops=10 * sequence * sequence * head_width,
            bytes_accessed=100 * 2**20,
            transcendentals=0,
        ),
    )(grad_resid, w_out, lse, head_query, head_output, head_key, head_value)


def per_device(
    grad_out,
    hidden,
    norm_gain,
    expert_ids,
    gate_weights,
    w_gate,
    w_up,
    w_down,
    w_out,
    queries,
    keys,
    values,
    attn_out,
    lse,
):
    token_rows, width = hidden.shape
    topk = expert_ids.shape[1]
    groups = lax.axis_size("grp")
    inner_product = lax.axis_size("inner")
    experts_all = w_gate.shape[0] * groups * inner_product
    capacity = max(2, 5 * token_rows * topk // (4 * experts_all))
    cols = groups // 2
    lines = inner_product // cols if cols else 0
    kernel_plan = (
        cols == 2
        and lines == 4
        and inner_product == lines * cols
        and w_gate.shape[0] == 1
        and (2 * capacity) % 16 == 0
        and token_rows == 128
        and width % 1024 == 0
        and w_gate.shape[2] % FF_TILE == 0
        and inner_product == KEY_VALUE_HEADS * cols
    )
    if kernel_plan:
        grad_resid, head_query, head_output, head_key, head_value = moe_input_grads(
            hidden,
            grad_out,
            norm_gain,
            expert_ids,
            gate_weights,
            w_gate,
            w_up,
            w_down,
            queries,
            attn_out,
            keys,
            values,
            lines,
            cols,
            capacity,
        )
        grads = attention_grads(
            grad_resid, w_out, head_query, head_output, head_key, head_value, lse, lines, cols
        )
        return (grad_resid,) + tuple(grads)
    hidden_f = hidden.astype(jnp.float32)
    inverse = lax.rsqrt(jnp.mean(hidden_f * hidden_f, axis=1, keepdims=True) + EPSILON)
    normed = (hidden_f * inverse * norm_gain).astype(jnp.bfloat16)
    upstream = grad_out.astype(jnp.float32)
    flat_count = token_rows * topk
    flat_ids = expert_ids.reshape(-1)
    one_hot = (flat_ids[:, None] == jnp.arange(experts_all, dtype=jnp.int32)[None, :]).astype(
        jnp.int32
    )
    before = jnp.tril(jnp.ones((flat_count, flat_count), jnp.bfloat16), -1)
    ahead = jnp.dot(
        before, one_hot.astype(jnp.bfloat16), preferred_element_type=jnp.float32
    ).astype(jnp.int32)
    slot_rank = jnp.sum(ahead * one_hot, axis=1)
    target = flat_ids * capacity + slot_rank
    owner = (
        jnp.full((experts_all * capacity,), flat_count, jnp.int32)
        .at[target]
        .set(jnp.arange(flat_count, dtype=jnp.int32))
    )
    source_tok = owner // topk
    scaled = (
        (upstream[:, None, :] * gate_weights[:, :, None])
        .reshape(flat_count, width)
        .astype(jnp.bfloat16)
    )
    zero_row = jnp.zeros((1, width), jnp.bfloat16)
    slot_inputs = jnp.concatenate([normed, zero_row], axis=0)[source_tok]
    slot_grads = jnp.concatenate([scaled, zero_row], axis=0)[owner]
    outgoing = jnp.concatenate([slot_inputs, slot_grads], axis=1).reshape(
        experts_all, capacity, 2 * width
    )
    returned = lax.all_to_all(
        expert_grads(
            lax.all_to_all(outgoing, ("grp", "inner"), split_axis=0, concat_axis=0, tiled=True),
            w_gate,
            w_up,
            w_down,
        ),
        ("grp", "inner"),
        split_axis=0,
        concat_axis=0,
        tiled=True,
    )
    expert_rows = returned.reshape(-1, width)[target].astype(jnp.float32)
    grad_normed = jnp.sum(expert_rows.reshape(token_rows, topk, width), axis=1)
    gained = grad_normed * norm_gain
    statistic = jnp.mean(gained * hidden_f, axis=1, keepdims=True)
    grad_resid = (
        upstream + inverse * gained - hidden_f * inverse * inverse * inverse * statistic
    ).astype(jnp.bfloat16)
    head_width = queries.shape[1] // inner_product
    per_head = head_width // HEAD_SIZE
    shared_portion = inner_product // KEY_VALUE_HEADS
    key_value_pairs = jnp.concatenate(
        [
            keys.reshape(token_rows, KEY_VALUE_HEADS, 1, HEAD_SIZE),
            values.reshape(token_rows, KEY_VALUE_HEADS, 1, HEAD_SIZE),
        ],
        axis=2,
    )
    key_value_broadcast = jnp.broadcast_to(
        key_value_pairs[:, :, None], (token_rows, KEY_VALUE_HEADS, shared_portion, 2, HEAD_SIZE)
    ).reshape(token_rows, inner_product * 2 * HEAD_SIZE)
    head_query, head_output, head_kv = (
        lax.all_to_all(queries, "inner", split_axis=1, concat_axis=0, tiled=True),
        lax.all_to_all(attn_out, "inner", split_axis=1, concat_axis=0, tiled=True),
        lax.all_to_all(key_value_broadcast, "inner", split_axis=1, concat_axis=0, tiled=True),
    )
    head_grad = contract_last(
        lax.all_gather(grad_resid, "inner", axis=0, tiled=True), w_out
    ).astype(jnp.bfloat16)
    seq_len = head_query.shape[0]
    head_key = head_kv[:, :HEAD_SIZE]
    head_value = head_kv[:, HEAD_SIZE:]
    lse_rows = lse.T
    scale = float(HEAD_SIZE) ** (-0.5)
    blocks = 1
    while blocks < 8 and seq_len % (2 * blocks) == 0 and (seq_len // (2 * blocks) >= 512):
        blocks = blocks * 2
    block_len = seq_len // blocks
    grad_key_acc = jnp.zeros((seq_len, HEAD_SIZE), jnp.float32)
    grad_value_acc = jnp.zeros((seq_len, HEAD_SIZE), jnp.float32)
    query_parts = []
    for block_index in range(blocks):
        low = block_index * block_len
        high = low + block_len
        block_query = head_query[low:high].reshape(block_len * per_head, HEAD_SIZE)
        block_output = head_output[low:high].reshape(block_len * per_head, HEAD_SIZE)
        block_grad = head_grad[low:high].reshape(block_len * per_head, HEAD_SIZE)
        block_lse = lse_rows[low:high].reshape(-1)
        seen_key = head_key[:high]
        seen_value = head_value[:high]
        scores = contract_last(block_query, seen_key) * scale
        row_position = low + jnp.arange(block_len * per_head, dtype=jnp.int32) // per_head
        visible = jnp.arange(high, dtype=jnp.int32)[None, :] <= row_position[:, None]
        probs = jnp.where(visible, jnp.exp(scores - block_lse[:, None]), 0.0)
        grad_probs = contract_last(block_grad, seen_value)
        delta = jnp.sum(
            block_grad.astype(jnp.float32) * block_output.astype(jnp.float32), axis=1, keepdims=True
        )
        grad_scores = (probs * (grad_probs - delta)).astype(jnp.bfloat16)
        query_part = jnp.dot(grad_scores, seen_key, preferred_element_type=jnp.float32) * scale
        query_parts.append(query_part.reshape(block_len, head_width))
        grad_key_acc = grad_key_acc.at[:high].add(contract_first(grad_scores, block_query) * scale)
        grad_value_acc = grad_value_acc.at[:high].add(
            contract_first(probs.astype(jnp.bfloat16), block_grad)
        )
    grad_query_heads = jnp.concatenate(query_parts, axis=0)
    kv_heads = jnp.concatenate([grad_key_acc, grad_value_acc], axis=1)
    token_query, token_key_value = (
        lax.all_to_all(
            grad_query_heads.astype(jnp.bfloat16), "inner", split_axis=0, concat_axis=1, tiled=True
        ).astype(grad_query_heads.dtype),
        lax.all_to_all(
            kv_heads.astype(jnp.bfloat16), "inner", split_axis=0, concat_axis=1, tiled=True
        ).astype(kv_heads.dtype),
    )
    summed_total = jnp.sum(
        token_key_value.reshape(token_rows, KEY_VALUE_HEADS, shared_portion, 2, HEAD_SIZE), axis=2
    )
    keys_gradient = (
        summed_total[:, :, 0].reshape(token_rows, KEY_VALUE_HEADS * HEAD_SIZE).astype(jnp.bfloat16)
    )
    values_gradient = (
        summed_total[:, :, 1].reshape(token_rows, KEY_VALUE_HEADS * HEAD_SIZE).astype(jnp.bfloat16)
    )
    return (grad_resid, token_query.astype(jnp.bfloat16), keys_gradient, values_gradient)


def solution(mesh):
    placed = (
        P(("grp", "inner"), None),
        P(("grp", "inner"), None),
        P(),
        P(("grp", "inner"), None),
        P(("grp", "inner"), None),
        P(("grp", "inner"), None, None),
        P(("grp", "inner"), None, None),
        P(("grp", "inner"), None, None),
        P("inner", None),
        P(("grp", "inner"), None),
        P(("grp", "inner"), None),
        P(("grp", "inner"), None),
        P(("grp", "inner"), None),
        P("inner", "grp"),
    )
    return jax.shard_map(
        per_device,
        mesh=mesh,
        in_specs=placed,
        out_specs=(
            P(("grp", "inner"), None),
            P(("grp", "inner"), None),
            P(("grp", "inner"), None),
            P(("grp", "inner"), None),
        ),
        check_vma=False,
    )
```

```python
import functools

import jax
import jax.numpy as jnp
from jax import lax
from jax.experimental import pallas as pl
from jax.experimental.pallas import tpu as pltpu
from jax.sharding import PartitionSpec as P

KEY_VALUE_HEADS = 4
HEAD_SIZE = 128


EPSILON = 1e-06


def contract_last(left, right):
    return lax.dot_general(
        left, right, (((1,), (1,)), ((), ())), preferred_element_type=jnp.float32
    )


def contract_first(left, right):
    return lax.dot_general(
        left, right, (((0,), (0,)), ((), ())), preferred_element_type=jnp.float32
    )


def expert_grads(received, w_gate, w_up, w_down):
    local = w_gate.shape[0]
    width = w_gate.shape[1]
    shaped = received.reshape((-1, local) + received.shape[1:])
    inputs = shaped[..., :width]
    upstream = shaped[..., width:]
    gate_pre = jnp.einsum("nlcd,ldf->nlcf", inputs, w_gate, preferred_element_type=jnp.float32)
    up_pre = jnp.einsum("nlcd,ldf->nlcf", inputs, w_up, preferred_element_type=jnp.float32)
    back_hidden = jnp.einsum("nlcd,lfd->nlcf", upstream, w_down, preferred_element_type=jnp.float32)
    sigmoid = jax.nn.sigmoid(gate_pre)
    grad_gate = (back_hidden * up_pre * sigmoid * (1.0 + gate_pre * (1.0 - sigmoid))).astype(
        jnp.bfloat16
    )
    grad_up = (back_hidden * gate_pre * sigmoid).astype(jnp.bfloat16)
    grad_in = jnp.einsum("nlcf,ldf->nlcd", grad_gate, w_gate, preferred_element_type=jnp.float32)
    grad_in = grad_in + jnp.einsum(
        "nlcf,ldf->nlcd", grad_up, w_up, preferred_element_type=jnp.float32
    )
    return grad_in.astype(jnp.bfloat16).reshape(received.shape[:-1] + (width,))


MESH_ID = pl.DeviceIdType.MESH
FEATURE_CHUNKS = 4
FF_TILE = 256
TILE_ROWS = 16


def moe_kernel(
    lines,
    cols,
    capacity,
    hidden_ref,
    grad_ref,
    gain_ref,
    ids_ref,
    gates_ref,
    gate_hbm,
    up_hbm,
    down_hbm,
    query_hbm,
    output_hbm,
    key_hbm,
    value_hbm,
    out_ref,
    head_query,
    head_output,
    head_key,
    head_value,
    block,
    meta,
    pick,
    pick_back,
    weight,
    outgoing,
    received,
    w_gate,
    w_up,
    w_down,
    hidden_gate,
    hidden_up,
    slope_gate,
    slope_up,
    returned,
    partial,
    arrived,
    own_sum,
    weight_sem,
    line_send,
    line_recv,
    meta_send,
    meta_recv,
    out_send,
    out_recv,
    back_send,
    back_recv,
    sum_send,
    sum_recv,
    head_send,
    head_recv,
    head_own,
):
    group = lax.axis_index("grp")
    place = lax.axis_index("inner")
    plane, col = place // cols, place % cols
    groups = 2 * cols
    members = groups * cols
    me = group * cols + col
    tokens, width = hidden_ref.shape
    chunk = 2 * width // FEATURE_CHUNKS
    halves = FEATURE_CHUNKS // 2
    pair_rows = 2 * capacity
    peers = lines * cols
    tiles = w_gate.shape[0]

    def member(number):
        return (number // cols, plane * cols + number % cols)

    def ahead(step):
        return member(lax.rem(me + step, members))

    def behind(step):
        return member(lax.rem(me + members - step, members))

    last = lines - 1

    def plane_of(slot):
        low = jnp.where(plane < 2, plane, last - plane)
        there = (low, 2, 1 - low, 3)[slot]
        return jnp.where(plane < 2, there, last - there)

    def slot_of(there, origin):
        seen = jnp.where(there < 2, origin, last - origin)
        slot = jnp.where(seen == 3, 3, jnp.where(seen == 2, 1, 2))
        return jnp.where(there == origin, 0, slot)

    def remote(source, target, send, recv, device):
        return pltpu.make_async_remote_copy(
            src_ref=source,
            dst_ref=target,
            send_sem=send,
            recv_sem=recv,
            device_id=device,
            device_id_type=MESH_ID,
        )

    def block_at(slot, part):
        rows = pl.ds(pl.multiple_of((slot % 2) * tokens, tokens), tokens)
        return block.at[slot // 2, part, rows]

    def line_copy(way, origin, part):
        there = jnp.clip(plane + (1 - 2 * way), 0, last)
        return remote(
            block_at(slot_of(plane, origin), part),
            block_at(slot_of(there, origin), part),
            line_send.at[way, origin, part],
            line_recv.at[origin, part],
            (group, there * cols + col),
        )

    def meta_copy(way, origin):
        there = jnp.clip(plane + (1 - 2 * way), 0, last)
        return remote(
            meta.at[slot_of(plane, origin)],
            meta.at[slot_of(there, origin)],
            meta_send.at[way, origin],
            meta_recv.at[origin],
            (group, there * cols + col),
        )

    def send_on(origin, part, up, down):
        for way, sending in enumerate((up, down)):

            @pl.when(sending)
            def _():
                if part == 0:
                    meta_copy(way, origin).start()
                line_copy(way, origin, part).start()

    def send_own(part):
        send_on(plane, part, plane < last, plane > 0)

    def take(slot, part):
        origin = plane_of(slot)
        landed = block_at(slot, part)
        device = (group, origin * cols + col)
        if part == 0:
            remote(
                meta.at[slot], meta.at[slot], meta_send.at[0, origin], meta_recv.at[origin], device
            ).wait_recv()
        remote(
            landed, landed, line_send.at[0, origin, part], line_recv.at[origin, part], device
        ).wait_recv()
        send_on(
            origin,
            part,
            (origin < plane) & (plane < last),
            (origin > plane) & (plane > 0),
        )

    def step_rows(step):
        return pl.ds(step * pair_rows, pair_rows)

    def out_copy(phase, part, step):
        return remote(
            outgoing.at[phase, part, step_rows(step)],
            received.at[phase, part, step_rows(step)],
            out_send.at[phase, part, step],
            out_recv.at[phase, part, step],
            ahead(step),
        )

    tile_width = min(chunk, 512)
    pieces = [
        (half, piece) for half in range(halves) for piece in range(chunk // tile_width)
    ]

    def piece_columns(piece):
        return pl.ds(piece * tile_width, tile_width)

    def back_copy(phase, half, piece, step):
        columns = piece_columns(piece)
        return remote(
            outgoing.at[phase, half, step_rows(step), columns],
            returned.at[phase, half, step_rows(step), columns],
            back_send.at[phase, half, piece, step],
            back_recv.at[phase, half, piece, step],
            behind(step),
        )

    def sum_copy(away, half, piece):
        columns = piece_columns(piece)
        return remote(
            partial.at[away - 1, half, :, columns],
            arrived.at[plane, half, :, columns],
            sum_send.at[away - 1, half, piece],
            sum_recv.at[plane, half, piece],
            (group, plane_of(away) * cols + col),
        )

    def sum_landing(away, half, piece):
        columns = piece_columns(piece)
        origin = plane_of(away)
        return remote(
            partial.at[away - 1, half, :, columns],
            arrived.at[origin, half, :, columns],
            sum_send.at[away - 1, half, piece],
            sum_recv.at[origin, half, piece],
            (group, origin * cols + col),
        )

    head_width = head_query.shape[1]
    kv_width = head_key.shape[1]
    share = peers // (key_hbm.shape[1] // kv_width)

    def head_pairs(to, source):
        columns = pl.ds(pl.multiple_of(to * head_width, head_width), head_width)
        kv_columns = pl.ds(pl.multiple_of((to // share) * kv_width, kv_width), kv_width)
        rows = pl.ds(pl.multiple_of(source * tokens, tokens), tokens)
        return (
            (query_hbm.at[:, columns], head_query.at[rows]),
            (output_hbm.at[:, columns], head_output.at[rows]),
            (key_hbm.at[:, kv_columns], head_key.at[rows]),
            (value_hbm.at[:, kv_columns], head_value.at[rows]),
        )

    def head_copies(to, slot, source, target):
        return [
            remote(
                src, dst, head_send.at[number, slot], head_recv.at[number, slot], (group, target)
            )
            for number, (src, dst) in enumerate(head_pairs(to, source))
        ]

    own_heads = [
        pltpu.make_async_copy(src, dst, head_own.at[number])
        for number, (src, dst) in enumerate(head_pairs(place, place))
    ]

    barrier = pltpu.get_barrier_semaphore()
    for step in range(1, peers):
        pl.semaphore_signal(
            barrier, inc=1, device_id=(group, lax.rem(place + step, peers)), device_id_type=MESH_ID
        )
    for step in range(1, members):
        pl.semaphore_signal(barrier, inc=1, device_id=ahead(step), device_id_type=MESH_ID)

    weight_copies = []
    for tile in range(tiles):
        columns = pl.ds(tile * FF_TILE, FF_TILE)
        weight_copies += [
            pltpu.make_async_copy(
                gate_hbm.at[0, :, columns], w_gate.at[tile], weight_sem.at[0, tile]
            ),
            pltpu.make_async_copy(up_hbm.at[0, :, columns], w_up.at[tile], weight_sem.at[1, tile]),
            pltpu.make_async_copy(
                down_hbm.at[0, columns, :], w_down.at[tile], weight_sem.at[2, tile]
            ),
        ]
    for copy in weight_copies:
        copy.start()

    def norm_rows(index, carry):
        rows = pl.ds(pl.multiple_of(index * TILE_ROWS, TILE_ROWS), TILE_ROWS)
        hidden = hidden_ref[rows, :].astype(jnp.float32)
        inverse = lax.rsqrt(jnp.mean(hidden * hidden, axis=1, keepdims=True) + EPSILON)
        normed = (hidden * inverse * gain_ref[...]).astype(jnp.bfloat16)
        upstream = grad_ref[rows, :]
        for half in range(halves):
            columns = slice(half * chunk, (half + 1) * chunk)
            block[0, half, rows, :] = normed[:, columns]
            block[0, halves + half, rows, :] = upstream[:, columns]
        return carry

    lax.fori_loop(0, tokens // TILE_ROWS, norm_rows, 0)

    experts = meta.shape[1] // 2
    topk = ids_ref.shape[0]
    expert = lax.broadcasted_iota(jnp.int32, (experts, tokens), 0)
    mine = jnp.zeros((experts, tokens), jnp.float32)
    gates = jnp.zeros((experts, tokens), jnp.float32)
    for slot in range(topk):
        hit = ids_ref[slot : slot + 1, :] == expert
        mine = mine + jnp.where(hit, 1.0, 0.0)
        gates = gates + jnp.where(hit, gates_ref[slot : slot + 1, :], 0.0)
    earlier = lax.broadcasted_iota(jnp.int32, (tokens, tokens), 0)
    later = lax.broadcasted_iota(jnp.int32, (tokens, tokens), 1)
    before = jnp.where(earlier < later, 1.0, 0.0).astype(jnp.bfloat16)
    rank = jnp.dot(mine.astype(jnp.bfloat16), before, preferred_element_type=jnp.float32)
    meta[0, :experts, :] = jnp.where(mine > 0.5, rank, -1.0)
    meta[0, experts:, :] = gates

    pl.semaphore_wait(barrier, members + peers - 2)
    near_step = 1 + (peers - 2) * col

    def start_heads(step):
        to = lax.rem(place + step, peers)
        for copy in head_copies(to, step, place, to):
            copy.start()

    send_own(0)
    start_heads(near_step)
    send_own(1)

    def build_pick(phase):
        lane = lax.broadcasted_iota(jnp.int32, (1, 2 * tokens), 1)
        shift = jnp.where(lane >= tokens, float(capacity), 0.0)
        row = lax.broadcasted_iota(jnp.int32, (pair_rows, 2 * tokens), 0).astype(jnp.float32)
        for step in range(members):
            number = lax.rem(me + step, members)
            named = (number // cols) * peers + plane * cols + number % cols
            slots = jnp.concatenate(
                [meta[2 * phase + j, pl.ds(named, 1), :] for j in range(2)], axis=1
            )
            goal = jnp.where(slots >= 0.0, slots + shift, -1.0)
            hot = jnp.where(row == goal, 1.0, 0.0)
            rows = slice(step * pair_rows, (step + 1) * pair_rows)
            pick[phase, rows, :] = hot.astype(jnp.bfloat16)

    def build_weight(phase):
        for step in range(members):
            number = lax.rem(me + step, members)
            named = (number // cols) * peers + plane * cols + number % cols
            shares = jnp.concatenate(
                [meta[2 * phase + j, pl.ds(experts + named, 1), :] for j in range(2)], axis=1
            )
            rows = slice(step * pair_rows, (step + 1) * pair_rows)
            hot = pick[phase, rows, :].astype(jnp.float32)
            weight[phase, rows, :] = jnp.broadcast_to(
                jnp.sum(hot * shares, axis=1, keepdims=True), (pair_rows, 128)
            )
        pick_back[phase] = pick[phase].astype(jnp.float32).T.astype(jnp.bfloat16)

    def select(phase, part):
        def columns_of(index, carry):
            columns = pl.ds(pl.multiple_of(index * tile_width, tile_width), tile_width)
            rows = jnp.dot(
                pick[phase], block[phase, part, :, columns], preferred_element_type=jnp.float32
            )
            if part >= halves:
                rows = rows * weight[phase][:, :1]
            rows = rows.astype(jnp.bfloat16)
            outgoing[phase, part, :, columns] = rows
            received[phase, part, :pair_rows, columns] = rows[:pair_rows]
            return carry

        lax.fori_loop(0, chunk // tile_width, columns_of, 0)

    for phase in range(2):
        for part in range(FEATURE_CHUNKS):
            if phase == 0:
                take(1, part)
            elif part == FEATURE_CHUNKS - 1:
                take(3, part)
            if part == 0:
                build_pick(phase)
            select(phase, part)
            for step in range(1, members):
                out_copy(phase, part, step).start()
            if phase == 0:
                if part + 2 < FEATURE_CHUNKS:
                    send_own(part + 2)
                take(2, part)
                if part:
                    take(3, part - 1)
            if part == 0:
                build_weight(phase)

    for step in (peers - near_step,) + tuple(range(2, peers - 1)):
        start_heads(step)
    for copy in own_heads:
        copy.start()

    for copy in weight_copies:
        copy.wait()

    def expert_products(phase):
        def take(part):
            for step in range(1, members):
                out_copy(phase, part, step).wait_recv()

        for half in range(halves):
            take(half)

        def gate_tile(tile, carry):
            def product(weights):
                return sum(
                    jnp.dot(
                        received[phase, half],
                        weights[tile, half * chunk : (half + 1) * chunk, :],
                        preferred_element_type=jnp.float32,
                    )
                    for half in range(halves)
                )

            gate_pre = product(w_gate)
            up_pre = product(w_up)
            sigmoid = jax.nn.sigmoid(gate_pre)
            slope_gate[tile] = up_pre * sigmoid * (1.0 + gate_pre * (1.0 - sigmoid))
            slope_up[tile] = gate_pre * sigmoid
            return carry

        lax.fori_loop(0, tiles, gate_tile, 0)
        for half in range(halves):
            take(halves + half)

        def hidden_tile(tile, carry):
            back_hidden = sum(
                contract_last(
                    received[phase, halves + half],
                    w_down[tile, :, half * chunk : (half + 1) * chunk],
                )
                for half in range(halves)
            )
            hidden_gate[tile] = (back_hidden * slope_gate[tile]).astype(jnp.bfloat16)
            hidden_up[tile] = (back_hidden * slope_up[tile]).astype(jnp.bfloat16)
            return carry

        lax.fori_loop(0, tiles, hidden_tile, 0)
        for half, piece in pieces:
            if piece == 0:
                for step in range(1, members):
                    out_copy(phase, half, step).wait_send()
            columns = piece_columns(piece)
            rows = pl.ds(half * chunk + piece * tile_width, tile_width)

            def add_tile(tile):
                return contract_last(hidden_gate[tile], w_gate[tile, rows, :]) + contract_last(
                    hidden_up[tile], w_up[tile, rows, :]
                )

            total = sum(add_tile(tile) for tile in range(tiles)).astype(jnp.bfloat16)
            outgoing[phase, half, :, columns] = total
            returned[phase, half, :pair_rows, columns] = total[:pair_rows]
            for step in range(1, members):
                back_copy(phase, half, piece, step).start()

    def combine(phase):
        for half, piece in pieces:
            for step in range(1, members):
                back_copy(phase, half, piece, step).wait_recv()
            columns = piece_columns(piece)
            total = jnp.dot(
                pick_back[phase],
                returned[phase, half, :, columns],
                preferred_element_type=jnp.float32,
            )
            for j in range(2):
                rows = total[j * tokens : (j + 1) * tokens]
                away = 2 * phase + j
                if away:
                    partial[away - 1, half, :, columns] = rows.astype(jnp.bfloat16)
                    sum_copy(away, half, piece).start()
                else:
                    own_sum[half, :, columns] = rows

    for phase in range(2):
        expert_products(phase)
    for phase in range(2):
        combine(phase)

    for away in range(1, lines):
        for half, piece in pieces:
            sum_landing(away, half, piece).wait_recv()

    def finish(index, carry):
        rows = pl.ds(pl.multiple_of(index * TILE_ROWS, TILE_ROWS), TILE_ROWS)
        hidden = hidden_ref[rows, :].astype(jnp.float32)
        inverse = lax.rsqrt(jnp.mean(hidden * hidden, axis=1, keepdims=True) + EPSILON)
        grad_normed = []
        for half in range(halves):
            total = own_sum[half, rows, :]
            for away in range(1, lines):
                total = total + arrived[plane_of(away), half, rows, :].astype(jnp.float32)
            grad_normed.append(total)
        gained = jnp.concatenate(grad_normed, axis=1) * gain_ref[...]
        statistic = jnp.mean(gained * hidden, axis=1, keepdims=True)
        out_ref[rows, :] = (
            grad_ref[rows, :].astype(jnp.float32)
            + inverse * gained
            - hidden * (inverse * inverse * inverse * statistic)
        ).astype(jnp.bfloat16)
        return carry

    lax.fori_loop(0, tokens // TILE_ROWS, finish, 0)

    for step in range(1, peers):
        source = lax.rem(place + peers - step, peers)
        for copy in head_copies(place, step, source, source):
            copy.wait_recv()
        for copy in head_copies(lax.rem(place + step, peers), step, place, source):
            copy.wait_send()
    for copy in own_heads:
        copy.wait()
    for origin in range(lines):
        for way, sent in enumerate(
            ((origin <= plane) & (plane < last), (origin >= plane) & (plane > 0))
        ):

            @pl.when(sent)
            def _():
                meta_copy(way, origin).wait_send()
                for part in range(FEATURE_CHUNKS):
                    line_copy(way, origin, part).wait_send()

    for away in range(1, lines):
        for half, piece in pieces:
            sum_copy(away, half, piece).wait_send()
    for phase in range(2):
        for step in range(1, members):
            for part in range(halves, FEATURE_CHUNKS):
                out_copy(phase, part, step).wait_send()
            for half, piece in pieces:
                back_copy(phase, half, piece, step).wait_send()


def moe_input_grads(
    hidden,
    grad_out,
    norm_gain,
    expert_ids,
    gate_weights,
    w_gate,
    w_up,
    w_down,
    queries,
    attn_out,
    keys,
    values,
    lines,
    cols,
    capacity,
):
    tokens, width = hidden.shape
    ff = w_gate.shape[2]
    peers = lines * cols
    experts = 2 * cols * peers
    members = 2 * cols * cols
    chunk = 2 * width // FEATURE_CHUNKS
    halves = FEATURE_CHUNKS // 2
    rows = members * 2 * capacity
    tiles = ff // FF_TILE
    head_width = queries.shape[1] // peers
    low, full = jnp.bfloat16, jnp.float32
    dma = pltpu.SemaphoreType.DMA
    vmem = pl.BlockSpec(memory_space=pltpu.VMEM)
    hbm = pl.BlockSpec(memory_space=pl.ANY)
    sequence = peers * tokens
    return pl.pallas_call(
        functools.partial(moe_kernel, lines, cols, capacity),
        out_shape=(
            jax.ShapeDtypeStruct((tokens, width), low),
            jax.ShapeDtypeStruct((sequence, head_width), low),
            jax.ShapeDtypeStruct((sequence, head_width), low),
            jax.ShapeDtypeStruct((sequence, HEAD_SIZE), low),
            jax.ShapeDtypeStruct((sequence, HEAD_SIZE), low),
        ),
        in_specs=[vmem] * 5 + [hbm] * 7,
        out_specs=[vmem] + [hbm] * 4,
        scratch_shapes=[
            pltpu.VMEM((2, FEATURE_CHUNKS, 2 * tokens, chunk), low),
            pltpu.VMEM((lines, 2 * experts, tokens), full),
            pltpu.VMEM((2, rows, 2 * tokens), low),
            pltpu.VMEM((2, 2 * tokens, rows), low),
            pltpu.VMEM((2, rows, 128), full),
            pltpu.VMEM((2, FEATURE_CHUNKS, rows, chunk), low),
            pltpu.VMEM((2, FEATURE_CHUNKS, rows, chunk), low),
            pltpu.VMEM((tiles, width, FF_TILE), low),
            pltpu.VMEM((tiles, width, FF_TILE), low),
            pltpu.VMEM((tiles, FF_TILE, width), low),
            pltpu.VMEM((tiles, rows, FF_TILE), low),
            pltpu.VMEM((tiles, rows, FF_TILE), low),
            pltpu.VMEM((tiles, rows, FF_TILE), full),
            pltpu.VMEM((tiles, rows, FF_TILE), full),
            pltpu.VMEM((2, halves, rows, chunk), low),
            pltpu.VMEM((lines - 1, halves, tokens, chunk), low),
            pltpu.VMEM((lines, halves, tokens, chunk), low),
            pltpu.VMEM((halves, tokens, chunk), full),
            dma((3, tiles)),
            dma((2, lines, FEATURE_CHUNKS)),
            dma((lines, FEATURE_CHUNKS)),
            dma((2, lines)),
            dma((lines,)),
            dma((2, FEATURE_CHUNKS, members)),
            dma((2, FEATURE_CHUNKS, members)),
            dma((2, halves, chunk // min(chunk, 512), members)),
            dma((2, halves, chunk // min(chunk, 512), members)),
            dma((lines - 1, halves, chunk // min(chunk, 512))),
            dma((lines, halves, chunk // min(chunk, 512))),
            dma((4, peers)),
            dma((4, peers)),
            dma((4,)),
        ],
        compiler_params=pltpu.CompilerParams(
            collective_id=0, has_side_effects=True, vmem_limit_bytes=60 * 2**20
        ),
        cost_estimate=pl.CostEstimate(
            flops=20 * rows * width * ff, bytes_accessed=400 * 2**20, transcendentals=0
        ),
    )(
        hidden,
        grad_out,
        norm_gain.reshape(1, width),
        expert_ids.T,
        gate_weights.T,
        w_gate,
        w_up,
        w_down,
        queries,
        attn_out,
        keys,
        values,
    )


def attention_kernel(
    lines,
    cols,
    resid_ref,
    w_out_ref,
    lse_ref,
    query_hbm,
    output_hbm,
    key_hbm,
    value_hbm,
    grad_query,
    grad_key,
    grad_value,
    query_ref,
    output_ref,
    key_ref,
    value_ref,
    resid_all,
    key_turned,
    query_rows,
    grad_rows,
    query_sum,
    query_parts,
    key_sum,
    value_sum,
    kv_out,
    kv_in,
    line_send,
    side_send,
    resid_recv,
    query_send,
    query_recv,
    kv_send,
    kv_recv,
    own_sem,
):
    group = lax.axis_index("grp")
    place = lax.axis_index("inner")
    plane, col = place // cols, place % cols
    tokens, width = resid_ref.shape
    halves, part_width = resid_all.shape[2], resid_all.shape[4]
    head_width = query_ref.shape[1]
    heads = head_width // HEAD_SIZE
    peers = lines * cols
    scale = float(HEAD_SIZE) ** (-0.5)
    key_block = 2 * tokens
    last = lines - 1

    def device_of(side, there):
        return there * cols + (col if side == 0 else 1 - col)

    def remote(source, target, send, recv, to):
        return pltpu.make_async_remote_copy(
            src_ref=source,
            dst_ref=target,
            send_sem=send,
            recv_sem=recv,
            device_id=(group, to),
            device_id_type=MESH_ID,
        )

    def line_copy(way, origin, half):
        there = jnp.clip(plane + (1 - 2 * way), 0, last)
        return remote(
            resid_all.at[0, origin, half],
            resid_all.at[0, origin, half],
            line_send.at[way, origin, half],
            resid_recv.at[0, origin, half],
            device_of(0, there),
        )

    def side_copy(origin, half):
        return remote(
            resid_all.at[0, origin, half],
            resid_all.at[1, origin, half],
            side_send.at[origin, half],
            resid_recv.at[1, origin, half],
            device_of(1, plane),
        )

    def columns_at(device):
        return pl.ds(pl.multiple_of(device * head_width, head_width), head_width)

    def query_copy(side, there):
        return remote(
            query_parts.at[side, there],
            grad_query.at[:, columns_at(place)],
            query_send.at[side, there],
            query_recv.at[side, plane],
            device_of(side, there),
        )

    def query_landing(side, there):
        source = device_of(side, there)
        return remote(
            query_parts.at[side, there],
            grad_query.at[:, columns_at(source)],
            query_send.at[side, there],
            query_recv.at[side, there],
            source,
        )

    def kv_copy(side, there):
        return remote(
            kv_out.at[side, there],
            kv_in.at[side, plane],
            kv_send.at[side, there],
            kv_recv.at[side, plane],
            device_of(side, there),
        )

    def kv_landing(side, there):
        return remote(
            kv_out.at[side, there],
            kv_in.at[side, there],
            kv_send.at[side, there],
            kv_recv.at[side, there],
            device_of(side, there),
        )

    def nth_plane(number):
        low = jnp.where(plane < 2, plane, last - plane)
        there = 1 - low if number == 1 else number
        return jnp.where(plane < 2, there, last - there)

    others = [(1, plane)]
    for number in range(1, lines):
        others += [(0, nth_plane(number)), (1, nth_plane(number))]

    inputs = [
        pltpu.make_async_copy(source, target, own_sem.at[1 + number])
        for number, (source, target) in enumerate(
            (
                (query_hbm, query_ref),
                (output_hbm, output_ref),
                (key_hbm, key_ref),
                (value_hbm, value_ref),
            )
        )
    ]
    for copy in inputs:
        copy.start()
    barrier = pltpu.get_barrier_semaphore()
    for side, there in others:
        pl.semaphore_signal(
            barrier, inc=1, device_id=(group, device_of(side, there)), device_id_type=MESH_ID
        )
    for half in range(halves):
        resid_all[0, plane, half] = resid_ref[:, half * part_width : (half + 1) * part_width]
    pl.semaphore_wait(barrier, peers - 1)
    for half in range(halves):

        @pl.when(plane < last)
        def _():
            line_copy(0, plane, half).start()

        @pl.when(plane > 0)
        def _():
            line_copy(1, plane, half).start()

        side_copy(plane, half).start()

    key_sum[...] = jnp.zeros_like(key_sum)
    value_sum[...] = jnp.zeros_like(value_sum)
    for copy in inputs:
        copy.wait()
    key_turned[...] = key_ref[...].astype(jnp.float32).T.astype(jnp.bfloat16)

    def attend(side, there):
        source = device_of(side, there)
        start = pl.multiple_of(source * tokens, tokens)
        rows = pl.ds(start, tokens)
        grad = sum(
            contract_last(
                resid_all[side, there, half],
                w_out_ref[:, half * part_width : (half + 1) * part_width],
            )
            for half in range(halves)
        ).astype(jnp.bfloat16)
        deltas, lses = [], []
        for head in range(heads):
            columns = slice(head * HEAD_SIZE, (head + 1) * HEAD_SIZE)
            lanes = slice(head * tokens, (head + 1) * tokens)
            query_rows[lanes, :] = query_ref[rows, columns]
            grad_rows[lanes, :] = grad[:, columns]
            product = grad[:, columns].astype(jnp.float32) * output_ref[rows, columns].astype(
                jnp.float32
            )
            deltas.append(jnp.sum(product.T, axis=0, keepdims=True))
            lses.append(lse_ref[head : head + 1, rows])
        delta = jnp.concatenate(deltas, axis=1)
        lse = jnp.concatenate(lses, axis=1)
        lane = lax.broadcasted_iota(jnp.int32, (1, heads * tokens), 1)
        token = start + lane % tokens
        query_sum[...] = jnp.zeros_like(query_sum)

        def keys_of(index, carry):
            first = pl.multiple_of(index * key_block, key_block)
            seen = pl.ds(first, key_block)
            scores = contract_last(key_ref[seen, :], query_rows[...]) * scale
            position = first + lax.broadcasted_iota(jnp.int32, (key_block, 1), 0)
            probs = jnp.where(position <= token, jnp.exp(scores - lse), 0.0)
            grad_probs = contract_last(value_ref[seen, :], grad_rows[...])
            grad_scores = (probs * (grad_probs - delta)).astype(jnp.bfloat16)
            value_sum[seen, :] += jnp.dot(
                probs.astype(jnp.bfloat16), grad_rows[...], preferred_element_type=jnp.float32
            )
            key_sum[seen, :] += jnp.dot(
                grad_scores, query_rows[...], preferred_element_type=jnp.float32
            )
            query_sum[...] += jnp.dot(
                key_turned[:, seen], grad_scores, preferred_element_type=jnp.float32
            )
            return carry

        lax.fori_loop(0, source // 2 + 1, keys_of, 0)
        for head in range(heads):
            lanes = slice(head * tokens, (head + 1) * tokens)
            query_parts[side, there, :, head * HEAD_SIZE : (head + 1) * HEAD_SIZE] = (
                (query_sum[:, lanes] * scale).T.astype(jnp.bfloat16)
            )

    def take(origin):
        for half in range(halves):
            line_copy(0, origin, half).wait_recv()

            @pl.when((origin < plane) & (plane < last))
            def _():
                line_copy(0, origin, half).start()

            @pl.when((origin > plane) & (plane > 0))
            def _():
                line_copy(1, origin, half).start()

            side_copy(origin, half).start()

    def take_side(origin):
        for half in range(halves):
            side_copy(origin, half).wait_recv()

    attend(0, plane)
    own_query = pltpu.make_async_copy(
        query_parts.at[0, plane], grad_query.at[:, columns_at(place)], own_sem.at[0]
    )
    own_query.start()
    before = plane
    for number in range(1, lines):
        there = nth_plane(number)
        take(there)
        take_side(before)
        attend(1, before)
        query_copy(1, before).start()
        attend(0, there)
        query_copy(0, there).start()
        before = there
    take_side(before)
    attend(1, before)
    query_copy(1, before).start()

    def keep(kept, slot, side, there):
        start = pl.multiple_of(device_of(side, there) * tokens, tokens)
        rows = pl.ds(start, tokens)
        kept[side, slot, :, :HEAD_SIZE] = (key_sum[rows, :] * scale).astype(jnp.bfloat16)
        kept[side, slot, :, HEAD_SIZE:] = value_sum[rows, :].astype(jnp.bfloat16)

    for side, there in others:
        keep(kv_out, there, side, there)
        kv_copy(side, there).start()
    keep(kv_in, plane, 0, plane)
    for side, there in others:
        kv_landing(side, there).wait_recv()
    for there in range(lines):
        head = slice(there * HEAD_SIZE, (there + 1) * HEAD_SIZE)
        total = sum(kv_in[side, there].astype(jnp.float32) for side in range(cols))
        grad_key[:, head] = total[:, :HEAD_SIZE].astype(jnp.bfloat16)
        grad_value[:, head] = total[:, HEAD_SIZE:].astype(jnp.bfloat16)
    own_query.wait()
    for side, there in others:
        query_landing(side, there).wait_recv()
        query_copy(side, there).wait_send()
        kv_copy(side, there).wait_send()
    for origin in range(lines):
        for half in range(halves):
            side_copy(origin, half).wait_send()

            @pl.when((origin <= plane) & (plane < last))
            def _():
                line_copy(0, origin, half).wait_send()

            @pl.when((origin >= plane) & (plane > 0))
            def _():
                line_copy(1, origin, half).wait_send()


def attention_grads(
    grad_resid, w_out, head_query, head_output, head_key, head_value, lse, lines, cols
):
    tokens, width = grad_resid.shape
    sequence, head_width = head_query.shape
    heads = head_width // HEAD_SIZE
    peers = lines * cols
    halves = 2
    low, full = jnp.bfloat16, jnp.float32
    dma = pltpu.SemaphoreType.DMA
    vmem = pl.BlockSpec(memory_space=pltpu.VMEM)
    hbm = pl.BlockSpec(memory_space=pl.ANY)
    kv_shape = jax.ShapeDtypeStruct((tokens, KEY_VALUE_HEADS * HEAD_SIZE), low)
    return pl.pallas_call(
        functools.partial(attention_kernel, lines, cols),
        out_shape=(
            jax.ShapeDtypeStruct((tokens, peers * head_width), low),
            kv_shape,
            kv_shape,
        ),
        in_specs=[vmem] * 3 + [hbm] * 4,
        out_specs=[hbm, vmem, vmem],
        scratch_shapes=[
            pltpu.VMEM(head_query.shape, low),
            pltpu.VMEM(head_output.shape, low),
            pltpu.VMEM(head_key.shape, low),
            pltpu.VMEM(head_value.shape, low),
            pltpu.VMEM((cols, lines, halves, tokens, width // halves), low),
            pltpu.VMEM((HEAD_SIZE, sequence), low),
            pltpu.VMEM((heads * tokens, HEAD_SIZE), low),
            pltpu.VMEM((heads * tokens, HEAD_SIZE), low),
            pltpu.VMEM((HEAD_SIZE, heads * tokens), full),
            pltpu.VMEM((cols, lines, tokens, head_width), low),
            pltpu.VMEM((sequence, HEAD_SIZE), full),
            pltpu.VMEM((sequence, HEAD_SIZE), full),
            pltpu.VMEM((cols, lines, tokens, 2 * HEAD_SIZE), low),
            pltpu.VMEM((cols, lines, tokens, 2 * HEAD_SIZE), low),
            dma((2, lines, halves)),
            dma((lines, halves)),
            dma((cols, lines, halves)),
            dma((cols, lines)),
            dma((cols, lines)),
            dma((cols, lines)),
            dma((cols, lines)),
            dma((5,)),
        ],
        compiler_params=pltpu.CompilerParams(
            collective_id=1, has_side_effects=True, vmem_limit_bytes=58 * 2**20
        ),
        cost_estimate=pl.CostEstimate(
            flops=10 * sequence * sequence * head_width,
            bytes_accessed=100 * 2**20,
            transcendentals=0,
        ),
    )(grad_resid, w_out, lse, head_query, head_output, head_key, head_value)


def per_device(
    grad_out,
    hidden,
    norm_gain,
    expert_ids,
    gate_weights,
    w_gate,
    w_up,
    w_down,
    w_out,
    queries,
    keys,
    values,
    attn_out,
    lse,
):
    token_rows, width = hidden.shape
    topk = expert_ids.shape[1]
    groups = lax.axis_size("grp")
    inner_product = lax.axis_size("inner")
    experts_all = w_gate.shape[0] * groups * inner_product
    capacity = max(2, 5 * token_rows * topk // (4 * experts_all))
    cols = groups // 2
    lines = inner_product // cols if cols else 0
    kernel_plan = (
        cols == 2
        and lines == 4
        and inner_product == lines * cols
        and w_gate.shape[0] == 1
        and (2 * capacity) % 16 == 0
        and token_rows == 128
        and width % 1024 == 0
        and w_gate.shape[2] % FF_TILE == 0
        and inner_product == KEY_VALUE_HEADS * cols
    )
    if kernel_plan:
        grad_resid, head_query, head_output, head_key, head_value = moe_input_grads(
            hidden,
            grad_out,
            norm_gain,
            expert_ids,
            gate_weights,
            w_gate,
            w_up,
            w_down,
            queries,
            attn_out,
            keys,
            values,
            lines,
            cols,
            capacity,
        )
        grads = attention_grads(
            grad_resid, w_out, head_query, head_output, head_key, head_value, lse, lines, cols
        )
        return (grad_resid,) + tuple(grads)
    hidden_f = hidden.astype(jnp.float32)
    inverse = lax.rsqrt(jnp.mean(hidden_f * hidden_f, axis=1, keepdims=True) + EPSILON)
    normed = (hidden_f * inverse * norm_gain).astype(jnp.bfloat16)
    upstream = grad_out.astype(jnp.float32)
    flat_count = token_rows * topk
    flat_ids = expert_ids.reshape(-1)
    one_hot = (flat_ids[:, None] == jnp.arange(experts_all, dtype=jnp.int32)[None, :]).astype(
        jnp.int32
    )
    before = jnp.tril(jnp.ones((flat_count, flat_count), jnp.bfloat16), -1)
    ahead = jnp.dot(
        before, one_hot.astype(jnp.bfloat16), preferred_element_type=jnp.float32
    ).astype(jnp.int32)
    slot_rank = jnp.sum(ahead * one_hot, axis=1)
    target = flat_ids * capacity + slot_rank
    owner = (
        jnp.full((experts_all * capacity,), flat_count, jnp.int32)
        .at[target]
        .set(jnp.arange(flat_count, dtype=jnp.int32))
    )
    source_tok = owner // topk
    scaled = (
        (upstream[:, None, :] * gate_weights[:, :, None])
        .reshape(flat_count, width)
        .astype(jnp.bfloat16)
    )
    zero_row = jnp.zeros((1, width), jnp.bfloat16)
    slot_inputs = jnp.concatenate([normed, zero_row], axis=0)[source_tok]
    slot_grads = jnp.concatenate([scaled, zero_row], axis=0)[owner]
    outgoing = jnp.concatenate([slot_inputs, slot_grads], axis=1).reshape(
        experts_all, capacity, 2 * width
    )
    returned = lax.all_to_all(
        expert_grads(
            lax.all_to_all(outgoing, ("grp", "inner"), split_axis=0, concat_axis=0, tiled=True),
            w_gate,
            w_up,
            w_down,
        ),
        ("grp", "inner"),
        split_axis=0,
        concat_axis=0,
        tiled=True,
    )
    expert_rows = returned.reshape(-1, width)[target].astype(jnp.float32)
    grad_normed = jnp.sum(expert_rows.reshape(token_rows, topk, width), axis=1)
    gained = grad_normed * norm_gain
    statistic = jnp.mean(gained * hidden_f, axis=1, keepdims=True)
    grad_resid = (
        upstream + inverse * gained - hidden_f * inverse * inverse * inverse * statistic
    ).astype(jnp.bfloat16)
    head_width = queries.shape[1] // inner_product
    per_head = head_width // HEAD_SIZE
    shared_portion = inner_product // KEY_VALUE_HEADS
    key_value_pairs = jnp.concatenate(
        [
            keys.reshape(token_rows, KEY_VALUE_HEADS, 1, HEAD_SIZE),
            values.reshape(token_rows, KEY_VALUE_HEADS, 1, HEAD_SIZE),
        ],
        axis=2,
    )
    key_value_broadcast = jnp.broadcast_to(
        key_value_pairs[:, :, None], (token_rows, KEY_VALUE_HEADS, shared_portion, 2, HEAD_SIZE)
    ).reshape(token_rows, inner_product * 2 * HEAD_SIZE)
    head_query, head_output, head_kv = (
        lax.all_to_all(queries, "inner", split_axis=1, concat_axis=0, tiled=True),
        lax.all_to_all(attn_out, "inner", split_axis=1, concat_axis=0, tiled=True),
        lax.all_to_all(key_value_broadcast, "inner", split_axis=1, concat_axis=0, tiled=True),
    )
    head_grad = contract_last(
        lax.all_gather(grad_resid, "inner", axis=0, tiled=True), w_out
    ).astype(jnp.bfloat16)
    seq_len = head_query.shape[0]
    head_key = head_kv[:, :HEAD_SIZE]
    head_value = head_kv[:, HEAD_SIZE:]
    lse_rows = lse.T
    scale = float(HEAD_SIZE) ** (-0.5)
    blocks = 1
    while blocks < 8 and seq_len % (2 * blocks) == 0 and (seq_len // (2 * blocks) >= 512):
        blocks = blocks * 2
    block_len = seq_len // blocks
    grad_key_acc = jnp.zeros((seq_len, HEAD_SIZE), jnp.float32)
    grad_value_acc = jnp.zeros((seq_len, HEAD_SIZE), jnp.float32)
    query_parts = []
    for block_index in range(blocks):
        low = block_index * block_len
        high = low + block_len
        block_query = head_query[low:high].reshape(block_len * per_head, HEAD_SIZE)
        block_output = head_output[low:high].reshape(block_len * per_head, HEAD_SIZE)
        block_grad = head_grad[low:high].reshape(block_len * per_head, HEAD_SIZE)
        block_lse = lse_rows[low:high].reshape(-1)
        seen_key = head_key[:high]
        seen_value = head_value[:high]
        scores = contract_last(block_query, seen_key) * scale
        row_position = low + jnp.arange(block_len * per_head, dtype=jnp.int32) // per_head
        visible = jnp.arange(high, dtype=jnp.int32)[None, :] <= row_position[:, None]
        probs = jnp.where(visible, jnp.exp(scores - block_lse[:, None]), 0.0)
        grad_probs = contract_last(block_grad, seen_value)
        delta = jnp.sum(
            block_grad.astype(jnp.float32) * block_output.astype(jnp.float32), axis=1, keepdims=True
        )
        grad_scores = (probs * (grad_probs - delta)).astype(jnp.bfloat16)
        query_part = jnp.dot(grad_scores, seen_key, preferred_element_type=jnp.float32) * scale
        query_parts.append(query_part.reshape(block_len, head_width))
        grad_key_acc = grad_key_acc.at[:high].add(contract_first(grad_scores, block_query) * scale)
        grad_value_acc = grad_value_acc.at[:high].add(
            contract_first(probs.astype(jnp.bfloat16), block_grad)
        )
    grad_query_heads = jnp.concatenate(query_parts, axis=0)
    kv_heads = jnp.concatenate([grad_key_acc, grad_value_acc], axis=1)
    token_query, token_key_value = (
        lax.all_to_all(
            grad_query_heads.astype(jnp.bfloat16), "inner", split_axis=0, concat_axis=1, tiled=True
        ).astype(grad_query_heads.dtype),
        lax.all_to_all(
            kv_heads.astype(jnp.bfloat16), "inner", split_axis=0, concat_axis=1, tiled=True
        ).astype(kv_heads.dtype),
    )
    summed_total = jnp.sum(
        token_key_value.reshape(token_rows, KEY_VALUE_HEADS, shared_portion, 2, HEAD_SIZE), axis=2
    )
    keys_gradient = (
        summed_total[:, :, 0].reshape(token_rows, KEY_VALUE_HEADS * HEAD_SIZE).astype(jnp.bfloat16)
    )
    values_gradient = (
        summed_total[:, :, 1].reshape(token_rows, KEY_VALUE_HEADS * HEAD_SIZE).astype(jnp.bfloat16)
    )
    return (grad_resid, token_query.astype(jnp.bfloat16), keys_gradient, values_gradient)


def solution(mesh):
    placed = (
        P(("grp", "inner"), None),
        P(("grp", "inner"), None),
        P(),
        P(("grp", "inner"), None),
        P(("grp", "inner"), None),
        P(("grp", "inner"), None, None),
        P(("grp", "inner"), None, None),
        P(("grp", "inner"), None, None),
        P("inner", None),
        P(("grp", "inner"), None),
        P(("grp", "inner"), None),
        P(("grp", "inner"), None),
        P(("grp", "inner"), None),
        P("inner", "grp"),
    )
    return jax.shard_map(
        per_device,
        mesh=mesh,
        in_specs=placed,
        out_specs=(
            P(("grp", "inner"), None),
            P(("grp", "inner"), None),
            P(("grp", "inner"), None),
            P(("grp", "inner"), None),
        ),
        check_vma=False,
    )
```

```python
import functools

import jax
import jax.numpy as jnp
from jax import lax
from jax.experimental import pallas as pl
from jax.experimental.pallas import tpu as pltpu
from jax.sharding import PartitionSpec as P

KEY_VALUE_HEADS = 4
HEAD_SIZE = 128


EPSILON = 1e-06


def contract_last(left, right):
    return lax.dot_general(
        left, right, (((1,), (1,)), ((), ())), preferred_element_type=jnp.float32
    )


def contract_first(left, right):
    return lax.dot_general(
        left, right, (((0,), (0,)), ((), ())), preferred_element_type=jnp.float32
    )


def expert_grads(received, w_gate, w_up, w_down):
    local = w_gate.shape[0]
    width = w_gate.shape[1]
    shaped = received.reshape((-1, local) + received.shape[1:])
    inputs = shaped[..., :width]
    upstream = shaped[..., width:]
    gate_pre = jnp.einsum("nlcd,ldf->nlcf", inputs, w_gate, preferred_element_type=jnp.float32)
    up_pre = jnp.einsum("nlcd,ldf->nlcf", inputs, w_up, preferred_element_type=jnp.float32)
    back_hidden = jnp.einsum("nlcd,lfd->nlcf", upstream, w_down, preferred_element_type=jnp.float32)
    sigmoid = jax.nn.sigmoid(gate_pre)
    grad_gate = (back_hidden * up_pre * sigmoid * (1.0 + gate_pre * (1.0 - sigmoid))).astype(
        jnp.bfloat16
    )
    grad_up = (back_hidden * gate_pre * sigmoid).astype(jnp.bfloat16)
    grad_in = jnp.einsum("nlcf,ldf->nlcd", grad_gate, w_gate, preferred_element_type=jnp.float32)
    grad_in = grad_in + jnp.einsum(
        "nlcf,ldf->nlcd", grad_up, w_up, preferred_element_type=jnp.float32
    )
    return grad_in.astype(jnp.bfloat16).reshape(received.shape[:-1] + (width,))


MESH_ID = pl.DeviceIdType.MESH
FEATURE_CHUNKS = 4
FF_TILE = 256
TILE_ROWS = 16


def moe_kernel(
    lines,
    cols,
    capacity,
    hidden_ref,
    grad_ref,
    gain_ref,
    ids_ref,
    gates_ref,
    gate_hbm,
    up_hbm,
    down_hbm,
    query_hbm,
    output_hbm,
    key_hbm,
    value_hbm,
    out_ref,
    head_query,
    head_output,
    head_key,
    head_value,
    block,
    meta,
    pick,
    pick_back,
    weight,
    outgoing,
    received,
    w_gate,
    w_up,
    w_down,
    hidden_gate,
    hidden_up,
    slope_gate,
    slope_up,
    returned,
    partial,
    arrived,
    own_sum,
    weight_sem,
    line_send,
    line_recv,
    meta_send,
    meta_recv,
    out_send,
    out_recv,
    back_send,
    back_recv,
    sum_send,
    sum_recv,
    head_send,
    head_recv,
    head_own,
):
    group = lax.axis_index("grp")
    place = lax.axis_index("inner")
    plane, col = place // cols, place % cols
    groups = 2 * cols
    members = groups * cols
    me = group * cols + col
    tokens, width = hidden_ref.shape
    chunk = 2 * width // FEATURE_CHUNKS
    halves = FEATURE_CHUNKS // 2
    pair_rows = 2 * capacity
    peers = lines * cols
    tiles = w_gate.shape[0]

    def member(number):
        return (number // cols, plane * cols + number % cols)

    def ahead(step):
        return member(lax.rem(me + step, members))

    def behind(step):
        return member(lax.rem(me + members - step, members))

    last = lines - 1

    def plane_of(slot):
        low = jnp.where(plane < 2, plane, last - plane)
        there = (low, 2, 1 - low, 3)[slot]
        return jnp.where(plane < 2, there, last - there)

    def slot_of(there, origin):
        seen = jnp.where(there < 2, origin, last - origin)
        slot = jnp.where(seen == 3, 3, jnp.where(seen == 2, 1, 2))
        return jnp.where(there == origin, 0, slot)

    def remote(source, target, send, recv, device):
        return pltpu.make_async_remote_copy(
            src_ref=source,
            dst_ref=target,
            send_sem=send,
            recv_sem=recv,
            device_id=device,
            device_id_type=MESH_ID,
        )

    def block_at(slot, part):
        rows = pl.ds(pl.multiple_of((slot % 2) * tokens, tokens), tokens)
        return block.at[slot // 2, part, rows]

    def line_copy(way, origin, part):
        there = jnp.clip(plane + (1 - 2 * way), 0, last)
        return remote(
            block_at(slot_of(plane, origin), part),
            block_at(slot_of(there, origin), part),
            line_send.at[way, origin, part],
            line_recv.at[origin, part],
            (group, there * cols + col),
        )

    def meta_copy(way, origin):
        there = jnp.clip(plane + (1 - 2 * way), 0, last)
        return remote(
            meta.at[slot_of(plane, origin)],
            meta.at[slot_of(there, origin)],
            meta_send.at[way, origin],
            meta_recv.at[origin],
            (group, there * cols + col),
        )

    def send_on(origin, part, up, down):
        for way, sending in enumerate((up, down)):

            @pl.when(sending)
            def _():
                if part == 0:
                    meta_copy(way, origin).start()
                line_copy(way, origin, part).start()

    def send_own(part):
        send_on(plane, part, plane < last, plane > 0)

    def take(slot, part):
        origin = plane_of(slot)
        landed = block_at(slot, part)
        device = (group, origin * cols + col)
        if part == 0:
            remote(
                meta.at[slot], meta.at[slot], meta_send.at[0, origin], meta_recv.at[origin], device
            ).wait_recv()
        remote(
            landed, landed, line_send.at[0, origin, part], line_recv.at[origin, part], device
        ).wait_recv()
        send_on(
            origin,
            part,
            (origin < plane) & (plane < last),
            (origin > plane) & (plane > 0),
        )

    def step_rows(step):
        return pl.ds(step * pair_rows, pair_rows)

    def out_copy(phase, part, step):
        return remote(
            outgoing.at[phase, part, step_rows(step)],
            received.at[phase, part, step_rows(step)],
            out_send.at[phase, part, step],
            out_recv.at[phase, part, step],
            ahead(step),
        )

    tile_width = min(chunk, 512)
    pieces = [
        (half, piece) for half in range(halves) for piece in range(chunk // tile_width)
    ]

    def piece_columns(piece):
        return pl.ds(piece * tile_width, tile_width)

    def back_copy(phase, half, piece, step):
        columns = piece_columns(piece)
        return remote(
            outgoing.at[phase, half, step_rows(step), columns],
            returned.at[phase, half, step_rows(step), columns],
            back_send.at[phase, half, piece, step],
            back_recv.at[phase, half, piece, step],
            behind(step),
        )

    def sum_copy(away, half, piece):
        columns = piece_columns(piece)
        return remote(
            partial.at[away - 1, half, :, columns],
            arrived.at[plane, half, :, columns],
            sum_send.at[away - 1, half, piece],
            sum_recv.at[plane, half, piece],
            (group, plane_of(away) * cols + col),
        )

    def sum_landing(away, half, piece):
        columns = piece_columns(piece)
        origin = plane_of(away)
        return remote(
            partial.at[away - 1, half, :, columns],
            arrived.at[origin, half, :, columns],
            sum_send.at[away - 1, half, piece],
            sum_recv.at[origin, half, piece],
            (group, origin * cols + col),
        )

    head_width = head_query.shape[1]
    kv_width = head_key.shape[1]
    share = peers // (key_hbm.shape[1] // kv_width)

    def head_pairs(to, source):
        columns = pl.ds(pl.multiple_of(to * head_width, head_width), head_width)
        kv_columns = pl.ds(pl.multiple_of((to // share) * kv_width, kv_width), kv_width)
        rows = pl.ds(pl.multiple_of(source * tokens, tokens), tokens)
        return (
            (query_hbm.at[:, columns], head_query.at[rows]),
            (output_hbm.at[:, columns], head_output.at[rows]),
            (key_hbm.at[:, kv_columns], head_key.at[rows]),
            (value_hbm.at[:, kv_columns], head_value.at[rows]),
        )

    def head_copies(to, slot, source, target):
        return [
            remote(
                src, dst, head_send.at[number, slot], head_recv.at[number, slot], (group, target)
            )
            for number, (src, dst) in enumerate(head_pairs(to, source))
        ]

    own_heads = [
        pltpu.make_async_copy(src, dst, head_own.at[number])
        for number, (src, dst) in enumerate(head_pairs(place, place))
    ]

    barrier = pltpu.get_barrier_semaphore()
    for step in range(1, peers):
        pl.semaphore_signal(
            barrier, inc=1, device_id=(group, lax.rem(place + step, peers)), device_id_type=MESH_ID
        )
    for step in range(1, members):
        pl.semaphore_signal(barrier, inc=1, device_id=ahead(step), device_id_type=MESH_ID)

    weight_copies = []
    for tile in range(tiles):
        columns = pl.ds(tile * FF_TILE, FF_TILE)
        weight_copies += [
            pltpu.make_async_copy(
                gate_hbm.at[0, :, columns], w_gate.at[tile], weight_sem.at[0, tile]
            ),
            pltpu.make_async_copy(up_hbm.at[0, :, columns], w_up.at[tile], weight_sem.at[1, tile]),
            pltpu.make_async_copy(
                down_hbm.at[0, columns, :], w_down.at[tile], weight_sem.at[2, tile]
            ),
        ]
    for copy in weight_copies:
        copy.start()

    def norm_rows(index, carry):
        rows = pl.ds(pl.multiple_of(index * TILE_ROWS, TILE_ROWS), TILE_ROWS)
        hidden = hidden_ref[rows, :].astype(jnp.float32)
        inverse = lax.rsqrt(jnp.mean(hidden * hidden, axis=1, keepdims=True) + EPSILON)
        normed = (hidden * inverse * gain_ref[...]).astype(jnp.bfloat16)
        upstream = grad_ref[rows, :]
        for half in range(halves):
            columns = slice(half * chunk, (half + 1) * chunk)
            block[0, half, rows, :] = normed[:, columns]
            block[0, halves + half, rows, :] = upstream[:, columns]
        return carry

    lax.fori_loop(0, tokens // TILE_ROWS, norm_rows, 0)

    experts = meta.shape[1] // 2
    topk = ids_ref.shape[0]
    expert = lax.broadcasted_iota(jnp.int32, (experts, tokens), 0)
    mine = jnp.zeros((experts, tokens), jnp.float32)
    gates = jnp.zeros((experts, tokens), jnp.float32)
    for slot in range(topk):
        hit = ids_ref[slot : slot + 1, :] == expert
        mine = mine + jnp.where(hit, 1.0, 0.0)
        gates = gates + jnp.where(hit, gates_ref[slot : slot + 1, :], 0.0)
    earlier = lax.broadcasted_iota(jnp.int32, (tokens, tokens), 0)
    later = lax.broadcasted_iota(jnp.int32, (tokens, tokens), 1)
    before = jnp.where(earlier < later, 1.0, 0.0).astype(jnp.bfloat16)
    rank = jnp.dot(mine.astype(jnp.bfloat16), before, preferred_element_type=jnp.float32)
    meta[0, :experts, :] = jnp.where(mine > 0.5, rank, -1.0)
    meta[0, experts:, :] = gates

    pl.semaphore_wait(barrier, members + peers - 2)
    near_step = 1 + (peers - 2) * col

    def start_heads(step):
        to = lax.rem(place + step, peers)
        for copy in head_copies(to, step, place, to):
            copy.start()

    send_own(0)
    start_heads(near_step)
    send_own(1)

    def build_pick(phase):
        lane = lax.broadcasted_iota(jnp.int32, (1, 2 * tokens), 1)
        shift = jnp.where(lane >= tokens, float(capacity), 0.0)
        row = lax.broadcasted_iota(jnp.int32, (pair_rows, 2 * tokens), 0).astype(jnp.float32)
        for step in range(members):
            number = lax.rem(me + step, members)
            named = (number // cols) * peers + plane * cols + number % cols
            slots = jnp.concatenate(
                [meta[2 * phase + j, pl.ds(named, 1), :] for j in range(2)], axis=1
            )
            goal = jnp.where(slots >= 0.0, slots + shift, -1.0)
            hot = jnp.where(row == goal, 1.0, 0.0)
            rows = slice(step * pair_rows, (step + 1) * pair_rows)
            pick[phase, rows, :] = hot.astype(jnp.bfloat16)

    def build_weight(phase):
        for step in range(members):
            number = lax.rem(me + step, members)
            named = (number // cols) * peers + plane * cols + number % cols
            shares = jnp.concatenate(
                [meta[2 * phase + j, pl.ds(experts + named, 1), :] for j in range(2)], axis=1
            )
            rows = slice(step * pair_rows, (step + 1) * pair_rows)
            hot = pick[phase, rows, :].astype(jnp.float32)
            weight[phase, rows, :] = jnp.broadcast_to(
                jnp.sum(hot * shares, axis=1, keepdims=True), (pair_rows, 128)
            )
        pick_back[phase] = pick[phase].astype(jnp.float32).T.astype(jnp.bfloat16)

    def select(phase, part):
        def columns_of(index, carry):
            columns = pl.ds(pl.multiple_of(index * tile_width, tile_width), tile_width)
            rows = jnp.dot(
                pick[phase], block[phase, part, :, columns], preferred_element_type=jnp.float32
            )
            if part >= halves:
                rows = rows * weight[phase][:, :1]
            rows = rows.astype(jnp.bfloat16)
            outgoing[phase, part, :, columns] = rows
            received[phase, part, :pair_rows, columns] = rows[:pair_rows]
            return carry

        lax.fori_loop(0, chunk // tile_width, columns_of, 0)

    for phase in range(2):
        for part in range(FEATURE_CHUNKS):
            if phase == 0:
                take(1, part)
            elif part == FEATURE_CHUNKS - 1:
                take(3, part)
            if part == 0:
                build_pick(phase)
            select(phase, part)
            for step in range(1, members):
                out_copy(phase, part, step).start()
            if phase == 0:
                if part + 2 < FEATURE_CHUNKS:
                    send_own(part + 2)
                take(2, part)
                if part:
                    take(3, part - 1)
            if part == 0:
                build_weight(phase)

    for step in (peers - near_step,) + tuple(range(2, peers - 1)):
        start_heads(step)
    for copy in own_heads:
        copy.start()

    for copy in weight_copies:
        copy.wait()

    def expert_products(phase):
        def take(part):
            for step in range(1, members):
                out_copy(phase, part, step).wait_recv()

        for half in range(halves):
            take(half)

        def gate_tile(tile, carry):
            def product(weights):
                return sum(
                    jnp.dot(
                        received[phase, half],
                        weights[tile, half * chunk : (half + 1) * chunk, :],
                        preferred_element_type=jnp.float32,
                    )
                    for half in range(halves)
                )

            gate_pre = product(w_gate)
            up_pre = product(w_up)
            sigmoid = jax.nn.sigmoid(gate_pre)
            slope_gate[tile] = up_pre * sigmoid * (1.0 + gate_pre * (1.0 - sigmoid))
            slope_up[tile] = gate_pre * sigmoid
            return carry

        lax.fori_loop(0, tiles, gate_tile, 0)
        for half in range(halves):
            take(halves + half)

        def hidden_tile(tile, carry):
            back_hidden = sum(
                contract_last(
                    received[phase, halves + half],
                    w_down[tile, :, half * chunk : (half + 1) * chunk],
                )
                for half in range(halves)
            )
            hidden_gate[tile] = (back_hidden * slope_gate[tile]).astype(jnp.bfloat16)
            hidden_up[tile] = (back_hidden * slope_up[tile]).astype(jnp.bfloat16)
            return carry

        lax.fori_loop(0, tiles, hidden_tile, 0)
        for half, piece in pieces:
            if piece == 0:
                for step in range(1, members):
                    out_copy(phase, half, step).wait_send()
            columns = piece_columns(piece)
            rows = pl.ds(half * chunk + piece * tile_width, tile_width)

            def add_tile(tile):
                return contract_last(hidden_gate[tile], w_gate[tile, rows, :]) + contract_last(
                    hidden_up[tile], w_up[tile, rows, :]
                )

            total = sum(add_tile(tile) for tile in range(tiles)).astype(jnp.bfloat16)
            outgoing[phase, half, :, columns] = total
            returned[phase, half, :pair_rows, columns] = total[:pair_rows]
            for step in range(1, members):
                back_copy(phase, half, piece, step).start()

    def combine(phase):
        for half, piece in pieces:
            for step in range(1, members):
                back_copy(phase, half, piece, step).wait_recv()
            columns = piece_columns(piece)
            total = jnp.dot(
                pick_back[phase],
                returned[phase, half, :, columns],
                preferred_element_type=jnp.float32,
            )
            for j in range(2):
                rows = total[j * tokens : (j + 1) * tokens]
                away = 2 * phase + j
                if away:
                    partial[away - 1, half, :, columns] = rows.astype(jnp.bfloat16)
                    sum_copy(away, half, piece).start()
                else:
                    own_sum[half, :, columns] = rows

    for phase in range(2):
        expert_products(phase)
    for phase in range(2):
        combine(phase)

    for away in range(1, lines):
        for half, piece in pieces:
            sum_landing(away, half, piece).wait_recv()

    def finish(index, carry):
        rows = pl.ds(pl.multiple_of(index * TILE_ROWS, TILE_ROWS), TILE_ROWS)
        hidden = hidden_ref[rows, :].astype(jnp.float32)
        inverse = lax.rsqrt(jnp.mean(hidden * hidden, axis=1, keepdims=True) + EPSILON)
        grad_normed = []
        for half in range(halves):
            total = own_sum[half, rows, :]
            for away in range(1, lines):
                total = total + arrived[plane_of(away), half, rows, :].astype(jnp.float32)
            grad_normed.append(total)
        gained = jnp.concatenate(grad_normed, axis=1) * gain_ref[...]
        statistic = jnp.mean(gained * hidden, axis=1, keepdims=True)
        out_ref[rows, :] = (
            grad_ref[rows, :].astype(jnp.float32)
            + inverse * gained
            - hidden * (inverse * inverse * inverse * statistic)
        ).astype(jnp.bfloat16)
        return carry

    lax.fori_loop(0, tokens // TILE_ROWS, finish, 0)

    for step in range(1, peers):
        source = lax.rem(place + peers - step, peers)
        for copy in head_copies(place, step, source, source):
            copy.wait_recv()
        for copy in head_copies(lax.rem(place + step, peers), step, place, source):
            copy.wait_send()
    for copy in own_heads:
        copy.wait()
    for origin in range(lines):
        for way, sent in enumerate(
            ((origin <= plane) & (plane < last), (origin >= plane) & (plane > 0))
        ):

            @pl.when(sent)
            def _():
                meta_copy(way, origin).wait_send()
                for part in range(FEATURE_CHUNKS):
                    line_copy(way, origin, part).wait_send()

    for away in range(1, lines):
        for half, piece in pieces:
            sum_copy(away, half, piece).wait_send()
    for phase in range(2):
        for step in range(1, members):
            for part in range(halves, FEATURE_CHUNKS):
                out_copy(phase, part, step).wait_send()
            for half, piece in pieces:
                back_copy(phase, half, piece, step).wait_send()


def moe_input_grads(
    hidden,
    grad_out,
    norm_gain,
    expert_ids,
    gate_weights,
    w_gate,
    w_up,
    w_down,
    queries,
    attn_out,
    keys,
    values,
    lines,
    cols,
    capacity,
):
    tokens, width = hidden.shape
    ff = w_gate.shape[2]
    peers = lines * cols
    experts = 2 * cols * peers
    members = 2 * cols * cols
    chunk = 2 * width // FEATURE_CHUNKS
    halves = FEATURE_CHUNKS // 2
    rows = members * 2 * capacity
    tiles = ff // FF_TILE
    head_width = queries.shape[1] // peers
    low, full = jnp.bfloat16, jnp.float32
    dma = pltpu.SemaphoreType.DMA
    vmem = pl.BlockSpec(memory_space=pltpu.VMEM)
    hbm = pl.BlockSpec(memory_space=pl.ANY)
    sequence = peers * tokens
    return pl.pallas_call(
        functools.partial(moe_kernel, lines, cols, capacity),
        out_shape=(
            jax.ShapeDtypeStruct((tokens, width), low),
            jax.ShapeDtypeStruct((sequence, head_width), low),
            jax.ShapeDtypeStruct((sequence, head_width), low),
            jax.ShapeDtypeStruct((sequence, HEAD_SIZE), low),
            jax.ShapeDtypeStruct((sequence, HEAD_SIZE), low),
        ),
        in_specs=[vmem] * 5 + [hbm] * 7,
        out_specs=[vmem] + [hbm] * 4,
        scratch_shapes=[
            pltpu.VMEM((2, FEATURE_CHUNKS, 2 * tokens, chunk), low),
            pltpu.VMEM((lines, 2 * experts, tokens), full),
            pltpu.VMEM((2, rows, 2 * tokens), low),
            pltpu.VMEM((2, 2 * tokens, rows), low),
            pltpu.VMEM((2, rows, 128), full),
            pltpu.VMEM((2, FEATURE_CHUNKS, rows, chunk), low),
            pltpu.VMEM((2, FEATURE_CHUNKS, rows, chunk), low),
            pltpu.VMEM((tiles, width, FF_TILE), low),
            pltpu.VMEM((tiles, width, FF_TILE), low),
            pltpu.VMEM((tiles, FF_TILE, width), low),
            pltpu.VMEM((tiles, rows, FF_TILE), low),
            pltpu.VMEM((tiles, rows, FF_TILE), low),
            pltpu.VMEM((tiles, rows, FF_TILE), full),
            pltpu.VMEM((tiles, rows, FF_TILE), full),
            pltpu.VMEM((2, halves, rows, chunk), low),
            pltpu.VMEM((lines - 1, halves, tokens, chunk), low),
            pltpu.VMEM((lines, halves, tokens, chunk), low),
            pltpu.VMEM((halves, tokens, chunk), full),
            dma((3, tiles)),
            dma((2, lines, FEATURE_CHUNKS)),
            dma((lines, FEATURE_CHUNKS)),
            dma((2, lines)),
            dma((lines,)),
            dma((2, FEATURE_CHUNKS, members)),
            dma((2, FEATURE_CHUNKS, members)),
            dma((2, halves, chunk // min(chunk, 512), members)),
            dma((2, halves, chunk // min(chunk, 512), members)),
            dma((lines - 1, halves, chunk // min(chunk, 512))),
            dma((lines, halves, chunk // min(chunk, 512))),
            dma((4, peers)),
            dma((4, peers)),
            dma((4,)),
        ],
        compiler_params=pltpu.CompilerParams(
            collective_id=0, has_side_effects=True, vmem_limit_bytes=60 * 2**20
        ),
        cost_estimate=pl.CostEstimate(
            flops=20 * rows * width * ff, bytes_accessed=400 * 2**20, transcendentals=0
        ),
    )(
        hidden,
        grad_out,
        norm_gain.reshape(1, width),
        expert_ids.T,
        gate_weights.T,
        w_gate,
        w_up,
        w_down,
        queries,
        attn_out,
        keys,
        values,
    )


def attention_kernel(
    lines,
    cols,
    resid_ref,
    w_out_ref,
    lse_ref,
    query_hbm,
    output_hbm,
    key_hbm,
    value_hbm,
    grad_query,
    grad_key,
    grad_value,
    query_ref,
    output_ref,
    key_ref,
    value_ref,
    resid_all,
    key_turned,
    query_rows,
    grad_rows,
    query_sum,
    query_parts,
    key_sum,
    value_sum,
    kv_out,
    kv_in,
    line_send,
    side_send,
    resid_recv,
    query_send,
    query_recv,
    kv_send,
    kv_recv,
    own_sem,
):
    group = lax.axis_index("grp")
    place = lax.axis_index("inner")
    plane, col = place // cols, place % cols
    tokens, width = resid_ref.shape
    halves, part_width = resid_all.shape[2], resid_all.shape[4]
    head_width = query_ref.shape[1]
    heads = head_width // HEAD_SIZE
    peers = lines * cols
    scale = float(HEAD_SIZE) ** (-0.5)
    key_block = 2 * tokens
    last = lines - 1

    def device_of(side, there):
        return there * cols + (col if side == 0 else 1 - col)

    def remote(source, target, send, recv, to):
        return pltpu.make_async_remote_copy(
            src_ref=source,
            dst_ref=target,
            send_sem=send,
            recv_sem=recv,
            device_id=(group, to),
            device_id_type=MESH_ID,
        )

    def line_copy(way, origin, half):
        there = jnp.clip(plane + (1 - 2 * way), 0, last)
        return remote(
            resid_all.at[0, origin, half],
            resid_all.at[0, origin, half],
            line_send.at[way, origin, half],
            resid_recv.at[0, origin, half],
            device_of(0, there),
        )

    def side_copy(origin, half):
        return remote(
            resid_all.at[0, origin, half],
            resid_all.at[1, origin, half],
            side_send.at[origin, half],
            resid_recv.at[1, origin, half],
            device_of(1, plane),
        )

    def columns_at(device):
        return pl.ds(pl.multiple_of(device * head_width, head_width), head_width)

    def query_copy(side, there):
        return remote(
            query_parts.at[side, there],
            grad_query.at[:, columns_at(place)],
            query_send.at[side, there],
            query_recv.at[side, plane],
            device_of(side, there),
        )

    def query_landing(side, there):
        source = device_of(side, there)
        return remote(
            query_parts.at[side, there],
            grad_query.at[:, columns_at(source)],
            query_send.at[side, there],
            query_recv.at[side, there],
            source,
        )

    def kv_copy(side, there):
        return remote(
            kv_out.at[side, there],
            kv_in.at[side, plane],
            kv_send.at[side, there],
            kv_recv.at[side, plane],
            device_of(side, there),
        )

    def kv_landing(side, there):
        return remote(
            kv_out.at[side, there],
            kv_in.at[side, there],
            kv_send.at[side, there],
            kv_recv.at[side, there],
            device_of(side, there),
        )

    def nth_plane(number):
        low = jnp.where(plane < 2, plane, last - plane)
        there = 1 - low if number == 1 else number
        return jnp.where(plane < 2, there, last - there)

    others = [(1, plane)]
    for number in range(1, lines):
        others += [(0, nth_plane(number)), (1, nth_plane(number))]

    inputs = [
        pltpu.make_async_copy(source, target, own_sem.at[1 + number])
        for number, (source, target) in enumerate(
            (
                (query_hbm, query_ref),
                (output_hbm, output_ref),
                (key_hbm, key_ref),
                (value_hbm, value_ref),
            )
        )
    ]
    for copy in inputs:
        copy.start()
    barrier = pltpu.get_barrier_semaphore()
    for side, there in others:
        pl.semaphore_signal(
            barrier, inc=1, device_id=(group, device_of(side, there)), device_id_type=MESH_ID
        )
    for half in range(halves):
        resid_all[0, plane, half] = resid_ref[:, half * part_width : (half + 1) * part_width]
    pl.semaphore_wait(barrier, peers - 1)
    for half in range(halves):

        @pl.when(plane < last)
        def _():
            line_copy(0, plane, half).start()

        @pl.when(plane > 0)
        def _():
            line_copy(1, plane, half).start()

        side_copy(plane, half).start()

    key_sum[...] = jnp.zeros_like(key_sum)
    value_sum[...] = jnp.zeros_like(value_sum)
    for copy in inputs:
        copy.wait()
    key_turned[...] = key_ref[...].astype(jnp.float32).T.astype(jnp.bfloat16)

    def attend(side, there):
        source = device_of(side, there)
        start = pl.multiple_of(source * tokens, tokens)
        rows = pl.ds(start, tokens)
        grad = sum(
            contract_last(
                resid_all[side, there, half],
                w_out_ref[:, half * part_width : (half + 1) * part_width],
            )
            for half in range(halves)
        ).astype(jnp.bfloat16)
        deltas, lses = [], []
        for head in range(heads):
            columns = slice(head * HEAD_SIZE, (head + 1) * HEAD_SIZE)
            lanes = slice(head * tokens, (head + 1) * tokens)
            query_rows[lanes, :] = query_ref[rows, columns]
            grad_rows[lanes, :] = grad[:, columns]
            product = grad[:, columns].astype(jnp.float32) * output_ref[rows, columns].astype(
                jnp.float32
            )
            deltas.append(jnp.sum(product.T, axis=0, keepdims=True))
            lses.append(lse_ref[head : head + 1, rows])
        delta = jnp.concatenate(deltas, axis=1)
        lse = jnp.concatenate(lses, axis=1)
        lane = lax.broadcasted_iota(jnp.int32, (1, heads * tokens), 1)
        token = start + lane % tokens
        query_sum[...] = jnp.zeros_like(query_sum)

        def keys_of(index, carry):
            first = pl.multiple_of(index * key_block, key_block)
            seen = pl.ds(first, key_block)
            scores = contract_last(key_ref[seen, :], query_rows[...]) * scale
            position = first + lax.broadcasted_iota(jnp.int32, (key_block, 1), 0)
            probs = jnp.where(position <= token, jnp.exp(scores - lse), 0.0)
            grad_probs = contract_last(value_ref[seen, :], grad_rows[...])
            grad_scores = (probs * (grad_probs - delta)).astype(jnp.bfloat16)
            value_sum[seen, :] += jnp.dot(
                probs.astype(jnp.bfloat16), grad_rows[...], preferred_element_type=jnp.float32
            )
            key_sum[seen, :] += jnp.dot(
                grad_scores, query_rows[...], preferred_element_type=jnp.float32
            )
            query_sum[...] += jnp.dot(
                key_turned[:, seen], grad_scores, preferred_element_type=jnp.float32
            )
            return carry

        lax.fori_loop(0, source // 2 + 1, keys_of, 0)
        for head in range(heads):
            lanes = slice(head * tokens, (head + 1) * tokens)
            query_parts[side, there, :, head * HEAD_SIZE : (head + 1) * HEAD_SIZE] = (
                (query_sum[:, lanes] * scale).T.astype(jnp.bfloat16)
            )

    def take(origin):
        for half in range(halves):
            line_copy(0, origin, half).wait_recv()

            @pl.when((origin < plane) & (plane < last))
            def _():
                line_copy(0, origin, half).start()

            @pl.when((origin > plane) & (plane > 0))
            def _():
                line_copy(1, origin, half).start()

            side_copy(origin, half).start()

    def take_side(origin):
        for half in range(halves):
            side_copy(origin, half).wait_recv()

    attend(0, plane)
    own_query = pltpu.make_async_copy(
        query_parts.at[0, plane], grad_query.at[:, columns_at(place)], own_sem.at[0]
    )
    own_query.start()
    before = plane
    for number in range(1, lines):
        there = nth_plane(number)
        take(there)
        take_side(before)
        attend(1, before)
        query_copy(1, before).start()
        attend(0, there)
        query_copy(0, there).start()
        before = there
    take_side(before)
    attend(1, before)
    query_copy(1, before).start()

    def keep(kept, slot, side, there):
        start = pl.multiple_of(device_of(side, there) * tokens, tokens)
        rows = pl.ds(start, tokens)
        kept[side, slot, :, :HEAD_SIZE] = (key_sum[rows, :] * scale).astype(jnp.bfloat16)
        kept[side, slot, :, HEAD_SIZE:] = value_sum[rows, :].astype(jnp.bfloat16)

    for side, there in reversed(others):
        keep(kv_out, there, side, there)
        kv_copy(side, there).start()
    keep(kv_in, plane, 0, plane)
    for side, there in others:
        kv_landing(side, there).wait_recv()
    for there in range(lines):
        head = slice(there * HEAD_SIZE, (there + 1) * HEAD_SIZE)
        total = sum(kv_in[side, there].astype(jnp.float32) for side in range(cols))
        grad_key[:, head] = total[:, :HEAD_SIZE].astype(jnp.bfloat16)
        grad_value[:, head] = total[:, HEAD_SIZE:].astype(jnp.bfloat16)
    own_query.wait()
    for side, there in others:
        query_landing(side, there).wait_recv()
        query_copy(side, there).wait_send()
        kv_copy(side, there).wait_send()
    for origin in range(lines):
        for half in range(halves):
            side_copy(origin, half).wait_send()

            @pl.when((origin <= plane) & (plane < last))
            def _():
                line_copy(0, origin, half).wait_send()

            @pl.when((origin >= plane) & (plane > 0))
            def _():
                line_copy(1, origin, half).wait_send()


def attention_grads(
    grad_resid, w_out, head_query, head_output, head_key, head_value, lse, lines, cols
):
    tokens, width = grad_resid.shape
    sequence, head_width = head_query.shape
    heads = head_width // HEAD_SIZE
    peers = lines * cols
    halves = 4
    low, full = jnp.bfloat16, jnp.float32
    dma = pltpu.SemaphoreType.DMA
    vmem = pl.BlockSpec(memory_space=pltpu.VMEM)
    hbm = pl.BlockSpec(memory_space=pl.ANY)
    kv_shape = jax.ShapeDtypeStruct((tokens, KEY_VALUE_HEADS * HEAD_SIZE), low)
    return pl.pallas_call(
        functools.partial(attention_kernel, lines, cols),
        out_shape=(
            jax.ShapeDtypeStruct((tokens, peers * head_width), low),
            kv_shape,
            kv_shape,
        ),
        in_specs=[vmem] * 3 + [hbm] * 4,
        out_specs=[hbm, vmem, vmem],
        scratch_shapes=[
            pltpu.VMEM(head_query.shape, low),
            pltpu.VMEM(head_output.shape, low),
            pltpu.VMEM(head_key.shape, low),
            pltpu.VMEM(head_value.shape, low),
            pltpu.VMEM((cols, lines, halves, tokens, width // halves), low),
            pltpu.VMEM((HEAD_SIZE, sequence), low),
            pltpu.VMEM((heads * tokens, HEAD_SIZE), low),
            pltpu.VMEM((heads * tokens, HEAD_SIZE), low),
            pltpu.VMEM((HEAD_SIZE, heads * tokens), full),
            pltpu.VMEM((cols, lines, tokens, head_width), low),
            pltpu.VMEM((sequence, HEAD_SIZE), full),
            pltpu.VMEM((sequence, HEAD_SIZE), full),
            pltpu.VMEM((cols, lines, tokens, 2 * HEAD_SIZE), low),
            pltpu.VMEM((cols, lines, tokens, 2 * HEAD_SIZE), low),
            dma((2, lines, halves)),
            dma((lines, halves)),
            dma((cols, lines, halves)),
            dma((cols, lines)),
            dma((cols, lines)),
            dma((cols, lines)),
            dma((cols, lines)),
            dma((5,)),
        ],
        compiler_params=pltpu.CompilerParams(
            collective_id=1, has_side_effects=True, vmem_limit_bytes=58 * 2**20
        ),
        cost_estimate=pl.CostEstimate(
            flops=10 * sequence * sequence * head_width,
            bytes_accessed=100 * 2**20,
            transcendentals=0,
        ),
    )(grad_resid, w_out, lse, head_query, head_output, head_key, head_value)


def per_device(
    grad_out,
    hidden,
    norm_gain,
    expert_ids,
    gate_weights,
    w_gate,
    w_up,
    w_down,
    w_out,
    queries,
    keys,
    values,
    attn_out,
    lse,
):
    token_rows, width = hidden.shape
    topk = expert_ids.shape[1]
    groups = lax.axis_size("grp")
    inner_product = lax.axis_size("inner")
    experts_all = w_gate.shape[0] * groups * inner_product
    capacity = max(2, 5 * token_rows * topk // (4 * experts_all))
    cols = groups // 2
    lines = inner_product // cols if cols else 0
    kernel_plan = (
        cols == 2
        and lines == 4
        and inner_product == lines * cols
        and w_gate.shape[0] == 1
        and (2 * capacity) % 16 == 0
        and token_rows == 128
        and width % 1024 == 0
        and w_gate.shape[2] % FF_TILE == 0
        and inner_product == KEY_VALUE_HEADS * cols
    )
    if kernel_plan:
        grad_resid, head_query, head_output, head_key, head_value = moe_input_grads(
            hidden,
            grad_out,
            norm_gain,
            expert_ids,
            gate_weights,
            w_gate,
            w_up,
            w_down,
            queries,
            attn_out,
            keys,
            values,
            lines,
            cols,
            capacity,
        )
        grads = attention_grads(
            grad_resid, w_out, head_query, head_output, head_key, head_value, lse, lines, cols
        )
        return (grad_resid,) + tuple(grads)
    hidden_f = hidden.astype(jnp.float32)
    inverse = lax.rsqrt(jnp.mean(hidden_f * hidden_f, axis=1, keepdims=True) + EPSILON)
    normed = (hidden_f * inverse * norm_gain).astype(jnp.bfloat16)
    upstream = grad_out.astype(jnp.float32)
    flat_count = token_rows * topk
    flat_ids = expert_ids.reshape(-1)
    one_hot = (flat_ids[:, None] == jnp.arange(experts_all, dtype=jnp.int32)[None, :]).astype(
        jnp.int32
    )
    before = jnp.tril(jnp.ones((flat_count, flat_count), jnp.bfloat16), -1)
    ahead = jnp.dot(
        before, one_hot.astype(jnp.bfloat16), preferred_element_type=jnp.float32
    ).astype(jnp.int32)
    slot_rank = jnp.sum(ahead * one_hot, axis=1)
    target = flat_ids * capacity + slot_rank
    owner = (
        jnp.full((experts_all * capacity,), flat_count, jnp.int32)
        .at[target]
        .set(jnp.arange(flat_count, dtype=jnp.int32))
    )
    source_tok = owner // topk
    scaled = (
        (upstream[:, None, :] * gate_weights[:, :, None])
        .reshape(flat_count, width)
        .astype(jnp.bfloat16)
    )
    zero_row = jnp.zeros((1, width), jnp.bfloat16)
    slot_inputs = jnp.concatenate([normed, zero_row], axis=0)[source_tok]
    slot_grads = jnp.concatenate([scaled, zero_row], axis=0)[owner]
    outgoing = jnp.concatenate([slot_inputs, slot_grads], axis=1).reshape(
        experts_all, capacity, 2 * width
    )
    returned = lax.all_to_all(
        expert_grads(
            lax.all_to_all(outgoing, ("grp", "inner"), split_axis=0, concat_axis=0, tiled=True),
            w_gate,
            w_up,
            w_down,
        ),
        ("grp", "inner"),
        split_axis=0,
        concat_axis=0,
        tiled=True,
    )
    expert_rows = returned.reshape(-1, width)[target].astype(jnp.float32)
    grad_normed = jnp.sum(expert_rows.reshape(token_rows, topk, width), axis=1)
    gained = grad_normed * norm_gain
    statistic = jnp.mean(gained * hidden_f, axis=1, keepdims=True)
    grad_resid = (
        upstream + inverse * gained - hidden_f * inverse * inverse * inverse * statistic
    ).astype(jnp.bfloat16)
    head_width = queries.shape[1] // inner_product
    per_head = head_width // HEAD_SIZE
    shared_portion = inner_product // KEY_VALUE_HEADS
    key_value_pairs = jnp.concatenate(
        [
            keys.reshape(token_rows, KEY_VALUE_HEADS, 1, HEAD_SIZE),
            values.reshape(token_rows, KEY_VALUE_HEADS, 1, HEAD_SIZE),
        ],
        axis=2,
    )
    key_value_broadcast = jnp.broadcast_to(
        key_value_pairs[:, :, None], (token_rows, KEY_VALUE_HEADS, shared_portion, 2, HEAD_SIZE)
    ).reshape(token_rows, inner_product * 2 * HEAD_SIZE)
    head_query, head_output, head_kv = (
        lax.all_to_all(queries, "inner", split_axis=1, concat_axis=0, tiled=True),
        lax.all_to_all(attn_out, "inner", split_axis=1, concat_axis=0, tiled=True),
        lax.all_to_all(key_value_broadcast, "inner", split_axis=1, concat_axis=0, tiled=True),
    )
    head_grad = contract_last(
        lax.all_gather(grad_resid, "inner", axis=0, tiled=True), w_out
    ).astype(jnp.bfloat16)
    seq_len = head_query.shape[0]
    head_key = head_kv[:, :HEAD_SIZE]
    head_value = head_kv[:, HEAD_SIZE:]
    lse_rows = lse.T
    scale = float(HEAD_SIZE) ** (-0.5)
    blocks = 1
    while blocks < 8 and seq_len % (2 * blocks) == 0 and (seq_len // (2 * blocks) >= 512):
        blocks = blocks * 2
    block_len = seq_len // blocks
    grad_key_acc = jnp.zeros((seq_len, HEAD_SIZE), jnp.float32)
    grad_value_acc = jnp.zeros((seq_len, HEAD_SIZE), jnp.float32)
    query_parts = []
    for block_index in range(blocks):
        low = block_index * block_len
        high = low + block_len
        block_query = head_query[low:high].reshape(block_len * per_head, HEAD_SIZE)
        block_output = head_output[low:high].reshape(block_len * per_head, HEAD_SIZE)
        block_grad = head_grad[low:high].reshape(block_len * per_head, HEAD_SIZE)
        block_lse = lse_rows[low:high].reshape(-1)
        seen_key = head_key[:high]
        seen_value = head_value[:high]
        scores = contract_last(block_query, seen_key) * scale
        row_position = low + jnp.arange(block_len * per_head, dtype=jnp.int32) // per_head
        visible = jnp.arange(high, dtype=jnp.int32)[None, :] <= row_position[:, None]
        probs = jnp.where(visible, jnp.exp(scores - block_lse[:, None]), 0.0)
        grad_probs = contract_last(block_grad, seen_value)
        delta = jnp.sum(
            block_grad.astype(jnp.float32) * block_output.astype(jnp.float32), axis=1, keepdims=True
        )
        grad_scores = (probs * (grad_probs - delta)).astype(jnp.bfloat16)
        query_part = jnp.dot(grad_scores, seen_key, preferred_element_type=jnp.float32) * scale
        query_parts.append(query_part.reshape(block_len, head_width))
        grad_key_acc = grad_key_acc.at[:high].add(contract_first(grad_scores, block_query) * scale)
        grad_value_acc = grad_value_acc.at[:high].add(
            contract_first(probs.astype(jnp.bfloat16), block_grad)
        )
    grad_query_heads = jnp.concatenate(query_parts, axis=0)
    kv_heads = jnp.concatenate([grad_key_acc, grad_value_acc], axis=1)
    token_query, token_key_value = (
        lax.all_to_all(
            grad_query_heads.astype(jnp.bfloat16), "inner", split_axis=0, concat_axis=1, tiled=True
        ).astype(grad_query_heads.dtype),
        lax.all_to_all(
            kv_heads.astype(jnp.bfloat16), "inner", split_axis=0, concat_axis=1, tiled=True
        ).astype(kv_heads.dtype),
    )
    summed_total = jnp.sum(
        token_key_value.reshape(token_rows, KEY_VALUE_HEADS, shared_portion, 2, HEAD_SIZE), axis=2
    )
    keys_gradient = (
        summed_total[:, :, 0].reshape(token_rows, KEY_VALUE_HEADS * HEAD_SIZE).astype(jnp.bfloat16)
    )
    values_gradient = (
        summed_total[:, :, 1].reshape(token_rows, KEY_VALUE_HEADS * HEAD_SIZE).astype(jnp.bfloat16)
    )
    return (grad_resid, token_query.astype(jnp.bfloat16), keys_gradient, values_gradient)


def solution(mesh):
    placed = (
        P(("grp", "inner"), None),
        P(("grp", "inner"), None),
        P(),
        P(("grp", "inner"), None),
        P(("grp", "inner"), None),
        P(("grp", "inner"), None, None),
        P(("grp", "inner"), None, None),
        P(("grp", "inner"), None, None),
        P("inner", None),
        P(("grp", "inner"), None),
        P(("grp", "inner"), None),
        P(("grp", "inner"), None),
        P(("grp", "inner"), None),
        P("inner", "grp"),
    )
    return jax.shard_map(
        per_device,
        mesh=mesh,
        in_specs=placed,
        out_specs=(
            P(("grp", "inner"), None),
            P(("grp", "inner"), None),
            P(("grp", "inner"), None),
            P(("grp", "inner"), None),
        ),
        check_vma=False,
    )
```
